32 devices in a mesh: grp: 2 (over y), seq: 4 (over z), head: 4 (over x, core).
Axes of the slice: x: 2, y: 2, z: 4, core: 2. Of those that a mesh axis runs over, the one named last changes fastest.
Arguments:
- tokens: bfloat16 [1024, 2048], P(('grp', 'seq')), parts along dimension 0, may hold values from -6 to 6
- attn_weight: bfloat16 [4, 2048, 2048], P(None, 'seq', 'head'), may hold values from -0.125 to 0.125
- attn_gain: float32 [2048], replicated, may hold values from 0.25 to 1.75
- moe_gain: float32 [2048], replicated, may hold values from 0.25 to 1.75
- routes: int32 [1024, 8], P(('grp', 'seq')), parts along dimension 0, may hold values from 0 to 63, all different within a row; in each aligned block of 128 rows (0 to 127, 128 to 255, ...) at most 18 rows name the same one
- gates: float32 [1024, 8], P(('grp', 'seq')), parts along dimension 0, may hold values from 0.05 to 0.4
- expert_gate: bfloat16 [64, 2048, 1024], P('seq', None, 'head'), may hold values from -0.125 to 0.125
- expert_up: bfloat16 [64, 2048, 1024], P('seq', None, 'head'), may hold values from -0.125 to 0.125
- expert_down: bfloat16 [64, 1024, 2048], P('seq', 'head'), may hold values from -0.1875 to 0.1875
Outputs:
- mixed: bfloat16 [1024, 2048], P(('grp', 'seq')), parts along dimension 0
The draws below stay inside these ranges and needn't reach their ends.
There are 2 independent parts, one for each index of `grp`. The reference program is written for one: setup_inputs(seed, part) draws one part's arguments, and reference() takes and returns one part's arrays. A program takes and returns all parts, laid end to end along the dimension named above; an argument that names none is the same for every part. Nothing has to cross between parts.
Inputs may be any that keep to these rules, and one draw needn't show every extreme that they name: `routes`: in each aligned block of 128 tokens, no expert is named by more than 18 pairs of a token and a choice, a bound that some block reaches; a token's 8 experts differ.
All inputs are finite; a program needn't handle non-finite values.
Results may differ from the reference program's by a relative error of at most 0.015.
Values may be sent and summed in bfloat16 or wider, within the bound.
A program may use at most 128 MiB of HBM per device.

```python
import math
import jax
import jax.numpy as jnp
import numpy as np
from jax import lax

D = 2048
HEADS = 16
HEAD_DIM = 128
EXPERTS = 64
FFE = 1024
TOPK = 8
TOK_DEV = 128
CAP = 18
TOKENS = 512
N_SEQ = 4
N_HEAD = 4


def levels(key, shape, cuts, smallest, top_value):
    def one(dim, blocks):
        heights = jax.random.uniform(jax.random.fold_in(jax.random.fold_in(key, 6), dim), (blocks,), jnp.float32, smallest / len(cuts), top_value / len(cuts))
        return jnp.repeat(jnp.exp(heights), shape[dim] // blocks).reshape((-1,) + (1,) * (len(shape) - dim - 1))

    level = one(*cuts[0])
    for cut in cuts[1:]:
        level = level * one(*cut)
    return level


def shared_out(stream_key, own, number, rows, amount, top, most, skew):
    ranking = jax.random.permutation(stream_key, amount)
    heavy_load, ordinary = shares(amount, rows * top, most, skew, True), shares(amount, rows * top, most, skew, False)
    places = jnp.arange(amount)

    def named(sizes, offset_by):
        used = int((sizes > 0).sum())
        fixed = max(1, used // 4)
        shifted = fixed + (places - fixed + offset_by * (used - fixed)) % max(1, amount - fixed)
        return jnp.zeros((amount,), jnp.int32).at[ranking[jnp.where(places < fixed, places, shifted)]].set(jnp.asarray(sizes, jnp.int32))

    sizes = jnp.where(number % 4 == 0, named(heavy_load, number // 4), named(ordinary, number - number // 4 - 1))
    mixed = jax.random.permutation(jax.random.fold_in(own, 3), amount)
    source_of, receiver = mixed[0:amount // 2 * 2:2], mixed[1:amount // 2 * 2:2]
    slack = jnp.minimum(sizes[source_of] - 1, most - sizes[receiver]) // 2
    slack = jnp.where((source_of == ranking[0]) | (receiver == ranking[0]) | (sizes[receiver] == 0), 0, jnp.maximum(slack, 0))
    shifted = jax.random.randint(jax.random.fold_in(own, 4), (amount // 2,), 0, 1 << 20) % (slack + 1)
    sizes = sizes.at[source_of].add(-shifted).at[receiver].add(shifted)
    members = jnp.searchsorted(jnp.cumsum(sizes), jnp.arange(rows * top), side="right").astype(jnp.int32)
    table = members.reshape(top, rows).T
    table = table[jax.random.permutation(jax.random.fold_in(own, 1), rows)]
    offset_by = jax.random.randint(jax.random.fold_in(own, 2), (rows, 1), 0, top)
    return jnp.take_along_axis(table, (jnp.arange(top)[None, :] + offset_by) % top, axis=1)


def shares(count, total, limit, slope, full):
    portions = [(1 << 20) // math.isqrt(rank ** slope) + 1 for rank in range(1, count + 1)]
    largest = limit if full else min(limit, max(-(-total // count), total * portions[0] // sum(portions)))
    least = 1 if total - largest >= count - 1 else 0
    counts, spare = [largest] + [least] * (count - 1), total - largest - least * (count - 1)
    while spare > 0:
        movable = [i for i in range(1, count) if counts[i] < largest] or [i for i in range(1, count) if counts[i] < limit]
        whole, budget = sum([portions[i] for i in movable]), spare
        for i in movable:
            extra = min(limit - counts[i], max(1, budget * portions[i] // whole), spare)
            counts[i] = counts[i] + extra
            spare = spare - extra
    return np.array(counts)


def bell_draw(stream_key, shape, spread, bound, split=(), kind=jnp.bfloat16):
    drawn = jax.random.normal(stream_key, shape, jnp.float32) * spread
    if len(split) > 0:
        drawn = levels(stream_key, shape, split, -0.22, 0.18) * drawn
    return jnp.clip(drawn, min=-bound, max=bound).astype(kind)


def setup_inputs(seed: int = 0, part: int = 0) -> dict:
    keys = jax.random.split(jax.random.key(seed), 10)
    part_splits = jax.random.split(jax.random.fold_in(keys[9], part), 10)
    tokens = bell_draw(part_splits[0], (TOKENS, D), 1.0, 6.0, ((0, 4),))
    attn_weight = bell_draw(keys[1], (4, D, HEADS * HEAD_DIM), D ** -0.5, 0.125, ((1, 4), (2, 4)))
    attn_gain = jnp.clip(1.0 + 0.15 * jax.random.normal(keys[2], (D,), jnp.float32), 0.25, 1.75)
    moe_gain = jnp.clip(1.0 + 0.15 * jax.random.normal(keys[3], (D,), jnp.float32), 0.25, 1.75)
    routes_keys = jax.random.split(jax.random.fold_in(part_splits[4], 1), TOKENS // TOK_DEV)
    routes_turns = jax.random.permutation(jax.random.fold_in(part_splits[4], 3), TOKENS // TOK_DEV)
    routes = jax.vmap(lambda own, number: shared_out(jax.random.fold_in(part_splits[4], 2), own, number, TOK_DEV, EXPERTS, TOPK, CAP, 2))(routes_keys, routes_turns).reshape((TOKENS, TOPK))
    gates = jnp.clip(0.05 + 0.35 * jax.random.uniform(part_splits[5], (TOKENS, TOPK), jnp.float32) ** levels(part_splits[5], (TOKENS, TOPK), ((0, 4),), -0.2, 0.2), 0.05, 0.4)
    expert_gate = bell_draw(keys[6], (EXPERTS, D, FFE), D ** -0.5, 0.125, ((0, 4), (2, 4)))
    expert_up = bell_draw(keys[7], (EXPERTS, D, FFE), D ** -0.5, 0.125, ((0, 4), (2, 4)))
    expert_down = bell_draw(keys[8], (EXPERTS, FFE, D), FFE ** -0.5, 0.1875, ((0, 4), (1, 4)))
    return dict(tokens=tokens, attn_weight=attn_weight, attn_gain=attn_gain, moe_gain=moe_gain, routes=routes, gates=gates, expert_gate=expert_gate, expert_up=expert_up, expert_down=expert_down)


PRECISE = lax.Precision.HIGHEST

def rms_scale(row_block, gain_vec):
    widened = row_block.astype(jnp.float32)
    factor = lax.rsqrt(lax.optimization_barrier(jnp.mean(widened * widened, axis=-1, keepdims=True)) + 1e-06)
    return widened * factor * gain_vec

def head_norm(outputs):
    return outputs * lax.rsqrt(lax.optimization_barrier(jnp.mean(outputs * outputs, axis=-1, keepdims=True)) + 1e-06)

def causal_linear(query_rows, key_rows, value_rows):
    block_count = query_rows.shape[0] // TOK_DEV
    shaped = [matrix.reshape(block_count, TOK_DEV, HEADS, HEAD_DIM).astype(jnp.float32) for matrix in (query_rows, key_rows, value_rows)]
    lower_mask = jnp.arange(TOK_DEV)[:, None] >= jnp.arange(TOK_DEV)[None, :]

    def advance(carry_state, block):
        query_blk, key_blk, value_blk = block
        inter_part = jnp.einsum('thd,hde->the', query_blk, carry_state, precision=PRECISE)
        scores = jnp.einsum('thd,shd->hts', query_blk, key_blk, precision=PRECISE)
        scores = jnp.where(lower_mask[None], scores, 0.0)
        intra_part = jnp.einsum('hts,she->the', scores, value_blk, precision=PRECISE)
        carry_state = carry_state + jnp.einsum('thd,the->hde', key_blk, value_blk, precision=PRECISE)
        return (carry_state, inter_part + intra_part)
    start_state = jnp.zeros((HEADS, HEAD_DIM, HEAD_DIM), jnp.float32)
    final_state, outputs = lax.scan(advance, start_state, tuple(shaped))
    return outputs.reshape(block_count * TOK_DEV, HEADS, HEAD_DIM)

def slot_numbers(route_rows):
    one_hot = (route_rows[..., None] == jnp.arange(EXPERTS, dtype=jnp.int32)).astype(jnp.int32)
    earlier = jnp.cumsum(one_hot, axis=-2) - one_hot
    return route_rows * CAP + lax.optimization_barrier(jnp.sum(earlier * one_hot, axis=-1))

def expert_apply(slot_rows, gate_mat, up_mat, down_mat):
    gate_val = jnp.dot(slot_rows, gate_mat, preferred_element_type=jnp.float32)
    up_val = jnp.dot(slot_rows, up_mat, preferred_element_type=jnp.float32)
    hidden = (jax.nn.silu(gate_val) * up_val).astype(jnp.bfloat16)
    grouped = hidden.reshape(-1, N_HEAD, FFE // N_HEAD).astype(jnp.float32)
    down_groups = down_mat.reshape(N_HEAD, FFE // N_HEAD, D).astype(jnp.float32)
    partial_value = jnp.einsum('rgf,gfd->rgd', grouped, down_groups, precision=PRECISE).astype(jnp.bfloat16)
    return lax.optimization_barrier(jnp.sum(partial_value.astype(jnp.float32), axis=1))

def reference(tokens, attn_weight, attn_gain, moe_gain, routes, gates, expert_gate, expert_up, expert_down):
    total_rows = tokens.shape[0]
    normed = rms_scale(tokens, attn_gain).astype(jnp.bfloat16)
    projected = [jnp.dot(normed, attn_weight[which], preferred_element_type=jnp.float32).astype(jnp.bfloat16) for which in range(3)]
    outputs = causal_linear(projected[0], projected[1], projected[2])
    attended = head_norm(outputs).reshape(total_rows, HEADS * HEAD_DIM).astype(jnp.bfloat16)
    out_proj = lax.dot_general(attended, attn_weight[3], (((1,), (1,)), ((), ())), preferred_element_type=jnp.float32)
    residual = (tokens.astype(jnp.float32) + out_proj).astype(jnp.bfloat16)
    moe_in = rms_scale(residual, moe_gain).astype(jnp.bfloat16)
    route_rows = routes.reshape(N_SEQ, TOK_DEV * TOPK)
    slots = slot_numbers(route_rows)
    token_ids = jnp.repeat(jnp.arange(total_rows, dtype=jnp.int32).reshape(N_SEQ, TOK_DEV), TOPK, axis=1)
    block_ids = jnp.broadcast_to(jnp.arange(N_SEQ, dtype=jnp.int32)[:, None], slots.shape)
    owner_table = jnp.full((N_SEQ, EXPERTS * CAP), total_rows, jnp.int32).at[block_ids, slots].set(token_ids)
    weight_table = jnp.zeros((N_SEQ, EXPERTS * CAP), jnp.float32).at[block_ids, slots].set(gates.reshape(N_SEQ, TOK_DEV * TOPK))
    padded_in = jnp.concatenate([moe_in, jnp.zeros((1, D), jnp.bfloat16)], axis=0)

    def one_expert(moe_sum, expert_id):
        picked = lax.dynamic_slice_in_dim(owner_table, expert_id * CAP, CAP, 1).reshape(-1)
        slot_gate = lax.dynamic_slice_in_dim(weight_table, expert_id * CAP, CAP, 1).reshape(-1)
        produced = expert_apply(padded_in[picked], expert_gate[expert_id], expert_up[expert_id], expert_down[expert_id])
        return (moe_sum.at[picked].add(slot_gate[:, None] * produced), None)
    start_sum = jnp.zeros((total_rows + 1, D), jnp.float32)
    moe_sum, unused = lax.scan(one_expert, start_sum, jnp.arange(EXPERTS, dtype=jnp.int32))
    return (residual.astype(jnp.float32) + moe_sum[:total_rows]).astype(jnp.bfloat16)
```

```python
import functools

import jax
import jax.numpy as jnp
from jax import lax
from jax.experimental import pallas as pl
from jax.experimental.pallas import tpu as pltpu
from jax.sharding import PartitionSpec as P

HEAD_DIM = 128
EXPERTS = 64
TOPK = 8
CAP = 18
MESH = pl.DeviceIdType.MESH
VMEM_LIMIT = 63 * 1024 * 1024


PRECISE = lax.Precision.HIGHEST


def prefix_2(array, axis, combine, identity):
    peers, position = (lax.axis_size(axis), lax.axis_index(axis))
    everything = lax.all_gather(array.astype(jnp.bfloat16), axis)
    start = jnp.broadcast_to(jnp.asarray(identity, array.dtype), array.shape)

    def hop(k, before):
        reached = k < position
        new = combine(before, everything[k].astype(array.dtype))
        return jnp.where(reached, new, before)

    return lax.fori_loop(0, peers, hop, start)


def rms_scale(row_block, gain_vec):
    widened = row_block.astype(jnp.float32)
    factor = lax.rsqrt(jnp.mean(widened * widened, axis=-1, keepdims=True) + 1e-06)
    return widened * factor * gain_vec


def head_norm(outputs):
    return outputs * lax.rsqrt(jnp.mean(outputs * outputs, axis=-1, keepdims=True) + 1e-06)


def add_states(earlier, later):
    return earlier + later


def slot_numbers(route_flat):
    one_hot = (route_flat[:, None] == jnp.arange(EXPERTS, dtype=jnp.int32)[None, :]).astype(
        jnp.int32
    )
    earlier = jnp.cumsum(one_hot, axis=0) - one_hot
    return route_flat * CAP + jnp.sum(earlier * one_hot, axis=1)


def make_runner(expert_gate, expert_up, expert_down):

    def run_experts(received):
        gate_val = jnp.einsum(
            "necd,edf->necf", received, expert_gate, preferred_element_type=jnp.float32
        )
        up_val = jnp.einsum(
            "necd,edf->necf", received, expert_up, preferred_element_type=jnp.float32
        )
        hidden = (jax.nn.silu(gate_val) * up_val).astype(jnp.bfloat16)
        partial_value = jnp.einsum(
            "necf,efd->necd", hidden, expert_down, preferred_element_type=jnp.float32
        ).astype(jnp.bfloat16)
        groups = lax.axis_size("head")
        shape_now = partial_value.shape
        split = partial_value.reshape(
            shape_now[0], shape_now[1], shape_now[2], groups, shape_now[3] // groups
        )
        by_group = lax.all_to_all(split, "head", split_axis=3, concat_axis=3, tiled=True)
        summed = jnp.sum(by_group.astype(jnp.float32), axis=3)
        return lax.all_to_all(
            summed.astype(jnp.bfloat16), "seq", split_axis=0, concat_axis=0, tiled=True
        ).astype(summed.dtype)

    return run_experts


def body(
    tokens, attn_weight, attn_gain, moe_gain, routes, gates, expert_gate, expert_up, expert_down
):
    local_rows = tokens.shape[0]
    normed = rms_scale(tokens, attn_gain).astype(jnp.bfloat16)
    weights = lax.all_gather(attn_weight, "seq", axis=1, tiled=True)
    head_count = weights.shape[2] // HEAD_DIM
    projected = [
        jnp.dot(normed, weights[which], preferred_element_type=jnp.float32)
        .astype(jnp.bfloat16)
        .reshape(local_rows, head_count, HEAD_DIM)
        for which in range(3)
    ]
    query_rows, key_rows, value_rows = projected
    own_state = jnp.einsum("thd,the->hde", key_rows, value_rows, preferred_element_type=jnp.float32)
    prefix = prefix_2(own_state, "seq", add_states, jnp.zeros_like(own_state))
    inter_part = jnp.einsum(
        "thd,hde->the", query_rows.astype(jnp.float32), prefix, precision=PRECISE
    )
    scores = jnp.einsum("thd,shd->hts", query_rows, key_rows, preferred_element_type=jnp.float32)
    lower_mask = jnp.arange(local_rows)[:, None] >= jnp.arange(local_rows)[None, :]
    scores = jnp.where(lower_mask[None], scores, 0.0)
    intra_part = jnp.einsum(
        "hts,she->the", scores, value_rows.astype(jnp.float32), precision=PRECISE
    )
    attended = (
        head_norm(inter_part + intra_part)
        .reshape(local_rows, head_count * HEAD_DIM)
        .astype(jnp.bfloat16)
    )
    out_part = lax.dot_general(
        attended, weights[3], (((1,), (1,)), ((), ())), preferred_element_type=jnp.float32
    )
    residual = (
        tokens.astype(jnp.float32)
        + lax.psum(out_part.astype(jnp.bfloat16), "head").astype(jnp.float32)
    ).astype(jnp.bfloat16)
    moe_in = rms_scale(residual, moe_gain).astype(jnp.bfloat16)
    route_flat = routes.reshape(-1)
    slots = slot_numbers(route_flat)
    owners = lax.axis_size("seq")
    local_experts = expert_gate.shape[0]
    source_row = jnp.arange(route_flat.shape[0], dtype=jnp.int32) // TOPK
    run_experts = make_runner(expert_gate, expert_up, expert_down)
    outbound = (
        jnp.zeros((EXPERTS * CAP, moe_in.shape[1]), jnp.bfloat16).at[slots].set(moe_in[source_row])
    )
    outbound = outbound.reshape(owners, local_experts, CAP, moe_in.shape[1])
    returned = run_experts(lax.all_to_all(outbound, "seq", split_axis=0, concat_axis=0, tiled=True))
    arrived = returned.reshape(EXPERTS * CAP, -1)[slots].reshape(local_rows, TOPK, -1)
    moe_partial = jnp.einsum("tkd,tk->td", arrived, gates, precision=PRECISE)
    column_span = moe_partial.shape[1]
    residual_share = lax.dynamic_slice_in_dim(
        residual, lax.axis_index("head") * column_span, column_span, 1
    )
    mixed_share = (residual_share.astype(jnp.float32) + moe_partial).astype(jnp.bfloat16)
    return lax.all_gather(mixed_share, "head", axis=1, tiled=True)


def flip(index, bit):
    return index + bit * (1 - 2 * lax.rem(index // bit, 2))


def remote(source, dest, send_sem, recv_sem, target):
    return pltpu.make_async_remote_copy(
        src_ref=source,
        dst_ref=dest,
        send_sem=send_sem,
        recv_sem=recv_sem,
        device_id=target,
        device_id_type=MESH,
    )


def aligned(index, size):
    return pl.ds(pl.multiple_of(index * size, size), size)


def dot(a, b):
    return jnp.dot(a, b, preferred_element_type=jnp.float32)


def dot_nt(a, b):
    return lax.dot_general(a, b, (((1,), (1,)), ((), ())), preferred_element_type=jnp.float32)


def nearest(i, me, peers):
    both = jnp.minimum(me, peers - 1 - me)
    step = (i + 1) // 2
    side = -1 if i % 2 else 1
    rest = jnp.where(me <= peers - 1 - me, i - both, both - i)
    return me + jnp.where(i <= 2 * both, side * step, rest)


class Chain:
    def __init__(self, piece, sends, recvs):
        self.piece, self.sends, self.recvs = piece, sends, recvs
        self.peers, self.me = lax.axis_size("seq"), lax.axis_index("seq")

    def copy(self, origin, way):
        ref = self.piece(origin)
        to = lax.rem(self.me + (self.peers - 1 if way else 1), self.peers)
        return remote(ref, ref, self.sends.at[way, origin], self.recvs.at[origin], {"seq": to})

    def wanted(self, origin, way):
        if way:
            return (origin >= self.me) & (self.me > 0)
        return (origin <= self.me) & (self.me < self.peers - 1)

    def arrive(self, origin):
        self.copy(origin, 0).wait_recv()

    def forward(self, origin):
        for way in range(2):

            @pl.when(self.wanted(origin, way))
            def _():
                self.copy(origin, way).start()

    def sent(self, origin):
        for way in range(2):

            @pl.when(self.wanted(origin, way))
            def _():
                self.copy(origin, way).wait_send()


def layer_kernel(slots, *refs):
    (
        tok, aw, attn_gain, moe_gain, small, eg, eu, ed, o_ref,
        xall, xn, wbuf, w3, acc, qkv, att, psend, precv, xsend, xrecv, res, sm, pick, mix, xs, ssq,
        fs, ms, hid, gbuf, ubuf, dbuf, csend, crecv, keep, osend, orecv, zsend, zrecv, share,
        own_sems, w_z, w_y, x_zs, x_zr, x_x, x_c, s_sems, a_zs, a_zr, p_c, p_x, r_zs, r_zr, r_c,
        g_sems, u_sems, d_sems, o_c, o_x, o_z, f_sems,
    ) = refs
    f32, bf16 = jnp.float32, jnp.bfloat16
    n_seq, n_grp = lax.axis_size("seq"), lax.axis_size("grp")
    grp, seq, head = lax.axis_index("grp"), lax.axis_index("seq"), lax.axis_index("head")
    core, col = lax.rem(head, 2), head // 2
    other_x, other_c = {"head": flip(head, 2)}, {"head": flip(head, 1)}
    other_y = {"grp": lax.rem(grp + 1, n_grp)}
    local, width = tok.shape
    total = n_seq * local
    depth, columns = aw.shape[1:]
    own = columns // n_seq
    part = depth // n_grp
    quarter = local // 4
    half_rows, block = total // 2, total // 4
    amount, ring = ed.shape[0], gbuf.shape[0]
    span = width // 4
    near = [nearest(i, seq, n_seq) for i in range(n_seq)]

    barrier = pltpu.get_barrier_semaphore()
    friends = [{"seq": lax.rem(seq + k, n_seq)} for k in range(1, n_seq)] + [other_x, other_c]
    if n_grp > 1:
        friends.append(other_y)
    for friend in friends:
        pl.semaphore_signal(barrier, inc=1, device_id=friend, device_id_type=MESH)

    own_copies = [
        pltpu.make_async_copy(
            aw.at[which, :, aligned(seq, own)],
            wbuf.at[seq, :, pl.ds(which * own, own)],
            own_sems.at[which],
        )
        for which in range(3)
    ] + [pltpu.make_async_copy(aw.at[3], w3, own_sems.at[3])]
    for copy in own_copies:
        copy.start()
    xall[aligned(seq, local), :] = tok[...]
    sm[:, aligned(seq, local)] = small[...]
    pl.semaphore_wait(barrier, len(friends))

    tokens_z = Chain(
        lambda p: xall.at[pl.ds(pl.multiple_of(p * local + head * quarter, quarter), quarter), :],
        x_zs, x_zr,
    )
    tokens_z.forward(seq)

    def table_copy(to, origin):
        ref = sm.at[:, aligned(origin, local)]
        return remote(ref, ref, s_sems.at[0, to], s_sems.at[1, origin], {"seq": to})

    def w_copy(which, to):
        return remote(
            aw.at[which, aligned(grp, part), aligned(to, own)],
            wbuf.at[seq, aligned(grp, part), pl.ds(which * own, own)],
            w_z.at[0, which, to], w_z.at[1, which, seq], {"seq": to},
        )

    def w_piece(which, origin, side):
        return wbuf.at[origin, aligned(side, part), pl.ds(which * own, own)]

    def w_arrival(which, origin):
        ref = w_piece(which, origin, grp)
        return remote(ref, ref, w_z.at[0, which, origin], w_z.at[1, which, origin], {"seq": origin})

    def w_over(which, origin):
        ref = w_piece(which, origin, grp)
        return remote(ref, ref, w_y.at[0, which, origin], w_y.at[1, which, origin], other_y)

    for p in near[1:]:
        table_copy(p, seq).start()
    for which in range(3):
        for p in reversed(near[1:]):
            w_copy(which, p).start()

    def fetch(e, slot):
        return [
            pltpu.make_async_copy(eg.at[e], gbuf.at[slot], g_sems.at[slot]),
            pltpu.make_async_copy(eu.at[e], ubuf.at[slot], u_sems.at[slot]),
        ]

    def fetch_down(e):
        return pltpu.make_async_copy(ed.at[e], dbuf.at[e], d_sems.at[e])

    def begin(e, carry):
        for copy in fetch(e, e):
            copy.start()
        return carry

    def begin_down(e, carry):
        fetch_down(e).start()
        return carry

    lax.fori_loop(0, ring, begin, 0)
    lax.fori_loop(0, amount, begin_down, 0)

    def norm_rows(p):
        def step(j, carry):
            rows = pl.ds(pl.multiple_of(p * local + j * quarter, quarter), quarter)
            value = xall[rows, :].astype(f32)
            factor = lax.rsqrt(jnp.mean(value * value, axis=-1, keepdims=True) + 1e-06)
            xn[rows, :] = (value * factor * attn_gain[...]).astype(bf16)
            return carry

        lax.fori_loop(0, 4, step, 0)

    norm_rows(seq)

    def across(p):
        ref = xall.at[pl.ds(pl.multiple_of(p * local + head * quarter, quarter), quarter), :]
        return remote(ref, ref, x_x.at[0, p], x_x.at[1, p], other_x)

    def beside(p, which):
        owner = flip(head, 2) if which else head
        ref = xall.at[pl.ds(pl.multiple_of(p * local + owner * quarter, quarter), quarter), :]
        return remote(ref, ref, x_c.at[0, which, p], x_c.at[1, which, p], other_c)

    for i in range(1, n_seq):
        p = near[i]
        tokens_z.arrive(p)
        tokens_z.forward(p)
        across(p).start()
        beside(p, 0).start()
        if i <= 3:
            for q in near[1:]:
                w_arrival(i - 1, q).wait_recv()
                if n_grp > 1:
                    w_over(i - 1, q).start()
        across(near[i]).wait_recv()
        beside(near[i], 1).start()
    for which in range(min(3, n_seq - 1), 3):
        for q in near[1:]:
            w_arrival(which, q).wait_recv()
            if n_grp > 1:
                w_over(which, q).start()

    for p in near[1:]:
        table_copy(p, p).wait_recv()
    top = small.shape[0] // 2
    ids = lax.broadcasted_iota(jnp.int32, (128, total), 0).astype(f32)
    ids = ids + (seq * amount).astype(f32)
    named = jnp.zeros((128, total), f32)
    weight = jnp.zeros((128, total), f32)
    for k in range(top):
        hit = sm[k : k + 1, :] == ids
        named = jnp.where(hit, 1.0, named)
        weight = jnp.where(hit, sm[top + k : top + k + 1, :], weight)
    before = lax.broadcasted_iota(jnp.int32, (total, total), 0) < lax.broadcasted_iota(
        jnp.int32, (total, total), 1
    )
    rank = dot(named.astype(bf16), jnp.where(before, 1.0, 0.0).astype(bf16))
    place = jnp.where(named > 0.0, rank, -1.0)
    spot = lax.broadcasted_iota(jnp.int32, (slots, total), 0).astype(f32)
    for e in range(amount):
        pick[e * slots : (e + 1) * slots, :] = jnp.where(
            place[e : e + 1, :] == spot, 1.0, 0.0
        ).astype(bf16)
    wide = lax.broadcasted_iota(jnp.int32, (128, amount * slots), 1).astype(f32)
    owner = jnp.floor((wide + 0.5) * (1.0 / slots))
    mine = lax.broadcasted_iota(jnp.int32, (128, amount * slots), 0).astype(f32)
    spread = jnp.where(owner == mine, 1.0, 0.0).astype(bf16)
    spot_of = (wide - owner * slots)[:1, :]
    place_t = jnp.transpose(place).astype(bf16)
    weight_t = jnp.transpose(weight).astype(bf16)
    for b in range(0, total, 128):
        mix[b : b + 128, :] = jnp.where(
            dot(place_t[b : b + 128], spread) == spot_of, dot(weight_t[b : b + 128], spread), 0.0
        ).astype(bf16)

    for i in range(1, n_seq):
        beside(near[i], 0).wait_recv()
        beside(near[i], 1).wait_recv()
        norm_rows(near[i])
    for copy in own_copies:
        copy.wait()
    acc[...] = dot(xn[:, aligned(seq, depth)], wbuf[seq])
    for i in range(1, n_seq):
        p = near[i]
        if n_grp > 1:
            for which in range(3):
                ref = w_piece(which, p, lax.rem(grp + 1, n_grp))
                remote(ref, ref, w_y.at[0, which, p], w_y.at[1, which, p], other_y).wait_recv()
        acc[...] += dot(xn[:, aligned(p, depth)], wbuf[p])
    qkv[...] = acc[...].astype(bf16)

    attended = [
        Chain(
            lambda p, r=r: att.at[pl.ds(r * half_rows, half_rows), aligned(p, own)],
            a_zs.at[r], a_zr.at[r],
        )
        for r in range(2)
    ]
    for r in range(2):
        for i in (2 * r, 2 * r + 1):
            seen = (i + 1) * block
            lower = (
                lax.broadcasted_iota(jnp.int32, (block, seen), 0) + i * block
                >= lax.broadcasted_iota(jnp.int32, (block, seen), 1)
            )
            for a in range(own // HEAD_DIM):
                at = a * HEAD_DIM
                query = qkv[i * block : seen, at : at + HEAD_DIM]
                key = qkv[0:seen, own + at : own + at + HEAD_DIM]
                value = qkv[0:seen, 2 * own + at : 2 * own + at + HEAD_DIM]
                scores = jnp.where(lower, dot_nt(query, key), 0.0).astype(bf16)
                result = head_norm(dot(scores, value)).astype(bf16)
                place_at = pl.ds(pl.multiple_of(seq * own + at, HEAD_DIM), HEAD_DIM)
                att[i * block : seen, place_at] = result
        attended[r].forward(seq)

    def part_copy(r):
        return remote(psend.at[r], precv.at[r], p_c.at[0, r], p_c.at[1, r], other_c)

    def sum_copy(r):
        return remote(xsend.at[r], xrecv.at[r], p_x.at[0, r], p_x.at[1, r], other_x)

    def project(r):
        rows = pl.ds(pl.multiple_of(r * half_rows + (1 - core) * block, block), block)
        psend[r] = dot_nt(att[rows, :], w3[...]).astype(bf16)
        part_copy(r).start()
        rows = pl.ds(pl.multiple_of(r * half_rows + core * block, block), block)
        mine = dot_nt(att[rows, :], w3[...])
        part_copy(r).wait_recv()
        xsend[r] = (mine + precv[r].astype(f32)).astype(bf16)
        sum_copy(r).start()

    for i in range(1, n_seq):
        for r in range(2):
            attended[r].arrive(near[i])
            attended[r].forward(near[i])
            if i == n_seq - 1:
                project(r)

    residual = [
        Chain(
            lambda p, r=r: res.at[
                pl.ds(pl.multiple_of(r * half_rows + core * block, block), block),
                aligned(p, depth),
            ],
            r_zs.at[r], r_zr.at[r],
        )
        for r in range(2)
    ]

    def res_over(p, r, side):
        ref = res.at[
            pl.ds(pl.multiple_of(r * half_rows + side * block, block), block), aligned(p, depth)
        ]
        return remote(ref, ref, r_c.at[0, r, p], r_c.at[1, r, p], other_c)

    for r in range(2):
        sum_copy(r).wait_recv()
        rows = pl.ds(pl.multiple_of(r * half_rows + core * block, block), block)
        cols = aligned(seq, depth)
        res[rows, cols] = (
            xall[rows, cols].astype(f32) + (xsend[r].astype(f32) + xrecv[r].astype(f32))
        ).astype(bf16)
        residual[r].forward(seq)
        res_over(seq, r, core).start()

    def gather(p):
        for r in range(2):
            res_over(p, r, 1 - core).wait_recv()
        cols = aligned(p, depth)

        def scale(j, carry):
            rows = pl.ds(pl.multiple_of(j * 64, 64), 64)
            value = res[rows, cols].astype(f32)
            square = value * value
            add = square[:, 0:128]
            for k in range(128, depth, 128):
                add += square[:, k : k + 128]
            ssq[rows, :] += add
            ms[rows, :] = (value * moe_gain[:, cols]).astype(bf16)
            return carry

        lax.fori_loop(0, total // 64, scale, 0)
        for k in range(0, depth, 256):
            xs[:, pl.ds(pl.multiple_of(p * depth + k, 256), 256)] = dot(
                pick[...], ms[:, k : k + 256]
            ).astype(bf16)

    ssq[...] = jnp.zeros_like(ssq)
    for i in range(1, n_seq + 1):
        if i < n_seq:
            for r in range(2):
                residual[r].arrive(near[i])
                residual[r].forward(near[i])
                res_over(near[i], r, core).start()
        gather(near[i - 1])
    factor = lax.rsqrt(jnp.sum(ssq[...], axis=-1, keepdims=True) * (1.0 / width) + 1e-06)
    high = factor.astype(bf16).astype(f32)
    middle = (factor - high).astype(bf16).astype(f32)
    lane = lax.broadcasted_iota(jnp.int32, (total, 128), 1)
    terms = jnp.where(
        lane == 0, high, jnp.where(lane == 1, middle, jnp.where(lane == 2, factor - high - middle, 0.0))
    )
    per_slot = jnp.sum(dot(pick[...], terms.astype(bf16)), axis=-1, keepdims=True)
    fs[...] = jnp.broadcast_to(per_slot, fs.shape)

    def inner(e):
        slot = lax.rem(e, ring)
        for copy in fetch(e, slot):
            copy.wait()
        rows = pl.ds(pl.multiple_of(e * slots, slots), slots)
        x = xs[rows, :]
        scale = fs[rows, 0:1]
        gate_val = dot(x, gbuf[slot]) * scale
        up_val = dot(x, ubuf[slot]) * scale
        hid[rows, :] = (gate_val * jax.nn.sigmoid(gate_val) * up_val).astype(bf16)

        @pl.when(e + ring < amount)
        def _():
            for copy in fetch(e + ring, slot):
                copy.start()

    def inner_pair(j, carry):
        inner(2 * j)
        inner(2 * j + 1)
        return carry

    lax.fori_loop(0, amount // 2, inner_pair, 0)

    def wait_down(e, carry):
        fetch_down(e).wait()
        return carry

    lax.fori_loop(0, amount, wait_down, 0)

    def down(side):
        cols = aligned(side, 2 * span)

        def step(j, carry):
            for e in (2 * j, 2 * j + 1):
                rows = pl.ds(pl.multiple_of(e * slots, slots), slots)
                xs[rows, cols] = dot(hid[rows, :], dbuf[e, :, cols]).astype(bf16)
            return carry

        lax.fori_loop(0, amount // 2, step, 0)

    def pair_copy(u, p):
        return remote(csend.at[u, p], crecv.at[u, p], o_c.at[0, u, p], o_c.at[1, u, p], other_c)

    def over_copy(p):
        return remote(osend.at[p], orecv.at[p], o_x.at[0, p], o_x.at[1, p], other_x)

    def back_copy(to, origin):
        return remote(
            zsend.at[to], zrecv.at[origin], o_z.at[0, to], o_z.at[1, origin], {"seq": to}
        )

    def share_out(u, side, p):
        rows = aligned(p, local)
        cols = pl.ds(pl.multiple_of(side * 2 * span + (1 - core) * span, span), span)
        csend[u, p] = dot(mix[rows, :], xs[:, cols]).astype(bf16)
        pair_copy(u, p).start()
        cols = pl.ds(pl.multiple_of(side * 2 * span + core * span, span), span)
        keep[p] = dot(mix[rows, :], xs[:, cols])

    order = near[::-1]

    def hand_over(p):
        pair_copy(0, p).wait_recv()
        osend[p] = (keep[p] + crecv[0, p].astype(f32)).astype(bf16)
        over_copy(p).start()

    down(1 - col)
    for n in range(n_seq + 1):
        if n < n_seq:
            share_out(0, 1 - col, order[n])
        if n > 0:
            hand_over(order[n - 1])

    def add_up(p):
        pair_copy(1, p).wait_recv()
        over_copy(p).wait_recv()
        return keep[p] + crecv[1, p].astype(f32) + orecv[p].astype(f32)

    down(col)
    for p in order:
        share_out(1, col, p)
    for p in order[:-1]:
        zsend[p] = add_up(p).astype(bf16)
        back_copy(p, seq).start()
    mine_cols = aligned(head, span)
    summed = add_up(seq) + res[aligned(seq, local), mine_cols].astype(f32)
    for p in order[:-1]:
        back_copy(p, p).wait_recv()
        summed = summed + zrecv[p].astype(f32)
    share[...] = summed.astype(bf16)

    def final_copy(owner, k, target, source=None):
        ref = o_ref.at[:, aligned(owner, span)]
        return remote(share if source is None else ref, ref, f_sems.at[0, k], f_sems.at[1, k], target)

    finals = [final_copy(head, 0, other_x), final_copy(head, 1, other_c)]
    for copy in finals:
        copy.start()
    o_ref[:, mine_cols] = share[...]
    finals[0].wait_recv()
    finals.append(final_copy(flip(head, 2), 2, other_c, o_ref))
    finals[2].start()
    for copy in finals[1:]:
        copy.wait_recv()

    for copy in finals:
        copy.wait_send()
    tokens_z.sent(seq)
    for chain in attended + residual:
        chain.sent(seq)
    for p in near[1:]:
        tokens_z.sent(p)
        table_copy(p, seq).wait_send()
        across(p).wait_send()
        for which in range(2):
            beside(p, which).wait_send()
        for which in range(3):
            w_copy(which, p).wait_send()
            if n_grp > 1:
                w_over(which, p).wait_send()
        for chain in attended + residual:
            chain.sent(p)
        back_copy(p, seq).wait_send()
    for r in range(2):
        part_copy(r).wait_send()
        sum_copy(r).wait_send()
        for p in near:
            res_over(p, r, core).wait_send()
    for p in near:
        over_copy(p).wait_send()
        for u in range(2):
            pair_copy(u, p).wait_send()


def layer(
    tokens, attn_weight, attn_gain, moe_gain, routes, gates, expert_gate, expert_up, expert_down
):
    local, width = tokens.shape
    n_seq = lax.axis_size("seq")
    total = n_seq * local
    depth, columns = attn_weight.shape[1:]
    own = columns // n_seq
    amount, _, inner = expert_gate.shape
    slots = -(-CAP * n_seq // 16) * 16
    span = width // 4
    ring = min(8, amount)
    small = jnp.concatenate([routes.T.astype(jnp.float32), gates.T])
    bf16, f32 = jnp.bfloat16, jnp.float32
    vmem, sem = pltpu.VMEM, pltpu.SemaphoreType.DMA
    block = total // 4
    here, away = pl.BlockSpec(memory_space=pltpu.VMEM), pl.BlockSpec(memory_space=pl.ANY)
    return pl.pallas_call(
        functools.partial(layer_kernel, slots),
        out_shape=jax.ShapeDtypeStruct(tokens.shape, tokens.dtype),
        in_specs=[here, away, here, here, here, away, away, away],
        out_specs=here,
        scratch_shapes=[
            vmem((total, width), bf16),
            vmem((total, width), bf16),
            vmem((n_seq, depth, 3 * own), bf16),
            vmem((depth, columns), bf16),
            vmem((total, 3 * own), f32),
            vmem((total, 3 * own), bf16),
            vmem((total, columns), bf16),
            vmem((2, block, depth), bf16),
            vmem((2, block, depth), bf16),
            vmem((2, block, depth), bf16),
            vmem((2, block, depth), bf16),
            vmem((total, width), bf16),
            vmem((small.shape[0], total), f32),
            vmem((amount * slots, total), bf16),
            vmem((total, amount * slots), bf16),
            vmem((amount * slots, width), bf16),
            vmem((total, 128), f32),
            vmem((amount * slots, 128), f32),
            vmem((total, depth), bf16),
            vmem((amount * slots, inner), bf16),
            vmem((ring, width, inner), bf16),
            vmem((ring, width, inner), bf16),
            vmem((amount, inner, width), bf16),
            vmem((2, n_seq, local, span), bf16),
            vmem((2, n_seq, local, span), bf16),
            vmem((n_seq, local, span), f32),
            vmem((n_seq, local, span), bf16),
            vmem((n_seq, local, span), bf16),
            vmem((n_seq, local, span), bf16),
            vmem((n_seq, local, span), bf16),
            vmem((local, span), bf16),
            sem((4,)),
            sem((2, 3, n_seq)),
            sem((2, 3, n_seq)),
            sem((2, n_seq)),
            sem((n_seq,)),
            sem((2, n_seq)),
            sem((2, 2, n_seq)),
            sem((2, n_seq)),
            sem((2, 2, n_seq)),
            sem((2, n_seq)),
            sem((2, 2)),
            sem((2, 2)),
            sem((2, 2, n_seq)),
            sem((2, n_seq)),
            sem((2, 2, n_seq)),
            sem((ring,)),
            sem((ring,)),
            sem((amount,)),
            sem((2, 2, n_seq)),
            sem((2, n_seq)),
            sem((2, n_seq)),
            sem((2, 3)),
        ],
        compiler_params=pltpu.CompilerParams(
            collective_id=2, has_side_effects=True, vmem_limit_bytes=VMEM_LIMIT
        ),
    )(
        tokens, attn_weight, attn_gain[None], moe_gain[None], small,
        expert_gate, expert_up, expert_down,
    )


def fits(mesh, tokens, attn_weight, expert_gate):
    n_seq, local = mesh.shape["seq"], tokens.shape[0]
    own = attn_weight.shape[2] // n_seq
    return (
        mesh.shape["head"] == 4
        and mesh.shape["grp"] <= 2
        and n_seq > 1
        and own % HEAD_DIM == 0
        and attn_weight.shape[2] % n_seq == 0
        and local % 128 == 0
        and n_seq * local <= 512
        and expert_gate.shape[0] <= 16
        and expert_gate.shape[0] % 2 == 0
    )


def solution(mesh):
    def run(tokens, attn_weight, attn_gain, moe_gain, routes, gates, *experts):
        whole = layer if fits(mesh, tokens, attn_weight, experts[0]) else body
        return whole(tokens, attn_weight, attn_gain, moe_gain, routes, gates, *experts)

    return jax.shard_map(
        run,
        mesh=mesh,
        in_specs=(
            P(("grp", "seq"), None),
            P(None, "seq", "head"),
            P(),
            P(),
            P(("grp", "seq"), None),
            P(("grp", "seq"), None),
            P("seq", None, "head"),
            P("seq", None, "head"),
            P("seq", "head", None),
        ),
        out_specs=P(("grp", "seq"), None),
        check_vma=False,
    )
```

```python
import functools

import jax
import jax.numpy as jnp
from jax import lax
from jax.experimental import pallas as pl
from jax.experimental.pallas import tpu as pltpu
from jax.sharding import PartitionSpec as P

HEAD_DIM = 128
EXPERTS = 64
TOPK = 8
CAP = 18
MESH = pl.DeviceIdType.MESH
VMEM_LIMIT = 63 * 1024 * 1024
XCUT = 2
WCUT = 2
WAHEAD = 2
SCHEDULE = [
    ("x", 1), ("x", 2), ("w", 0), ("x", 3), ("a", 1), ("w", 1), ("a", 2), ("w", 2), ("a", 3), ("w", 3),
    ("w", 4), ("w", 5),
]
CUTS = 4


PRECISE = lax.Precision.HIGHEST


def prefix_2(array, axis, combine, identity):
    peers, position = (lax.axis_size(axis), lax.axis_index(axis))
    everything = lax.all_gather(array.astype(jnp.bfloat16), axis)
    start = jnp.broadcast_to(jnp.asarray(identity, array.dtype), array.shape)

    def hop(k, before):
        reached = k < position
        new = combine(before, everything[k].astype(array.dtype))
        return jnp.where(reached, new, before)

    return lax.fori_loop(0, peers, hop, start)


def rms_scale(row_block, gain_vec):
    widened = row_block.astype(jnp.float32)
    factor = lax.rsqrt(jnp.mean(widened * widened, axis=-1, keepdims=True) + 1e-06)
    return widened * factor * gain_vec


def head_norm(outputs):
    return outputs * lax.rsqrt(jnp.mean(outputs * outputs, axis=-1, keepdims=True) + 1e-06)


def add_states(earlier, later):
    return earlier + later


def slot_numbers(route_flat):
    one_hot = (route_flat[:, None] == jnp.arange(EXPERTS, dtype=jnp.int32)[None, :]).astype(
        jnp.int32
    )
    earlier = jnp.cumsum(one_hot, axis=0) - one_hot
    return route_flat * CAP + jnp.sum(earlier * one_hot, axis=1)


def make_runner(expert_gate, expert_up, expert_down):

    def run_experts(received):
        gate_val = jnp.einsum(
            "necd,edf->necf", received, expert_gate, preferred_element_type=jnp.float32
        )
        up_val = jnp.einsum(
            "necd,edf->necf", received, expert_up, preferred_element_type=jnp.float32
        )
        hidden = (jax.nn.silu(gate_val) * up_val).astype(jnp.bfloat16)
        partial_value = jnp.einsum(
            "necf,efd->necd", hidden, expert_down, preferred_element_type=jnp.float32
        ).astype(jnp.bfloat16)
        groups = lax.axis_size("head")
        shape_now = partial_value.shape
        split = partial_value.reshape(
            shape_now[0], shape_now[1], shape_now[2], groups, shape_now[3] // groups
        )
        by_group = lax.all_to_all(split, "head", split_axis=3, concat_axis=3, tiled=True)
        summed = jnp.sum(by_group.astype(jnp.float32), axis=3)
        return lax.all_to_all(
            summed.astype(jnp.bfloat16), "seq", split_axis=0, concat_axis=0, tiled=True
        ).astype(summed.dtype)

    return run_experts


def body(
    tokens, attn_weight, attn_gain, moe_gain, routes, gates, expert_gate, expert_up, expert_down
):
    local_rows = tokens.shape[0]
    normed = rms_scale(tokens, attn_gain).astype(jnp.bfloat16)
    weights = lax.all_gather(attn_weight, "seq", axis=1, tiled=True)
    head_count = weights.shape[2] // HEAD_DIM
    projected = [
        jnp.dot(normed, weights[which], preferred_element_type=jnp.float32)
        .astype(jnp.bfloat16)
        .reshape(local_rows, head_count, HEAD_DIM)
        for which in range(3)
    ]
    query_rows, key_rows, value_rows = projected
    own_state = jnp.einsum("thd,the->hde", key_rows, value_rows, preferred_element_type=jnp.float32)
    prefix = prefix_2(own_state, "seq", add_states, jnp.zeros_like(own_state))
    inter_part = jnp.einsum(
        "thd,hde->the", query_rows.astype(jnp.float32), prefix, precision=PRECISE
    )
    scores = jnp.einsum("thd,shd->hts", query_rows, key_rows, preferred_element_type=jnp.float32)
    lower_mask = jnp.arange(local_rows)[:, None] >= jnp.arange(local_rows)[None, :]
    scores = jnp.where(lower_mask[None], scores, 0.0)
    intra_part = jnp.einsum(
        "hts,she->the", scores, value_rows.astype(jnp.float32), precision=PRECISE
    )
    attended = (
        head_norm(inter_part + intra_part)
        .reshape(local_rows, head_count * HEAD_DIM)
        .astype(jnp.bfloat16)
    )
    out_part = lax.dot_general(
        attended, weights[3], (((1,), (1,)), ((), ())), preferred_element_type=jnp.float32
    )
    residual = (
        tokens.astype(jnp.float32)
        + lax.psum(out_part.astype(jnp.bfloat16), "head").astype(jnp.float32)
    ).astype(jnp.bfloat16)
    moe_in = rms_scale(residual, moe_gain).astype(jnp.bfloat16)
    route_flat = routes.reshape(-1)
    slots = slot_numbers(route_flat)
    owners = lax.axis_size("seq")
    local_experts = expert_gate.shape[0]
    source_row = jnp.arange(route_flat.shape[0], dtype=jnp.int32) // TOPK
    run_experts = make_runner(expert_gate, expert_up, expert_down)
    outbound = (
        jnp.zeros((EXPERTS * CAP, moe_in.shape[1]), jnp.bfloat16).at[slots].set(moe_in[source_row])
    )
    outbound = outbound.reshape(owners, local_experts, CAP, moe_in.shape[1])
    returned = run_experts(lax.all_to_all(outbound, "seq", split_axis=0, concat_axis=0, tiled=True))
    arrived = returned.reshape(EXPERTS * CAP, -1)[slots].reshape(local_rows, TOPK, -1)
    moe_partial = jnp.einsum("tkd,tk->td", arrived, gates, precision=PRECISE)
    column_span = moe_partial.shape[1]
    residual_share = lax.dynamic_slice_in_dim(
        residual, lax.axis_index("head") * column_span, column_span, 1
    )
    mixed_share = (residual_share.astype(jnp.float32) + moe_partial).astype(jnp.bfloat16)
    return lax.all_gather(mixed_share, "head", axis=1, tiled=True)


def flip(index, bit):
    return index + bit * (1 - 2 * lax.rem(index // bit, 2))


def remote(source, dest, send_sem, recv_sem, target):
    return pltpu.make_async_remote_copy(
        src_ref=source,
        dst_ref=dest,
        send_sem=send_sem,
        recv_sem=recv_sem,
        device_id=target,
        device_id_type=MESH,
    )


def aligned(index, size):
    return pl.ds(pl.multiple_of(index * size, size), size)


def dot(a, b):
    return jnp.dot(a, b, preferred_element_type=jnp.float32)


def dot_nt(a, b):
    return lax.dot_general(a, b, (((1,), (1,)), ((), ())), preferred_element_type=jnp.float32)


def nearest(i, me, peers):
    both = jnp.minimum(me, peers - 1 - me)
    step = (i + 1) // 2
    side = -1 if i % 2 else 1
    rest = jnp.where(me <= peers - 1 - me, i - both, both - i)
    return me + jnp.where(i <= 2 * both, side * step, rest)


class Chain:
    def __init__(self, piece, sends, recvs, left):
        self.piece, self.sends, self.recvs, self.left = piece, sends, recvs, left
        self.peers, self.me = lax.axis_size("seq"), lax.axis_index("seq")

    def copy(self, origin, way):
        ref = self.piece(origin)
        to = lax.rem(self.me + (self.peers - 1 if way else 1), self.peers)
        return remote(ref, ref, self.sends.at[way, origin], self.recvs.at[origin], {"seq": to})

    def wanted(self, origin, way):
        if way:
            return (origin >= self.me) & (self.me > 0)
        return (origin <= self.me) & (self.me < self.peers - 1)

    def arrive(self, origin):
        self.copy(origin, 0).wait_recv()

    def forward(self, origin):
        self.left.append(lambda: self.sent(origin))
        for way in range(2):

            @pl.when(self.wanted(origin, way))
            def _():
                self.copy(origin, way).start()

    def sent(self, origin):
        for way in range(2):

            @pl.when(self.wanted(origin, way))
            def _():
                self.copy(origin, way).wait_send()


def layer_kernel(slots, *refs):
    (
        tok, aw, attn_gain, moe_gain, routes, gates, eg, eu, ed, o_ref,
        xall, xn, wbuf, w3, acc, qkv, att, psend, precv, pown, xsend, xrecv, res, sm, pick, mix, xs, ssq,
        fs, ms, hid, gbuf, ubuf, dbuf, csend, crecv, keep, osend, orecv, zsend, zrecv, share,
        own_sems, w_z, w_y, x_zs, x_zr, x_x, x_c, s_sems, a_zs, a_zr, p_c, p_x, r_zs, r_zr, r_c,
        g_sems, u_sems, d_sems, o_c, o_x, o_z, f_sems,
    ) = refs
    f32, bf16 = jnp.float32, jnp.bfloat16
    n_seq, n_grp = lax.axis_size("seq"), lax.axis_size("grp")
    grp, seq, head = lax.axis_index("grp"), lax.axis_index("seq"), lax.axis_index("head")
    core, col = lax.rem(head, 2), head // 2
    other_x, other_c = {"head": flip(head, 2)}, {"head": flip(head, 1)}
    other_y = {"grp": lax.rem(grp + 1, n_grp)}
    local, width = tok.shape
    total = n_seq * local
    depth, columns = aw.shape[1:]
    own = columns // n_seq
    part = depth // n_grp
    quarter = local // 4
    amount, ring = ed.shape[0], gbuf.shape[0]
    span = width // 4
    near = [nearest(i, seq, n_seq) for i in range(n_seq)]

    left = []

    def go(copy):
        left.append(copy.wait_send)
        copy.start()

    barrier = pltpu.get_barrier_semaphore()
    friends = [{"seq": lax.rem(seq + k, n_seq)} for k in range(1, n_seq)] + [other_x, other_c]
    if n_grp > 1:
        friends.append(other_y)
    for friend in friends:
        pl.semaphore_signal(barrier, inc=1, device_id=friend, device_id_type=MESH)

    own_copies = [
        pltpu.make_async_copy(
            aw.at[which, :, aligned(seq, own)],
            wbuf.at[seq, :, pl.ds(which * own, own)],
            own_sems.at[which],
        )
        for which in range(3)
    ] + [pltpu.make_async_copy(aw.at[3], w3, own_sems.at[3])]
    for copy in own_copies:
        copy.start()
    xall[aligned(seq, local), :] = tok[...]
    top = routes.shape[0]
    sm[0:top, aligned(seq, local)] = routes[...].astype(f32)
    sm[top:, aligned(seq, local)] = gates[...]
    pl.semaphore_wait(barrier, len(friends))

    def token_rows(p, owner, n):
        start = p * local + owner * quarter + n * (quarter // XCUT)
        return xall.at[pl.ds(pl.multiple_of(start, quarter // XCUT), quarter // XCUT), :]

    tokens_z = [
        Chain(lambda p, n=n: token_rows(p, head, n), x_zs.at[n], x_zr.at[n], left)
        for n in range(XCUT)
    ]
    for chain in tokens_z:
        chain.forward(seq)

    def table_copy(to, origin):
        ref = sm.at[:, aligned(origin, local)]
        return remote(ref, ref, s_sems.at[0, to], s_sems.at[1, origin], {"seq": to})

    deep = part // WCUT

    def w_rows(side, n):
        return pl.ds(pl.multiple_of(side * part + n % WCUT * deep, deep), deep)

    def w_cols(n):
        return pl.ds(n // WCUT * own, own)

    def w_copy(n, to):
        return remote(
            aw.at[n // WCUT, w_rows(grp, n), aligned(to, own)],
            wbuf.at[seq, w_rows(grp, n), w_cols(n)],
            w_z.at[0, n, to], w_z.at[1, n, seq], {"seq": to},
        )

    def w_arrival(n, origin):
        ref = wbuf.at[origin, w_rows(grp, n), w_cols(n)]
        return remote(ref, ref, w_z.at[0, n, origin], w_z.at[1, n, origin], {"seq": origin})

    def w_over(n, origin, side):
        ref = wbuf.at[origin, w_rows(side, n), w_cols(n)]
        return remote(ref, ref, w_y.at[0, n, origin], w_y.at[1, n, origin], other_y)

    def send_w(n):
        for p in reversed(near[1:]):
            go(w_copy(n, p))

    for p in near[1:]:
        go(table_copy(p, seq))
    for n in range(WAHEAD):
        send_w(n)

    def fetch(e, slot):
        return [
            pltpu.make_async_copy(eg.at[e], gbuf.at[slot], g_sems.at[slot]),
            pltpu.make_async_copy(eu.at[e], ubuf.at[slot], u_sems.at[slot]),
        ]

    def fetch_down(e):
        return pltpu.make_async_copy(ed.at[e], dbuf.at[e], d_sems.at[e])

    def begin(e, carry):
        for copy in fetch(e, e):
            copy.start()
        return carry

    def begin_down(e, carry):
        fetch_down(e).start()
        return carry

    lax.fori_loop(0, ring, begin, 0)
    lax.fori_loop(0, amount, begin_down, 0)

    def norm_rows(p):
        def step(j, carry):
            rows = pl.ds(pl.multiple_of(p * local + j * quarter, quarter), quarter)
            value = xall[rows, :].astype(f32)
            factor = lax.rsqrt(jnp.mean(value * value, axis=-1, keepdims=True) + 1e-06)
            xn[rows, :] = (value * factor * attn_gain[...]).astype(bf16)
            return carry

        lax.fori_loop(0, 4, step, 0)

    norm_rows(seq)

    def across(p, n):
        ref = token_rows(p, head, n)
        return remote(ref, ref, x_x.at[0, n, p], x_x.at[1, n, p], other_x)

    def beside(p, which, n):
        ref = token_rows(p, flip(head, 2) if which else head, n)
        return remote(ref, ref, x_c.at[0, which, n, p], x_c.at[1, which, n, p], other_c)

    for kind, at in SCHEDULE:
        if kind == "w":
            for p in near[1:]:
                w_arrival(at, p).wait_recv()
                if n_grp > 1:
                    go(w_over(at, p, grp))
            if at + WAHEAD < 3 * WCUT:
                send_w(at + WAHEAD)
        elif at < n_seq:
            p = near[at]
            for n in range(XCUT):
                if kind == "x":
                    tokens_z[n].arrive(p)
                    tokens_z[n].forward(p)
                    go(across(p, n))
                    go(beside(p, 0, n))
                else:
                    across(p, n).wait_recv()
                    go(beside(p, 1, n))

    for p in near[1:]:
        table_copy(p, p).wait_recv()
    ids = lax.broadcasted_iota(jnp.int32, (128, total), 0).astype(f32)
    ids = ids + (seq * amount).astype(f32)
    named = jnp.zeros((128, total), f32)
    weight = jnp.zeros((128, total), f32)
    for k in range(top):
        hit = sm[k : k + 1, :] == ids
        named = jnp.where(hit, 1.0, named)
        weight = jnp.where(hit, sm[top + k : top + k + 1, :], weight)
    before = lax.broadcasted_iota(jnp.int32, (total, total), 0) < lax.broadcasted_iota(
        jnp.int32, (total, total), 1
    )
    rank = dot(named.astype(bf16), jnp.where(before, 1.0, 0.0).astype(bf16))
    place = jnp.where(named > 0.0, rank, -1.0)
    spot = lax.broadcasted_iota(jnp.int32, (slots, total), 0).astype(f32)
    for e in range(amount):
        pick[e * slots : (e + 1) * slots, :] = jnp.where(
            place[e : e + 1, :] == spot, 1.0, 0.0
        ).astype(bf16)
    wide = lax.broadcasted_iota(jnp.int32, (128, amount * slots), 1).astype(f32)
    owner = jnp.floor((wide + 0.5) * (1.0 / slots))
    mine = lax.broadcasted_iota(jnp.int32, (128, amount * slots), 0).astype(f32)
    spread = jnp.where(owner == mine, 1.0, 0.0).astype(bf16)
    spot_of = (wide - owner * slots)[:1, :]
    place_t = jnp.transpose(place).astype(bf16)
    weight_t = jnp.transpose(weight).astype(bf16)
    for b in range(0, total, 128):
        mix[b : b + 128, :] = jnp.where(
            dot(place_t[b : b + 128], spread) == spot_of, dot(weight_t[b : b + 128], spread), 0.0
        ).astype(bf16)

    for i in range(1, n_seq):
        for n in range(XCUT):
            beside(near[i], 0, n).wait_recv()
            beside(near[i], 1, n).wait_recv()
        norm_rows(near[i])
    for copy in own_copies:
        copy.wait()
    acc[...] = dot(xn[:, aligned(seq, depth)], wbuf[seq])
    for i in range(1, n_seq):
        p = near[i]
        if n_grp > 1:
            for n in range(3 * WCUT):
                w_over(n, p, lax.rem(grp + 1, n_grp)).wait_recv()
        acc[...] += dot(xn[:, aligned(p, depth)], wbuf[p])
    qkv[...] = acc[...].astype(bf16)

    cut = total // CUTS
    attended = [
        Chain(
            lambda p, n=n: att.at[pl.ds(n * cut, cut), aligned(p, own)],
            a_zs.at[n], a_zr.at[n], left,
        )
        for n in range(CUTS)
    ]
    for n in range(CUTS):
        seen = (n + 1) * cut
        lower = (
            lax.broadcasted_iota(jnp.int32, (cut, seen), 0) + n * cut
            >= lax.broadcasted_iota(jnp.int32, (cut, seen), 1)
        )
        for a in range(own // HEAD_DIM):
            at = a * HEAD_DIM
            query = qkv[n * cut : seen, at : at + HEAD_DIM]
            key = qkv[0:seen, own + at : own + at + HEAD_DIM]
            value = qkv[0:seen, 2 * own + at : 2 * own + at + HEAD_DIM]
            scores = jnp.where(lower, dot_nt(query, key), 0.0).astype(bf16)
            result = head_norm(dot(scores, value)).astype(bf16)
            place_at = pl.ds(pl.multiple_of(seq * own + at, HEAD_DIM), HEAD_DIM)
            att[n * cut : seen, place_at] = result
        attended[n].forward(seq)

    block = cut // 2

    def block_rows(n, side):
        return pl.ds(pl.multiple_of(n * cut + side * block, block), block)

    def part_copy(n):
        return remote(psend.at[n], precv.at[n], p_c.at[0, n], p_c.at[1, n], other_c)

    def sum_copy(n):
        return remote(xsend.at[n], xrecv.at[n], p_x.at[0, n], p_x.at[1, n], other_x)

    residual = [
        Chain(
            lambda p, n=n: res.at[block_rows(n, core), aligned(p, depth)],
            r_zs.at[n], r_zr.at[n], left,
        )
        for n in range(CUTS)
    ]

    def res_over(p, n, side):
        ref = res.at[block_rows(n, side), aligned(p, depth)]
        return remote(ref, ref, r_c.at[0, n, p], r_c.at[1, n, p], other_c)

    def project(n):
        psend[n] = dot_nt(att[block_rows(n, 1 - core), :], w3[...]).astype(bf16)
        go(part_copy(n))
        pown[n] = dot_nt(att[block_rows(n, core), :], w3[...])

    def join(n):
        part_copy(n).wait_recv()
        xsend[n] = (pown[n] + precv[n].astype(f32)).astype(bf16)
        go(sum_copy(n))

    def settle(n):
        sum_copy(n).wait_recv()
        rows, cols = block_rows(n, core), aligned(seq, depth)
        res[rows, cols] = (
            xall[rows, cols].astype(f32) + (xsend[n].astype(f32) + xrecv[n].astype(f32))
        ).astype(bf16)
        residual[n].forward(seq)
        go(res_over(seq, n, core))

    for i in range(1, n_seq):
        for n in range(CUTS):
            attended[n].arrive(near[i])
            attended[n].forward(near[i])
            if i == n_seq - 1:
                project(n)
                if n > 0:
                    join(n - 1)
    join(CUTS - 1)
    for n in range(CUTS):
        settle(n)

    def gather(p):
        for n in range(CUTS):
            res_over(p, n, 1 - core).wait_recv()
        cols = aligned(p, depth)

        def scale(j, carry):
            rows = pl.ds(pl.multiple_of(j * 64, 64), 64)
            value = res[rows, cols].astype(f32)
            square = value * value
            add = square[:, 0:128]
            for k in range(128, depth, 128):
                add += square[:, k : k + 128]
            ssq[rows, :] += add
            ms[rows, :] = (value * moe_gain[:, cols]).astype(bf16)
            return carry

        lax.fori_loop(0, total // 64, scale, 0)
        for k in range(0, depth, 256):
            xs[:, pl.ds(pl.multiple_of(p * depth + k, 256), 256)] = dot(
                pick[...], ms[:, k : k + 256]
            ).astype(bf16)

    ssq[...] = jnp.zeros_like(ssq)
    for i in range(1, n_seq + 1):
        if i < n_seq:
            for n in range(CUTS):
                residual[n].arrive(near[i])
                residual[n].forward(near[i])
                go(res_over(near[i], n, core))
        gather(near[i - 1])
    factor = lax.rsqrt(jnp.sum(ssq[...], axis=-1, keepdims=True) * (1.0 / width) + 1e-06)
    high = factor.astype(bf16).astype(f32)
    middle = (factor - high).astype(bf16).astype(f32)
    lane = lax.broadcasted_iota(jnp.int32, (total, 128), 1)
    terms = jnp.where(
        lane == 0, high, jnp.where(lane == 1, middle, jnp.where(lane == 2, factor - high - middle, 0.0))
    )
    per_slot = jnp.sum(dot(pick[...], terms.astype(bf16)), axis=-1, keepdims=True)
    fs[...] = jnp.broadcast_to(per_slot, fs.shape)

    def inner(e):
        slot = lax.rem(e, ring)
        for copy in fetch(e, slot):
            copy.wait()
        rows = pl.ds(pl.multiple_of(e * slots, slots), slots)
        x = xs[rows, :]
        scale = fs[rows, 0:1]
        gate_val = dot(x, gbuf[slot]) * scale
        up_val = dot(x, ubuf[slot]) * scale
        hid[rows, :] = (gate_val * jax.nn.sigmoid(gate_val) * up_val).astype(bf16)

        @pl.when(e + ring < amount)
        def _():
            for copy in fetch(e + ring, slot):
                copy.start()

    def inner_pair(j, carry):
        inner(2 * j)
        inner(2 * j + 1)
        return carry

    lax.fori_loop(0, amount // 2, inner_pair, 0)

    def wait_down(e, carry):
        fetch_down(e).wait()
        return carry

    lax.fori_loop(0, amount, wait_down, 0)

    def down(side):
        cols = aligned(side, 2 * span)

        def step(j, carry):
            for e in (2 * j, 2 * j + 1):
                rows = pl.ds(pl.multiple_of(e * slots, slots), slots)
                xs[rows, cols] = dot(hid[rows, :], dbuf[e, :, cols]).astype(bf16)
            return carry

        lax.fori_loop(0, amount // 2, step, 0)

    def pair_copy(u, p):
        return remote(csend.at[u, p], crecv.at[u, p], o_c.at[0, u, p], o_c.at[1, u, p], other_c)

    def over_copy(p):
        return remote(osend.at[p], orecv.at[p], o_x.at[0, p], o_x.at[1, p], other_x)

    def back_copy(to, origin):
        return remote(
            zsend.at[to], zrecv.at[origin], o_z.at[0, to], o_z.at[1, origin], {"seq": to}
        )

    def share_out(u, side, p):
        rows = aligned(p, local)
        cols = pl.ds(pl.multiple_of(side * 2 * span + (1 - core) * span, span), span)
        csend[u, p] = dot(mix[rows, :], xs[:, cols]).astype(bf16)
        go(pair_copy(u, p))
        cols = pl.ds(pl.multiple_of(side * 2 * span + core * span, span), span)
        keep[p] = dot(mix[rows, :], xs[:, cols])

    order = near[::-1]

    def hand_over(p):
        pair_copy(0, p).wait_recv()
        osend[p] = (keep[p] + crecv[0, p].astype(f32)).astype(bf16)
        go(over_copy(p))

    down(1 - col)
    for n in range(n_seq + 1):
        if n < n_seq:
            share_out(0, 1 - col, order[n])
        if n > 0:
            hand_over(order[n - 1])

    def add_up(p):
        pair_copy(1, p).wait_recv()
        over_copy(p).wait_recv()
        return keep[p] + crecv[1, p].astype(f32) + orecv[p].astype(f32)

    down(col)
    for p in order:
        share_out(1, col, p)
    for p in order[:-1]:
        zsend[p] = add_up(p).astype(bf16)
        go(back_copy(p, seq))
    mine_cols = aligned(head, span)
    summed = add_up(seq) + res[aligned(seq, local), mine_cols].astype(f32)
    for p in order[:-1]:
        back_copy(p, p).wait_recv()
        summed = summed + zrecv[p].astype(f32)
    share[...] = summed.astype(bf16)

    def final_copy(owner, k, target, source=None):
        ref = o_ref.at[:, aligned(owner, span)]
        return remote(share if source is None else ref, ref, f_sems.at[0, k], f_sems.at[1, k], target)

    finals = [final_copy(head, 0, other_x), final_copy(head, 1, other_c)]
    for copy in finals:
        go(copy)
    o_ref[:, mine_cols] = share[...]
    finals[0].wait_recv()
    finals.append(final_copy(flip(head, 2), 2, other_c, o_ref))
    go(finals[2])
    for copy in finals[1:]:
        copy.wait_recv()

    for wait in left:
        wait()


def layer(
    tokens, attn_weight, attn_gain, moe_gain, routes, gates, expert_gate, expert_up, expert_down
):
    local, width = tokens.shape
    n_seq = lax.axis_size("seq")
    total = n_seq * local
    depth, columns = attn_weight.shape[1:]
    own = columns // n_seq
    amount, _, inner = expert_gate.shape
    slots = -(-CAP * n_seq // 16) * 16
    span = width // 4
    ring = min(8, amount)
    bf16, f32 = jnp.bfloat16, jnp.float32
    vmem, sem = pltpu.VMEM, pltpu.SemaphoreType.DMA
    block = total // CUTS // 2
    here, away = pl.BlockSpec(memory_space=pltpu.VMEM), pl.BlockSpec(memory_space=pl.ANY)
    return pl.pallas_call(
        functools.partial(layer_kernel, slots),
        out_shape=jax.ShapeDtypeStruct(tokens.shape, tokens.dtype),
        in_specs=[here, away, here, here, here, here, away, away, away],
        out_specs=here,
        scratch_shapes=[
            vmem((total, width), bf16),
            vmem((total, width), bf16),
            vmem((n_seq, depth, 3 * own), bf16),
            vmem((depth, columns), bf16),
            vmem((total, 3 * own), f32),
            vmem((total, 3 * own), bf16),
            vmem((total, columns), bf16),
            vmem((CUTS, block, depth), bf16),
            vmem((CUTS, block, depth), bf16),
            vmem((CUTS, block, depth), f32),
            vmem((CUTS, block, depth), bf16),
            vmem((CUTS, block, depth), bf16),
            vmem((total, width), bf16),
            vmem((2 * routes.shape[1], total), f32),
            vmem((amount * slots, total), bf16),
            vmem((total, amount * slots), bf16),
            vmem((amount * slots, width), bf16),
            vmem((total, 128), f32),
            vmem((amount * slots, 128), f32),
            vmem((total, depth), bf16),
            vmem((amount * slots, inner), bf16),
            vmem((ring, width, inner), bf16),
            vmem((ring, width, inner), bf16),
            vmem((amount, inner, width), bf16),
            vmem((2, n_seq, local, span), bf16),
            vmem((2, n_seq, local, span), bf16),
            vmem((n_seq, local, span), f32),
            vmem((n_seq, local, span), bf16),
            vmem((n_seq, local, span), bf16),
            vmem((n_seq, local, span), bf16),
            vmem((n_seq, local, span), bf16),
            vmem((local, span), bf16),
            sem((4,)),
            sem((2, 3 * WCUT, n_seq)),
            sem((2, 3 * WCUT, n_seq)),
            sem((XCUT, 2, n_seq)),
            sem((XCUT, n_seq)),
            sem((2, XCUT, n_seq)),
            sem((2, 2, XCUT, n_seq)),
            sem((2, n_seq)),
            sem((CUTS, 2, n_seq)),
            sem((CUTS, n_seq)),
            sem((2, CUTS)),
            sem((2, CUTS)),
            sem((CUTS, 2, n_seq)),
            sem((CUTS, n_seq)),
            sem((2, CUTS, n_seq)),
            sem((ring,)),
            sem((ring,)),
            sem((amount,)),
            sem((2, 2, n_seq)),
            sem((2, n_seq)),
            sem((2, n_seq)),
            sem((2, 3)),
        ],
        compiler_params=pltpu.CompilerParams(
            collective_id=2, has_side_effects=True, vmem_limit_bytes=VMEM_LIMIT
        ),
    )(
        tokens, attn_weight, attn_gain[None], moe_gain[None], routes.T, gates.T,
        expert_gate, expert_up, expert_down,
    )


def fits(mesh, tokens, attn_weight, expert_gate):
    n_seq, local = mesh.shape["seq"], tokens.shape[0]
    own = attn_weight.shape[2] // n_seq
    return (
        mesh.shape["head"] == 4
        and mesh.shape["grp"] <= 2
        and n_seq > 1
        and own % HEAD_DIM == 0
        and attn_weight.shape[2] % n_seq == 0
        and local % 128 == 0
        and n_seq * local <= 512
        and expert_gate.shape[0] <= 16
        and expert_gate.shape[0] % 2 == 0
    )


def solution(mesh):
    def run(tokens, attn_weight, attn_gain, moe_gain, routes, gates, *experts):
        whole = layer if fits(mesh, tokens, attn_weight, experts[0]) else body
        return whole(tokens, attn_weight, attn_gain, moe_gain, routes, gates, *experts)

    return jax.shard_map(
        run,
        mesh=mesh,
        in_specs=(
            P(("grp", "seq"), None),
            P(None, "seq", "head"),
            P(),
            P(),
            P(("grp", "seq"), None),
            P(("grp", "seq"), None),
            P("seq", None, "head"),
            P("seq", None, "head"),
            P("seq", "head", None),
        ),
        out_specs=P(("grp", "seq"), None),
        check_vma=False,
    )
```

```python
import functools

import jax
import jax.numpy as jnp
from jax import lax
from jax.experimental import pallas as pl
from jax.experimental.pallas import tpu as pltpu
from jax.sharding import PartitionSpec as P

HEAD_DIM = 128
EXPERTS = 64
TOPK = 8
CAP = 18
MESH = pl.DeviceIdType.MESH
VMEM_LIMIT = 63 * 1024 * 1024
XCUT = 2
SCHEDULE = [
    "s0", "x1", "x2", "s1", "x3", "s2", "w0", "s3", "a1", "w1", "s4", "a2",
    "w2", "s5", "a3", "w3", "n1", "n2", "n3", "w4", "t", "w5",
]
SPLIT = 4
CUTS = 4


PRECISE = lax.Precision.HIGHEST


def prefix_2(array, axis, combine, identity):
    peers, position = (lax.axis_size(axis), lax.axis_index(axis))
    everything = lax.all_gather(array.astype(jnp.bfloat16), axis)
    start = jnp.broadcast_to(jnp.asarray(identity, array.dtype), array.shape)

    def hop(k, before):
        reached = k < position
        new = combine(before, everything[k].astype(array.dtype))
        return jnp.where(reached, new, before)

    return lax.fori_loop(0, peers, hop, start)


def rms_scale(row_block, gain_vec):
    widened = row_block.astype(jnp.float32)
    factor = lax.rsqrt(jnp.mean(widened * widened, axis=-1, keepdims=True) + 1e-06)
    return widened * factor * gain_vec


def head_norm(outputs):
    return outputs * lax.rsqrt(jnp.mean(outputs * outputs, axis=-1, keepdims=True) + 1e-06)


def add_states(earlier, later):
    return earlier + later


def slot_numbers(route_flat):
    one_hot = (route_flat[:, None] == jnp.arange(EXPERTS, dtype=jnp.int32)[None, :]).astype(
        jnp.int32
    )
    earlier = jnp.cumsum(one_hot, axis=0) - one_hot
    return route_flat * CAP + jnp.sum(earlier * one_hot, axis=1)


def make_runner(expert_gate, expert_up, expert_down):

    def run_experts(received):
        gate_val = jnp.einsum(
            "necd,edf->necf", received, expert_gate, preferred_element_type=jnp.float32
        )
        up_val = jnp.einsum(
            "necd,edf->necf", received, expert_up, preferred_element_type=jnp.float32
        )
        hidden = (jax.nn.silu(gate_val) * up_val).astype(jnp.bfloat16)
        partial_value = jnp.einsum(
            "necf,efd->necd", hidden, expert_down, preferred_element_type=jnp.float32
        ).astype(jnp.bfloat16)
        groups = lax.axis_size("head")
        shape_now = partial_value.shape
        split = partial_value.reshape(
            shape_now[0], shape_now[1], shape_now[2], groups, shape_now[3] // groups
        )
        by_group = lax.all_to_all(split, "head", split_axis=3, concat_axis=3, tiled=True)
        summed = jnp.sum(by_group.astype(jnp.float32), axis=3)
        return lax.all_to_all(
            summed.astype(jnp.bfloat16), "seq", split_axis=0, concat_axis=0, tiled=True
        ).astype(summed.dtype)

    return run_experts


def body(
    tokens, attn_weight, attn_gain, moe_gain, routes, gates, expert_gate, expert_up, expert_down
):
    local_rows = tokens.shape[0]
    normed = rms_scale(tokens, attn_gain).astype(jnp.bfloat16)
    weights = lax.all_gather(attn_weight, "seq", axis=1, tiled=True)
    head_count = weights.shape[2] // HEAD_DIM
    projected = [
        jnp.dot(normed, weights[which], preferred_element_type=jnp.float32)
        .astype(jnp.bfloat16)
        .reshape(local_rows, head_count, HEAD_DIM)
        for which in range(3)
    ]
    query_rows, key_rows, value_rows = projected
    own_state = jnp.einsum("thd,the->hde", key_rows, value_rows, preferred_element_type=jnp.float32)
    prefix = prefix_2(own_state, "seq", add_states, jnp.zeros_like(own_state))
    inter_part = jnp.einsum(
        "thd,hde->the", query_rows.astype(jnp.float32), prefix, precision=PRECISE
    )
    scores = jnp.einsum("thd,shd->hts", query_rows, key_rows, preferred_element_type=jnp.float32)
    lower_mask = jnp.arange(local_rows)[:, None] >= jnp.arange(local_rows)[None, :]
    scores = jnp.where(lower_mask[None], scores, 0.0)
    intra_part = jnp.einsum(
        "hts,she->the", scores, value_rows.astype(jnp.float32), precision=PRECISE
    )
    attended = (
        head_norm(inter_part + intra_part)
        .reshape(local_rows, head_count * HEAD_DIM)
        .astype(jnp.bfloat16)
    )
    out_part = lax.dot_general(
        attended, weights[3], (((1,), (1,)), ((), ())), preferred_element_type=jnp.float32
    )
    residual = (
        tokens.astype(jnp.float32)
        + lax.psum(out_part.astype(jnp.bfloat16), "head").astype(jnp.float32)
    ).astype(jnp.bfloat16)
    moe_in = rms_scale(residual, moe_gain).astype(jnp.bfloat16)
    route_flat = routes.reshape(-1)
    slots = slot_numbers(route_flat)
    owners = lax.axis_size("seq")
    local_experts = expert_gate.shape[0]
    source_row = jnp.arange(route_flat.shape[0], dtype=jnp.int32) // TOPK
    run_experts = make_runner(expert_gate, expert_up, expert_down)
    outbound = (
        jnp.zeros((EXPERTS * CAP, moe_in.shape[1]), jnp.bfloat16).at[slots].set(moe_in[source_row])
    )
    outbound = outbound.reshape(owners, local_experts, CAP, moe_in.shape[1])
    returned = run_experts(lax.all_to_all(outbound, "seq", split_axis=0, concat_axis=0, tiled=True))
    arrived = returned.reshape(EXPERTS * CAP, -1)[slots].reshape(local_rows, TOPK, -1)
    moe_partial = jnp.einsum("tkd,tk->td", arrived, gates, precision=PRECISE)
    column_span = moe_partial.shape[1]
    residual_share = lax.dynamic_slice_in_dim(
        residual, lax.axis_index("head") * column_span, column_span, 1
    )
    mixed_share = (residual_share.astype(jnp.float32) + moe_partial).astype(jnp.bfloat16)
    return lax.all_gather(mixed_share, "head", axis=1, tiled=True)


def flip(index, bit):
    return index + bit * (1 - 2 * lax.rem(index // bit, 2))


def remote(source, dest, send_sem, recv_sem, target):
    return pltpu.make_async_remote_copy(
        src_ref=source,
        dst_ref=dest,
        send_sem=send_sem,
        recv_sem=recv_sem,
        device_id=target,
        device_id_type=MESH,
    )


def aligned(index, size):
    return pl.ds(pl.multiple_of(index * size, size), size)


def dot(a, b):
    return jnp.dot(a, b, preferred_element_type=jnp.float32)


def dot_nt(a, b):
    return lax.dot_general(a, b, (((1,), (1,)), ((), ())), preferred_element_type=jnp.float32)


def nearest(i, me, peers):
    both = jnp.minimum(me, peers - 1 - me)
    step = (i + 1) // 2
    side = -1 if i % 2 else 1
    rest = jnp.where(me <= peers - 1 - me, i - both, both - i)
    return me + jnp.where(i <= 2 * both, side * step, rest)


class Chain:
    def __init__(self, piece, sends, recvs, left):
        self.piece, self.sends, self.recvs, self.left = piece, sends, recvs, left
        self.peers, self.me = lax.axis_size("seq"), lax.axis_index("seq")

    def copy(self, origin, way):
        ref = self.piece(origin)
        to = lax.rem(self.me + (self.peers - 1 if way else 1), self.peers)
        return remote(ref, ref, self.sends.at[way, origin], self.recvs.at[origin], {"seq": to})

    def wanted(self, origin, way):
        if way:
            return (origin >= self.me) & (self.me > 0)
        return (origin <= self.me) & (self.me < self.peers - 1)

    def arrive(self, origin):
        self.copy(origin, 0).wait_recv()

    def forward(self, origin):
        self.left.append(lambda: self.sent(origin))
        for way in range(2):

            @pl.when(self.wanted(origin, way))
            def _():
                self.copy(origin, way).start()

    def sent(self, origin):
        for way in range(2):

            @pl.when(self.wanted(origin, way))
            def _():
                self.copy(origin, way).wait_send()


def layer_kernel(slots, *refs):
    (
        tok, aw, attn_gain, moe_gain, routes, gates, eg, eu, ed, o_ref,
        xall, xn, wbuf, w3, acc, qkv, att, psend, precv, pown, xsend, xrecv, res, sm, pick, mix, xs, ssq,
        fs, ms, hid, gbuf, ubuf, dbuf, csend, crecv, keep, osend, orecv, zsend, zrecv, share,
        own_sems, w_z, w_y, x_zs, x_zr, x_x, x_c, s_sems, a_zs, a_zr, p_c, p_x, r_zs, r_zr, r_x, r_c,
        g_sems, u_sems, d_sems, o_c, o_x, o_z, f_sems,
    ) = refs
    f32, bf16 = jnp.float32, jnp.bfloat16
    n_seq, n_grp = lax.axis_size("seq"), lax.axis_size("grp")
    grp, seq, head = lax.axis_index("grp"), lax.axis_index("seq"), lax.axis_index("head")
    core, col = lax.rem(head, 2), head // 2
    other_x, other_c = {"head": flip(head, 2)}, {"head": flip(head, 1)}
    other_y = {"grp": lax.rem(grp + 1, n_grp)}
    local, width = tok.shape
    total = n_seq * local
    depth, columns = aw.shape[1:]
    own = columns // n_seq
    part = depth // n_grp
    quarter = local // 4
    amount, ring = ed.shape[0], gbuf.shape[0]
    span = width // 4
    near = [nearest(i, seq, n_seq) for i in range(n_seq)]

    left = []

    def go(copy):
        left.append(copy.wait_send)
        copy.start()

    barrier = pltpu.get_barrier_semaphore()
    friends = [{"seq": lax.rem(seq + k, n_seq)} for k in range(1, n_seq)] + [other_x, other_c]
    if n_grp > 1:
        friends.append(other_y)
    for friend in friends:
        pl.semaphore_signal(barrier, inc=1, device_id=friend, device_id_type=MESH)

    own_copies = [
        pltpu.make_async_copy(
            aw.at[which, :, aligned(seq, own)],
            wbuf.at[seq, :, pl.ds(which * own, own)],
            own_sems.at[which],
        )
        for which in range(3)
    ] + [pltpu.make_async_copy(aw.at[3], w3, own_sems.at[3])]
    for copy in own_copies:
        copy.start()
    xall[aligned(seq, local), :] = tok[...]
    top = routes.shape[0]
    sm[0:top, aligned(seq, local)] = routes[...].astype(f32)
    sm[top:, aligned(seq, local)] = gates[...]
    pl.semaphore_wait(barrier, len(friends))

    def token_rows(p, owner, n):
        start = p * local + owner * quarter + n * (quarter // XCUT)
        return xall.at[pl.ds(pl.multiple_of(start, quarter // XCUT), quarter // XCUT), :]

    tokens_z = [
        Chain(lambda p, n=n: token_rows(p, head, n), x_zs.at[n], x_zr.at[n], left)
        for n in range(XCUT)
    ]
    for chain in tokens_z:
        chain.forward(seq)

    def table_copy(to, origin):
        ref = sm.at[:, aligned(origin, local)]
        return remote(ref, ref, s_sems.at[0, to], s_sems.at[1, origin], {"seq": to})

    twice = 3 * depth // 8 if n_grp > 1 else 0
    once = (depth - twice) // n_grp
    batches = [(w, k * (part // 2), part // 2, part) for w in range(2) for k in range(2)]
    batches.append((2, 0, once, once))
    if twice:
        batches.append((2, depth - twice, twice, 0))
    passed_on = [n for n, batch in enumerate(batches) if batch[3] and n_grp > 1]

    def w_rows(side, n):
        _, start, size, stride = batches[n]
        return pl.ds(pl.multiple_of(side * stride + start, 16), size)

    def w_cols(n):
        return pl.ds(batches[n][0] * own, own)

    def w_copy(n, to):
        return remote(
            aw.at[batches[n][0], w_rows(grp, n), aligned(to, own)],
            wbuf.at[seq, w_rows(grp, n), w_cols(n)],
            w_z.at[0, n, to], w_z.at[1, n, seq], {"seq": to},
        )

    def w_arrival(n, origin):
        ref = wbuf.at[origin, w_rows(grp, n), w_cols(n)]
        return remote(ref, ref, w_z.at[0, n, origin], w_z.at[1, n, origin], {"seq": origin})

    def w_over(n, origin, side):
        ref = wbuf.at[origin, w_rows(side, n), w_cols(n)]
        return remote(ref, ref, w_y.at[0, n, origin], w_y.at[1, n, origin], other_y)

    def send_w(n):
        for p in reversed(near[1:]):
            go(w_copy(n, p))

    for p in near[1:]:
        go(table_copy(p, seq))

    def fetch(e, slot):
        return [
            pltpu.make_async_copy(eg.at[e], gbuf.at[slot], g_sems.at[slot]),
            pltpu.make_async_copy(eu.at[e], ubuf.at[slot], u_sems.at[slot]),
        ]

    def fetch_down(e):
        return pltpu.make_async_copy(ed.at[e], dbuf.at[e], d_sems.at[e])

    def begin(e, carry):
        for copy in fetch(e, e):
            copy.start()
        return carry

    def begin_down(e, carry):
        fetch_down(e).start()
        return carry

    lax.fori_loop(0, ring, begin, 0)
    lax.fori_loop(0, amount, begin_down, 0)

    def norm_rows(p):
        def step(j, carry):
            rows = pl.ds(pl.multiple_of(p * local + j * quarter, quarter), quarter)
            value = xall[rows, :].astype(f32)
            factor = lax.rsqrt(jnp.mean(value * value, axis=-1, keepdims=True) + 1e-06)
            xn[rows, :] = (value * factor * attn_gain[...]).astype(bf16)
            return carry

        lax.fori_loop(0, 4, step, 0)

    norm_rows(seq)

    def across(p, n):
        ref = token_rows(p, head, n)
        return remote(ref, ref, x_x.at[0, n, p], x_x.at[1, n, p], other_x)

    def beside(p, which, n):
        ref = token_rows(p, flip(head, 2) if which else head, n)
        return remote(ref, ref, x_c.at[0, which, n, p], x_c.at[1, which, n, p], other_c)

    def tables():
        for p in near[1:]:
            table_copy(p, p).wait_recv()
        ids = lax.broadcasted_iota(jnp.int32, (128, total), 0).astype(f32)
        ids = ids + (seq * amount).astype(f32)
        named = jnp.zeros((128, total), f32)
        weight = jnp.zeros((128, total), f32)
        for k in range(top):
            hit = sm[k : k + 1, :] == ids
            named = jnp.where(hit, 1.0, named)
            weight = jnp.where(hit, sm[top + k : top + k + 1, :], weight)
        before = lax.broadcasted_iota(jnp.int32, (total, total), 0) < lax.broadcasted_iota(
            jnp.int32, (total, total), 1
        )
        rank = dot(named.astype(bf16), jnp.where(before, 1.0, 0.0).astype(bf16))
        place = jnp.where(named > 0.0, rank, -1.0)
        spot = lax.broadcasted_iota(jnp.int32, (slots, total), 0).astype(f32)
        for e in range(amount):
            pick[e * slots : (e + 1) * slots, :] = jnp.where(
                place[e : e + 1, :] == spot, 1.0, 0.0
            ).astype(bf16)
        wide = lax.broadcasted_iota(jnp.int32, (128, amount * slots), 1).astype(f32)
        owner = jnp.floor((wide + 0.5) * (1.0 / slots))
        mine = lax.broadcasted_iota(jnp.int32, (128, amount * slots), 0).astype(f32)
        spread = jnp.where(owner == mine, 1.0, 0.0).astype(bf16)
        spot_of = (wide - owner * slots)[:1, :]
        place_t = jnp.transpose(place).astype(bf16)
        weight_t = jnp.transpose(weight).astype(bf16)
        for b in range(0, total, 128):
            mix[b : b + 128, :] = jnp.where(
                dot(place_t[b : b + 128], spread) == spot_of, dot(weight_t[b : b + 128], spread), 0.0
            ).astype(bf16)

    for event in SCHEDULE:
        kind, at = event[0], int(event[1:] or 0)
        if kind == "s":
            if at < len(batches):
                send_w(at)
        elif kind == "w":
            if at < len(batches):
                for p in near[1:]:
                    w_arrival(at, p).wait_recv()
                    if at in passed_on:
                        go(w_over(at, p, grp))
        elif kind == "t":
            tables()
        elif kind == "n":
            if at < n_seq:
                for n in range(XCUT):
                    beside(near[at], 0, n).wait_recv()
                    beside(near[at], 1, n).wait_recv()
                norm_rows(near[at])
        elif at < n_seq:
            for n in range(XCUT):
                if kind == "x":
                    tokens_z[n].arrive(near[at])
                    tokens_z[n].forward(near[at])
                    go(across(near[at], n))
                    go(beside(near[at], 0, n))
                else:
                    across(near[at], n).wait_recv()
                    go(beside(near[at], 1, n))

    for copy in own_copies:
        copy.wait()
    acc[...] = dot(xn[:, aligned(seq, depth)], wbuf[seq])
    for i in range(1, n_seq):
        p = near[i]
        for n in passed_on:
            w_over(n, p, lax.rem(grp + 1, n_grp)).wait_recv()
        acc[...] += dot(xn[:, aligned(p, depth)], wbuf[p])
    qkv[...] = acc[...].astype(bf16)

    cut = total // CUTS
    attended = [
        Chain(
            lambda p, n=n: att.at[pl.ds(n * cut, cut), aligned(p, own)],
            a_zs.at[n], a_zr.at[n], left,
        )
        for n in range(CUTS)
    ]
    for n in range(CUTS):
        seen = (n + 1) * cut
        lower = (
            lax.broadcasted_iota(jnp.int32, (cut, seen), 0) + n * cut
            >= lax.broadcasted_iota(jnp.int32, (cut, seen), 1)
        )
        for a in range(own // HEAD_DIM):
            at = a * HEAD_DIM
            query = qkv[n * cut : seen, at : at + HEAD_DIM]
            key = qkv[0:seen, own + at : own + at + HEAD_DIM]
            value = qkv[0:seen, 2 * own + at : 2 * own + at + HEAD_DIM]
            scores = jnp.where(lower, dot_nt(query, key), 0.0).astype(bf16)
            result = head_norm(dot(scores, value)).astype(bf16)
            place_at = pl.ds(pl.multiple_of(seq * own + at, HEAD_DIM), HEAD_DIM)
            att[n * cut : seen, place_at] = result
        attended[n].forward(seq)

    block = cut // 2

    def block_rows(n, side):
        return pl.ds(pl.multiple_of(n * cut + side * block, block), block)

    def part_copy(n):
        return remote(psend.at[n], precv.at[n], p_c.at[0, n], p_c.at[1, n], other_c)

    def owned(n):
        if n >= SPLIT:
            return block_rows(n, core)
        return split_rows(n, core, col)

    def split_rows(n, side, across):
        start = n * cut + side * block + across * (block // 2)
        return pl.ds(pl.multiple_of(start, block // 2), block // 2)

    def part_rows(n, across):
        if n >= SPLIT:
            return pl.ds(0, block)
        return pl.ds(pl.multiple_of(across * (block // 2), block // 2), block // 2)

    def sum_copy(n):
        rows = part_rows(n, 1 - col)
        return remote(
            xsend.at[n, rows], xrecv.at[n, rows], p_x.at[0, n], p_x.at[1, n], other_x
        )

    residual = [
        Chain(
            lambda p, n=n: res.at[owned(n), aligned(p, depth)], r_zs.at[n], r_zr.at[n], left
        )
        for n in range(CUTS)
    ]

    def res_across(p, n):
        ref = res.at[owned(n), aligned(p, depth)]
        return remote(ref, ref, r_x.at[0, n, p], r_x.at[1, n, p], other_x)

    def res_over(p, n, side, which):
        if n >= SPLIT:
            rows = block_rows(n, side)
        else:
            rows = split_rows(n, side, 1 - col if which else col)
        ref = res.at[rows, aligned(p, depth)]
        return remote(ref, ref, r_c.at[0, which, n, p], r_c.at[1, which, n, p], other_c)

    def pass_on(p, n):
        residual[n].forward(p)
        if n < SPLIT:
            go(res_across(p, n))
        go(res_over(p, n, core, 0))

    def project(n):
        psend[n] = dot_nt(att[block_rows(n, 1 - core), :], w3[...]).astype(bf16)
        go(part_copy(n))
        pown[n] = dot_nt(att[block_rows(n, core), :], w3[...])

    def join(n):
        part_copy(n).wait_recv()
        xsend[n] = (pown[n] + precv[n].astype(f32)).astype(bf16)
        go(sum_copy(n))

    def settle(n):
        sum_copy(n).wait_recv()
        rows, cols, at = owned(n), aligned(seq, depth), part_rows(n, col)
        summed = xsend[n, at, :].astype(f32) + xrecv[n, at, :].astype(f32)
        res[rows, cols] = (xall[rows, cols].astype(f32) + summed).astype(bf16)
        pass_on(seq, n)

    for i in range(1, n_seq):
        for n in range(CUTS):
            attended[n].arrive(near[i])
            attended[n].forward(near[i])
            if i == n_seq - 1:
                project(n)
                if n > 0:
                    join(n - 1)
    join(CUTS - 1)
    for n in range(CUTS):
        settle(n)

    def gather(p):
        for n in range(SPLIT):
            res_across(p, n).wait_recv()
            go(res_over(p, n, core, 1))
        for n in range(CUTS):
            res_over(p, n, 1 - core, 0).wait_recv()
            if n < SPLIT:
                res_over(p, n, 1 - core, 1).wait_recv()
        cols = aligned(p, depth)

        def scale(j, carry):
            rows = pl.ds(pl.multiple_of(j * 64, 64), 64)
            value = res[rows, cols].astype(f32)
            square = value * value
            add = square[:, 0:128]
            for k in range(128, depth, 128):
                add += square[:, k : k + 128]
            ssq[rows, :] += add
            ms[rows, :] = (value * moe_gain[:, cols]).astype(bf16)
            return carry

        lax.fori_loop(0, total // 64, scale, 0)
        for k in range(0, depth, 256):
            xs[:, pl.ds(pl.multiple_of(p * depth + k, 256), 256)] = dot(
                pick[...], ms[:, k : k + 256]
            ).astype(bf16)

    ssq[...] = jnp.zeros_like(ssq)
    for i in range(1, n_seq + 1):
        if i < n_seq:
            for n in range(CUTS):
                residual[n].arrive(near[i])
                pass_on(near[i], n)
        gather(near[i - 1])
    factor = lax.rsqrt(jnp.sum(ssq[...], axis=-1, keepdims=True) * (1.0 / width) + 1e-06)
    high = factor.astype(bf16).astype(f32)
    middle = (factor - high).astype(bf16).astype(f32)
    lane = lax.broadcasted_iota(jnp.int32, (total, 128), 1)
    terms = jnp.where(
        lane == 0, high, jnp.where(lane == 1, middle, jnp.where(lane == 2, factor - high - middle, 0.0))
    )
    per_slot = jnp.sum(dot(pick[...], terms.astype(bf16)), axis=-1, keepdims=True)
    fs[...] = jnp.broadcast_to(per_slot, fs.shape)

    def inner(e):
        slot = lax.rem(e, ring)
        for copy in fetch(e, slot):
            copy.wait()
        rows = pl.ds(pl.multiple_of(e * slots, slots), slots)
        x = xs[rows, :]
        scale = fs[rows, 0:1]
        gate_val = dot(x, gbuf[slot]) * scale
        up_val = dot(x, ubuf[slot]) * scale
        hid[rows, :] = (gate_val * jax.nn.sigmoid(gate_val) * up_val).astype(bf16)

        @pl.when(e + ring < amount)
        def _():
            for copy in fetch(e + ring, slot):
                copy.start()

    def inner_pair(j, carry):
        inner(2 * j)
        inner(2 * j + 1)
        return carry

    lax.fori_loop(0, amount // 2, inner_pair, 0)

    def wait_down(e, carry):
        fetch_down(e).wait()
        return carry

    lax.fori_loop(0, amount, wait_down, 0)

    def down(side):
        cols = aligned(side, 2 * span)

        def step(j, carry):
            for e in (2 * j, 2 * j + 1):
                rows = pl.ds(pl.multiple_of(e * slots, slots), slots)
                xs[rows, cols] = dot(hid[rows, :], dbuf[e, :, cols]).astype(bf16)
            return carry

        lax.fori_loop(0, amount // 2, step, 0)

    def pair_copy(u, p):
        return remote(csend.at[u, p], crecv.at[u, p], o_c.at[0, u, p], o_c.at[1, u, p], other_c)

    def over_copy(p):
        return remote(osend.at[p], orecv.at[p], o_x.at[0, p], o_x.at[1, p], other_x)

    def back_copy(to, origin):
        return remote(
            zsend.at[to], zrecv.at[origin], o_z.at[0, to], o_z.at[1, origin], {"seq": to}
        )

    def share_out(u, side, p):
        rows = aligned(p, local)
        cols = pl.ds(pl.multiple_of(side * 2 * span + (1 - core) * span, span), span)
        csend[u, p] = dot(mix[rows, :], xs[:, cols]).astype(bf16)
        go(pair_copy(u, p))
        cols = pl.ds(pl.multiple_of(side * 2 * span + core * span, span), span)
        keep[p] = dot(mix[rows, :], xs[:, cols])

    order = near[::-1]

    def hand_over(p):
        pair_copy(0, p).wait_recv()
        osend[p] = (keep[p] + crecv[0, p].astype(f32)).astype(bf16)
        go(over_copy(p))

    down(1 - col)
    for n in range(n_seq + 1):
        if n < n_seq:
            share_out(0, 1 - col, order[n])
        if n > 0:
            hand_over(order[n - 1])

    def add_up(p):
        pair_copy(1, p).wait_recv()
        over_copy(p).wait_recv()
        return keep[p] + crecv[1, p].astype(f32) + orecv[p].astype(f32)

    down(col)
    for p in order:
        share_out(1, col, p)
    for p in order[:-1]:
        zsend[p] = add_up(p).astype(bf16)
        go(back_copy(p, seq))
    mine_cols = aligned(head, span)
    summed = add_up(seq) + res[aligned(seq, local), mine_cols].astype(f32)
    for p in order[:-1]:
        back_copy(p, p).wait_recv()
        summed = summed + zrecv[p].astype(f32)
    share[...] = summed.astype(bf16)

    def final_copy(owner, n, k, target):
        rows = pl.ds(n * (local // 2), local // 2)
        ref = o_ref.at[rows, aligned(owner, span)]
        source = share.at[rows] if k < 2 else ref
        return remote(source, ref, f_sems.at[0, n, k], f_sems.at[1, n, k], target)

    for k, target in enumerate((other_x, other_c)):
        for n in range(2):
            go(final_copy(head, n, k, target))
    o_ref[:, mine_cols] = share[...]
    for n in range(2):
        final_copy(head, n, 0, other_x).wait_recv()
        go(final_copy(flip(head, 2), n, 2, other_c))
    for n in range(2):
        for k in (1, 2):
            final_copy(head, n, k, other_c).wait_recv()

    for wait in left:
        wait()


def layer(
    tokens, attn_weight, attn_gain, moe_gain, routes, gates, expert_gate, expert_up, expert_down
):
    local, width = tokens.shape
    n_seq = lax.axis_size("seq")
    total = n_seq * local
    depth, columns = attn_weight.shape[1:]
    own = columns // n_seq
    amount, _, inner = expert_gate.shape
    slots = -(-CAP * n_seq // 16) * 16
    span = width // 4
    ring = min(8, amount)
    bf16, f32 = jnp.bfloat16, jnp.float32
    vmem, sem = pltpu.VMEM, pltpu.SemaphoreType.DMA
    block = total // CUTS // 2
    here, away = pl.BlockSpec(memory_space=pltpu.VMEM), pl.BlockSpec(memory_space=pl.ANY)
    return pl.pallas_call(
        functools.partial(layer_kernel, slots),
        out_shape=jax.ShapeDtypeStruct(tokens.shape, tokens.dtype),
        in_specs=[here, away, here, here, here, here, away, away, away],
        out_specs=here,
        scratch_shapes=[
            vmem((total, width), bf16),
            vmem((total, width), bf16),
            vmem((n_seq, depth, 3 * own), bf16),
            vmem((depth, columns), bf16),
            vmem((total, 3 * own), f32),
            vmem((total, 3 * own), bf16),
            vmem((total, columns), bf16),
            vmem((CUTS, block, depth), bf16),
            vmem((CUTS, block, depth), bf16),
            vmem((CUTS, block, depth), f32),
            vmem((CUTS, block, depth), bf16),
            vmem((CUTS, block, depth), bf16),
            vmem((total, width), bf16),
            vmem((2 * routes.shape[1], total), f32),
            vmem((amount * slots, total), bf16),
            vmem((total, amount * slots), bf16),
            vmem((amount * slots, width), bf16),
            vmem((total, 128), f32),
            vmem((amount * slots, 128), f32),
            vmem((total, depth), bf16),
            vmem((amount * slots, inner), bf16),
            vmem((ring, width, inner), bf16),
            vmem((ring, width, inner), bf16),
            vmem((amount, inner, width), bf16),
            vmem((2, n_seq, local, span), bf16),
            vmem((2, n_seq, local, span), bf16),
            vmem((n_seq, local, span), f32),
            vmem((n_seq, local, span), bf16),
            vmem((n_seq, local, span), bf16),
            vmem((n_seq, local, span), bf16),
            vmem((n_seq, local, span), bf16),
            vmem((local, span), bf16),
            sem((4,)),
            sem((2, 6, n_seq)),
            sem((2, 6, n_seq)),
            sem((XCUT, 2, n_seq)),
            sem((XCUT, n_seq)),
            sem((2, XCUT, n_seq)),
            sem((2, 2, XCUT, n_seq)),
            sem((2, n_seq)),
            sem((CUTS, 2, n_seq)),
            sem((CUTS, n_seq)),
            sem((2, CUTS)),
            sem((2, CUTS)),
            sem((CUTS, 2, n_seq)),
            sem((CUTS, n_seq)),
            sem((2, CUTS, n_seq)),
            sem((2, 2, CUTS, n_seq)),
            sem((ring,)),
            sem((ring,)),
            sem((amount,)),
            sem((2, 2, n_seq)),
            sem((2, n_seq)),
            sem((2, n_seq)),
            sem((2, 2, 3)),
        ],
        compiler_params=pltpu.CompilerParams(
            collective_id=2, has_side_effects=True, vmem_limit_bytes=VMEM_LIMIT
        ),
    )(
        tokens, attn_weight, attn_gain[None], moe_gain[None], routes.T, gates.T,
        expert_gate, expert_up, expert_down,
    )


def fits(mesh, tokens, attn_weight, expert_gate):
    n_seq, local = mesh.shape["seq"], tokens.shape[0]
    own = attn_weight.shape[2] // n_seq
    return (
        mesh.shape["head"] == 4
        and mesh.shape["grp"] <= 2
        and n_seq > 1
        and own % HEAD_DIM == 0
        and attn_weight.shape[2] % n_seq == 0
        and local % 128 == 0
        and attn_weight.shape[1] % 256 == 0
        and n_seq * local <= 512
        and expert_gate.shape[0] <= 16
        and expert_gate.shape[0] % 2 == 0
    )


def solution(mesh):
    def run(tokens, attn_weight, attn_gain, moe_gain, routes, gates, *experts):
        whole = layer if fits(mesh, tokens, attn_weight, experts[0]) else body
        return whole(tokens, attn_weight, attn_gain, moe_gain, routes, gates, *experts)

    return jax.shard_map(
        run,
        mesh=mesh,
        in_specs=(
            P(("grp", "seq"), None),
            P(None, "seq", "head"),
            P(),
            P(),
            P(("grp", "seq"), None),
            P(("grp", "seq"), None),
            P("seq", None, "head"),
            P("seq", None, "head"),
            P("seq", "head", None),
        ),
        out_specs=P(("grp", "seq"), None),
        check_vma=False,
    )
```

```python
import functools

import jax
import jax.numpy as jnp
from jax import lax
from jax.experimental import pallas as pl
from jax.experimental.pallas import tpu as pltpu
from jax.sharding import PartitionSpec as P

HEAD_DIM = 128
EXPERTS = 64
TOPK = 8
CAP = 18
MESH = pl.DeviceIdType.MESH
VMEM_LIMIT = 63 * 1024 * 1024
XCUT = 2
SCHEDULE = [
    "s0", "x1", "x2", "s1", "x3", "s2", "w0", "s3", "a1", "w1", "s4", "a2",
    "w2", "s5", "a3", "w3", "n1", "n2", "n3", "w4", "t", "w5",
]
SPLIT = 4
CUTS = 4


PRECISE = lax.Precision.HIGHEST


def prefix_2(array, axis, combine, identity):
    peers, position = (lax.axis_size(axis), lax.axis_index(axis))
    everything = lax.all_gather(array.astype(jnp.bfloat16), axis)
    start = jnp.broadcast_to(jnp.asarray(identity, array.dtype), array.shape)

    def hop(k, before):
        reached = k < position
        new = combine(before, everything[k].astype(array.dtype))
        return jnp.where(reached, new, before)

    return lax.fori_loop(0, peers, hop, start)


def rms_scale(row_block, gain_vec):
    widened = row_block.astype(jnp.float32)
    factor = lax.rsqrt(jnp.mean(widened * widened, axis=-1, keepdims=True) + 1e-06)
    return widened * factor * gain_vec


def head_norm(outputs):
    return outputs * lax.rsqrt(jnp.mean(outputs * outputs, axis=-1, keepdims=True) + 1e-06)


def add_states(earlier, later):
    return earlier + later


def slot_numbers(route_flat):
    one_hot = (route_flat[:, None] == jnp.arange(EXPERTS, dtype=jnp.int32)[None, :]).astype(
        jnp.int32
    )
    earlier = jnp.cumsum(one_hot, axis=0) - one_hot
    return route_flat * CAP + jnp.sum(earlier * one_hot, axis=1)


def make_runner(expert_gate, expert_up, expert_down):

    def run_experts(received):
        gate_val = jnp.einsum(
            "necd,edf->necf", received, expert_gate, preferred_element_type=jnp.float32
        )
        up_val = jnp.einsum(
            "necd,edf->necf", received, expert_up, preferred_element_type=jnp.float32
        )
        hidden = (jax.nn.silu(gate_val) * up_val).astype(jnp.bfloat16)
        partial_value = jnp.einsum(
            "necf,efd->necd", hidden, expert_down, preferred_element_type=jnp.float32
        ).astype(jnp.bfloat16)
        groups = lax.axis_size("head")
        shape_now = partial_value.shape
        split = partial_value.reshape(
            shape_now[0], shape_now[1], shape_now[2], groups, shape_now[3] // groups
        )
        by_group = lax.all_to_all(split, "head", split_axis=3, concat_axis=3, tiled=True)
        summed = jnp.sum(by_group.astype(jnp.float32), axis=3)
        return lax.all_to_all(
            summed.astype(jnp.bfloat16), "seq", split_axis=0, concat_axis=0, tiled=True
        ).astype(summed.dtype)

    return run_experts


def body(
    tokens, attn_weight, attn_gain, moe_gain, routes, gates, expert_gate, expert_up, expert_down
):
    local_rows = tokens.shape[0]
    normed = rms_scale(tokens, attn_gain).astype(jnp.bfloat16)
    weights = lax.all_gather(attn_weight, "seq", axis=1, tiled=True)
    head_count = weights.shape[2] // HEAD_DIM
    projected = [
        jnp.dot(normed, weights[which], preferred_element_type=jnp.float32)
        .astype(jnp.bfloat16)
        .reshape(local_rows, head_count, HEAD_DIM)
        for which in range(3)
    ]
    query_rows, key_rows, value_rows = projected
    own_state = jnp.einsum("thd,the->hde", key_rows, value_rows, preferred_element_type=jnp.float32)
    prefix = prefix_2(own_state, "seq", add_states, jnp.zeros_like(own_state))
    inter_part = jnp.einsum(
        "thd,hde->the", query_rows.astype(jnp.float32), prefix, precision=PRECISE
    )
    scores = jnp.einsum("thd,shd->hts", query_rows, key_rows, preferred_element_type=jnp.float32)
    lower_mask = jnp.arange(local_rows)[:, None] >= jnp.arange(local_rows)[None, :]
    scores = jnp.where(lower_mask[None], scores, 0.0)
    intra_part = jnp.einsum(
        "hts,she->the", scores, value_rows.astype(jnp.float32), precision=PRECISE
    )
    attended = (
        head_norm(inter_part + intra_part)
        .reshape(local_rows, head_count * HEAD_DIM)
        .astype(jnp.bfloat16)
    )
    out_part = lax.dot_general(
        attended, weights[3], (((1,), (1,)), ((), ())), preferred_element_type=jnp.float32
    )
    residual = (
        tokens.astype(jnp.float32)
        + lax.psum(out_part.astype(jnp.bfloat16), "head").astype(jnp.float32)
    ).astype(jnp.bfloat16)
    moe_in = rms_scale(residual, moe_gain).astype(jnp.bfloat16)
    route_flat = routes.reshape(-1)
    slots = slot_numbers(route_flat)
    owners = lax.axis_size("seq")
    local_experts = expert_gate.shape[0]
    source_row = jnp.arange(route_flat.shape[0], dtype=jnp.int32) // TOPK
    run_experts = make_runner(expert_gate, expert_up, expert_down)
    outbound = (
        jnp.zeros((EXPERTS * CAP, moe_in.shape[1]), jnp.bfloat16).at[slots].set(moe_in[source_row])
    )
    outbound = outbound.reshape(owners, local_experts, CAP, moe_in.shape[1])
    returned = run_experts(lax.all_to_all(outbound, "seq", split_axis=0, concat_axis=0, tiled=True))
    arrived = returned.reshape(EXPERTS * CAP, -1)[slots].reshape(local_rows, TOPK, -1)
    moe_partial = jnp.einsum("tkd,tk->td", arrived, gates, precision=PRECISE)
    column_span = moe_partial.shape[1]
    residual_share = lax.dynamic_slice_in_dim(
        residual, lax.axis_index("head") * column_span, column_span, 1
    )
    mixed_share = (residual_share.astype(jnp.float32) + moe_partial).astype(jnp.bfloat16)
    return lax.all_gather(mixed_share, "head", axis=1, tiled=True)


def flip(index, bit):
    return index + bit * (1 - 2 * lax.rem(index // bit, 2))


def remote(source, dest, send_sem, recv_sem, target):
    return pltpu.make_async_remote_copy(
        src_ref=source,
        dst_ref=dest,
        send_sem=send_sem,
        recv_sem=recv_sem,
        device_id=target,
        device_id_type=MESH,
    )


def aligned(index, size):
    return pl.ds(pl.multiple_of(index * size, size), size)


def dot(a, b):
    return jnp.dot(a, b, preferred_element_type=jnp.float32)


def dot_nt(a, b):
    return lax.dot_general(a, b, (((1,), (1,)), ((), ())), preferred_element_type=jnp.float32)


def nearest(i, me, peers):
    both = jnp.minimum(me, peers - 1 - me)
    step = (i + 1) // 2
    side = -1 if i % 2 else 1
    rest = jnp.where(me <= peers - 1 - me, i - both, both - i)
    return me + jnp.where(i <= 2 * both, side * step, rest)


class Chain:
    def __init__(self, piece, sends, recvs, left):
        self.piece, self.sends, self.recvs, self.left = piece, sends, recvs, left
        self.peers, self.me = lax.axis_size("seq"), lax.axis_index("seq")

    def copy(self, origin, way):
        ref = self.piece(origin)
        to = lax.rem(self.me + (self.peers - 1 if way else 1), self.peers)
        return remote(ref, ref, self.sends.at[way, origin], self.recvs.at[origin], {"seq": to})

    def wanted(self, origin, way):
        if way:
            return (origin >= self.me) & (self.me > 0)
        return (origin <= self.me) & (self.me < self.peers - 1)

    def arrive(self, origin):
        self.copy(origin, 0).wait_recv()

    def forward(self, origin):
        self.left.append(lambda: self.sent(origin))
        for way in range(2):

            @pl.when(self.wanted(origin, way))
            def _():
                self.copy(origin, way).start()

    def sent(self, origin):
        for way in range(2):

            @pl.when(self.wanted(origin, way))
            def _():
                self.copy(origin, way).wait_send()


def layer_kernel(slots, *refs):
    (
        tok, aw, attn_gain, moe_gain, routes, gates, eg, eu, ed, o_ref,
        xall, xn, wbuf, w3, acc, qkv, att, psend, precv, pown, xsend, xrecv, res, sm, pick, mix, xs, ys, both, ssq,
        fs, ms, hid, wide, dbuf, csend, crecv, keep, osend, orecv, zsend, zrecv, share,
        own_sems, w_z, w_y, x_zs, x_zr, x_x, x_c, s_sems, a_zs, a_zr, p_c, p_x, r_zs, r_zr, r_x, r_c,
        g_sems, u_sems, d_sems, o_c, o_x, o_z, f_sems,
    ) = refs
    f32, bf16 = jnp.float32, jnp.bfloat16
    n_seq, n_grp = lax.axis_size("seq"), lax.axis_size("grp")
    grp, seq, head = lax.axis_index("grp"), lax.axis_index("seq"), lax.axis_index("head")
    core, col = lax.rem(head, 2), head // 2
    other_x, other_c = {"head": flip(head, 2)}, {"head": flip(head, 1)}
    other_y = {"grp": lax.rem(grp + 1, n_grp)}
    local, width = tok.shape
    total = n_seq * local
    depth, columns = aw.shape[1:]
    own = columns // n_seq
    part = depth // n_grp
    quarter = local // 4
    amount, inner = ed.shape[:2]
    span = width // 4
    near = [nearest(i, seq, n_seq) for i in range(n_seq)]

    left = []

    def go(copy):
        left.append(copy.wait_send)
        copy.start()

    barrier = pltpu.get_barrier_semaphore()
    friends = [{"seq": lax.rem(seq + k, n_seq)} for k in range(1, n_seq)] + [other_x, other_c]
    if n_grp > 1:
        friends.append(other_y)
    for friend in friends:
        pl.semaphore_signal(barrier, inc=1, device_id=friend, device_id_type=MESH)

    own_copies = [
        pltpu.make_async_copy(
            aw.at[which, :, aligned(seq, own)],
            wbuf.at[seq, :, pl.ds(which * own, own)],
            own_sems.at[which],
        )
        for which in range(3)
    ] + [pltpu.make_async_copy(aw.at[3], w3, own_sems.at[3])]
    for copy in own_copies:
        copy.start()
    xall[aligned(seq, local), :] = tok[...]
    top = routes.shape[0]
    sm[0:top, aligned(seq, local)] = routes[...].astype(f32)
    sm[top:, aligned(seq, local)] = gates[...]
    pl.semaphore_wait(barrier, len(friends))

    def token_rows(p, owner, n):
        start = p * local + owner * quarter + n * (quarter // XCUT)
        return xall.at[pl.ds(pl.multiple_of(start, quarter // XCUT), quarter // XCUT), :]

    tokens_z = [
        Chain(lambda p, n=n: token_rows(p, head, n), x_zs.at[n], x_zr.at[n], left)
        for n in range(XCUT)
    ]
    for chain in tokens_z:
        chain.forward(seq)

    def table_copy(to, origin):
        ref = sm.at[:, aligned(origin, local)]
        return remote(ref, ref, s_sems.at[0, to], s_sems.at[1, origin], {"seq": to})

    twice = 3 * depth // 8 if n_grp > 1 else 0
    once = (depth - twice) // n_grp
    batches = [(w, k * (part // 2), part // 2, part) for w in range(2) for k in range(2)]
    batches.append((2, 0, once, once))
    if twice:
        batches.append((2, depth - twice, twice, 0))
    passed_on = [n for n, batch in enumerate(batches) if batch[3] and n_grp > 1]

    def w_rows(side, n):
        _, start, size, stride = batches[n]
        return pl.ds(pl.multiple_of(side * stride + start, 16), size)

    def w_cols(n):
        return pl.ds(batches[n][0] * own, own)

    def w_copy(n, to):
        return remote(
            aw.at[batches[n][0], w_rows(grp, n), aligned(to, own)],
            wbuf.at[seq, w_rows(grp, n), w_cols(n)],
            w_z.at[0, n, to], w_z.at[1, n, seq], {"seq": to},
        )

    def w_arrival(n, origin):
        ref = wbuf.at[origin, w_rows(grp, n), w_cols(n)]
        return remote(ref, ref, w_z.at[0, n, origin], w_z.at[1, n, origin], {"seq": origin})

    def w_over(n, origin, side):
        ref = wbuf.at[origin, w_rows(side, n), w_cols(n)]
        return remote(ref, ref, w_y.at[0, n, origin], w_y.at[1, n, origin], other_y)

    def send_w(n):
        for p in reversed(near[1:]):
            go(w_copy(n, p))

    for p in near[1:]:
        go(table_copy(p, seq))

    def fetch(i):
        rows, place = aligned(near[i], depth), i % 2
        return [
            pltpu.make_async_copy(
                eg.at[:, rows], wide.at[place, :, :, pl.ds(0, inner)], g_sems.at[place]
            ),
            pltpu.make_async_copy(
                eu.at[:, rows], wide.at[place, :, :, pl.ds(inner, inner)], u_sems.at[place]
            ),
        ]

    fetch_down = pltpu.make_async_copy(ed, dbuf, d_sems.at[0])
    for i in range(2):
        for copy in fetch(i):
            copy.start()
    fetch_down.start()
    both[...] = jnp.zeros_like(both)

    def norm_rows(p):
        def step(j, carry):
            rows = pl.ds(pl.multiple_of(p * local + j * quarter, quarter), quarter)
            value = xall[rows, :].astype(f32)
            factor = lax.rsqrt(jnp.mean(value * value, axis=-1, keepdims=True) + 1e-06)
            xn[rows, :] = (value * factor * attn_gain[...]).astype(bf16)
            return carry

        lax.fori_loop(0, 4, step, 0)

    norm_rows(seq)

    def across(p, n):
        ref = token_rows(p, head, n)
        return remote(ref, ref, x_x.at[0, n, p], x_x.at[1, n, p], other_x)

    def beside(p, which, n):
        ref = token_rows(p, flip(head, 2) if which else head, n)
        return remote(ref, ref, x_c.at[0, which, n, p], x_c.at[1, which, n, p], other_c)

    def tables():
        for p in near[1:]:
            table_copy(p, p).wait_recv()
        ids = lax.broadcasted_iota(jnp.int32, (128, total), 0).astype(f32)
        ids = ids + (seq * amount).astype(f32)
        named = jnp.zeros((128, total), f32)
        weight = jnp.zeros((128, total), f32)
        for k in range(top):
            hit = sm[k : k + 1, :] == ids
            named = jnp.where(hit, 1.0, named)
            weight = jnp.where(hit, sm[top + k : top + k + 1, :], weight)
        before = lax.broadcasted_iota(jnp.int32, (total, total), 0) < lax.broadcasted_iota(
            jnp.int32, (total, total), 1
        )
        rank = dot(named.astype(bf16), jnp.where(before, 1.0, 0.0).astype(bf16))
        place = jnp.where(named > 0.0, rank, -1.0)
        spot = lax.broadcasted_iota(jnp.int32, (slots, total), 0).astype(f32)
        for e in range(amount):
            pick[e * slots : (e + 1) * slots, :] = jnp.where(
                place[e : e + 1, :] == spot, 1.0, 0.0
            ).astype(bf16)
        lanes = lax.broadcasted_iota(jnp.int32, (128, amount * slots), 1).astype(f32)
        owner = jnp.floor((lanes + 0.5) * (1.0 / slots))
        mine = lax.broadcasted_iota(jnp.int32, (128, amount * slots), 0).astype(f32)
        spread = jnp.where(owner == mine, 1.0, 0.0).astype(bf16)
        spot_of = (lanes - owner * slots)[:1, :]
        place_t = jnp.transpose(place).astype(bf16)
        weight_t = jnp.transpose(weight).astype(bf16)
        for b in range(0, total, 128):
            mix[b : b + 128, :] = jnp.where(
                dot(place_t[b : b + 128], spread) == spot_of, dot(weight_t[b : b + 128], spread), 0.0
            ).astype(bf16)

    for event in SCHEDULE:
        kind, at = event[0], int(event[1:] or 0)
        if kind == "s":
            if at < len(batches):
                send_w(at)
        elif kind == "w":
            if at < len(batches):
                for p in near[1:]:
                    w_arrival(at, p).wait_recv()
                    if at in passed_on:
                        go(w_over(at, p, grp))
        elif kind == "t":
            tables()
        elif kind == "n":
            if at < n_seq:
                for n in range(XCUT):
                    beside(near[at], 0, n).wait_recv()
                    beside(near[at], 1, n).wait_recv()
                norm_rows(near[at])
        elif at < n_seq:
            for n in range(XCUT):
                if kind == "x":
                    tokens_z[n].arrive(near[at])
                    tokens_z[n].forward(near[at])
                    go(across(near[at], n))
                    go(beside(near[at], 0, n))
                else:
                    across(near[at], n).wait_recv()
                    go(beside(near[at], 1, n))

    for copy in own_copies:
        copy.wait()
    acc[...] = dot(xn[:, aligned(seq, depth)], wbuf[seq])
    for i in range(1, n_seq):
        p = near[i]
        for n in passed_on:
            w_over(n, p, lax.rem(grp + 1, n_grp)).wait_recv()
        acc[...] += dot(xn[:, aligned(p, depth)], wbuf[p])
    qkv[...] = acc[...].astype(bf16)

    cut = total // CUTS
    attended = [
        Chain(
            lambda p, n=n: att.at[pl.ds(n * cut, cut), aligned(p, own)],
            a_zs.at[n], a_zr.at[n], left,
        )
        for n in range(CUTS)
    ]
    for n in range(CUTS):
        seen = (n + 1) * cut
        lower = (
            lax.broadcasted_iota(jnp.int32, (cut, seen), 0) + n * cut
            >= lax.broadcasted_iota(jnp.int32, (cut, seen), 1)
        )
        for a in range(own // HEAD_DIM):
            at = a * HEAD_DIM
            query = qkv[n * cut : seen, at : at + HEAD_DIM]
            key = qkv[0:seen, own + at : own + at + HEAD_DIM]
            value = qkv[0:seen, 2 * own + at : 2 * own + at + HEAD_DIM]
            scores = jnp.where(lower, dot_nt(query, key), 0.0).astype(bf16)
            result = head_norm(dot(scores, value)).astype(bf16)
            place_at = pl.ds(pl.multiple_of(seq * own + at, HEAD_DIM), HEAD_DIM)
            att[n * cut : seen, place_at] = result
        attended[n].forward(seq)

    block = cut // 2

    def block_rows(n, side):
        return pl.ds(pl.multiple_of(n * cut + side * block, block), block)

    def part_copy(n):
        return remote(psend.at[n], precv.at[n], p_c.at[0, n], p_c.at[1, n], other_c)

    def owned(n):
        if n >= SPLIT:
            return block_rows(n, core)
        return split_rows(n, core, col)

    def split_rows(n, side, across):
        start = n * cut + side * block + across * (block // 2)
        return pl.ds(pl.multiple_of(start, block // 2), block // 2)

    def part_rows(n, across):
        if n >= SPLIT:
            return pl.ds(0, block)
        return pl.ds(pl.multiple_of(across * (block // 2), block // 2), block // 2)

    def sum_copy(n):
        rows = part_rows(n, 1 - col)
        return remote(
            xsend.at[n, rows], xrecv.at[n, rows], p_x.at[0, n], p_x.at[1, n], other_x
        )

    residual = [
        Chain(
            lambda p, n=n: res.at[owned(n), aligned(p, depth)], r_zs.at[n], r_zr.at[n], left
        )
        for n in range(CUTS)
    ]

    def res_across(p, n):
        ref = res.at[owned(n), aligned(p, depth)]
        return remote(ref, ref, r_x.at[0, n, p], r_x.at[1, n, p], other_x)

    def res_over(p, n, side, which):
        if n >= SPLIT:
            rows = block_rows(n, side)
        else:
            rows = split_rows(n, side, 1 - col if which else col)
        ref = res.at[rows, aligned(p, depth)]
        return remote(ref, ref, r_c.at[0, which, n, p], r_c.at[1, which, n, p], other_c)

    def pass_on(p, n):
        residual[n].forward(p)
        if n < SPLIT:
            go(res_across(p, n))
        go(res_over(p, n, core, 0))

    def project(n):
        psend[n] = dot_nt(att[block_rows(n, 1 - core), :], w3[...]).astype(bf16)
        go(part_copy(n))
        pown[n] = dot_nt(att[block_rows(n, core), :], w3[...])

    def join(n):
        part_copy(n).wait_recv()
        xsend[n] = (pown[n] + precv[n].astype(f32)).astype(bf16)
        go(sum_copy(n))

    def settle(n):
        sum_copy(n).wait_recv()
        rows, cols, at = owned(n), aligned(seq, depth), part_rows(n, col)
        summed = xsend[n, at, :].astype(f32) + xrecv[n, at, :].astype(f32)
        res[rows, cols] = (xall[rows, cols].astype(f32) + summed).astype(bf16)
        pass_on(seq, n)

    for i in range(1, n_seq):
        for n in range(CUTS):
            attended[n].arrive(near[i])
            attended[n].forward(near[i])
            if i == n_seq - 1:
                project(n)
                if n > 0:
                    join(n - 1)
    join(CUTS - 1)
    for n in range(CUTS):
        settle(n)

    def gather(p):
        for n in range(SPLIT):
            res_across(p, n).wait_recv()
            go(res_over(p, n, core, 1))
        for n in range(CUTS):
            res_over(p, n, 1 - core, 0).wait_recv()
            if n < SPLIT:
                res_over(p, n, 1 - core, 1).wait_recv()
        cols = aligned(p, depth)

        def scale(j, carry):
            rows = pl.ds(pl.multiple_of(j * 64, 64), 64)
            value = res[rows, cols].astype(f32)
            square = value * value
            add = square[:, 0:128]
            for k in range(128, depth, 128):
                add += square[:, k : k + 128]
            ssq[rows, :] += add
            ms[rows, :] = (value * moe_gain[:, cols]).astype(bf16)
            return carry

        lax.fori_loop(0, total // 64, scale, 0)
        for k in range(0, depth, 256):
            xs[:, k : k + 256] = dot(pick[...], ms[:, k : k + 256]).astype(bf16)

    def products(i):
        for copy in fetch(i):
            copy.wait()

        def step(j, carry):
            for e in range(4):
                e = 4 * j + e
                rows = pl.ds(pl.multiple_of(e * slots, slots), slots)
                both[rows, :] += dot(xs[rows, :], wide[i % 2, e])
            return carry

        lax.fori_loop(0, amount // 4, step, 0)
        if i + 2 < n_seq:
            for copy in fetch(i + 2):
                copy.start()

    ssq[...] = jnp.zeros_like(ssq)
    def reach_res(i):
        for n in range(CUTS):
            residual[n].arrive(near[i])
            pass_on(near[i], n)

    for i in range(1, n_seq + 1):
        if i < n_seq:
            reach_res(i)
        if i > 1:
            gather(near[i - 2])
            products(i - 2)
    gather(near[n_seq - 1])
    products(n_seq - 1)
    factor = lax.rsqrt(jnp.sum(ssq[...], axis=-1, keepdims=True) * (1.0 / width) + 1e-06)
    high = factor.astype(bf16).astype(f32)
    middle = (factor - high).astype(bf16).astype(f32)
    lane = lax.broadcasted_iota(jnp.int32, (total, 128), 1)
    terms = jnp.where(
        lane == 0, high, jnp.where(lane == 1, middle, jnp.where(lane == 2, factor - high - middle, 0.0))
    )
    per_slot = jnp.sum(dot(pick[...], terms.astype(bf16)), axis=-1, keepdims=True)
    fs[...] = jnp.broadcast_to(per_slot, fs.shape)

    def activate(e, carry):
        rows = pl.ds(pl.multiple_of(e * slots, slots), slots)
        scale = fs[rows, 0:1]
        gate_val = both[rows, 0:inner] * scale
        up_val = both[rows, inner : 2 * inner] * scale
        hid[rows, :] = (gate_val * jax.nn.sigmoid(gate_val) * up_val).astype(bf16)
        return carry

    lax.fori_loop(0, amount, activate, 0)

    fetch_down.wait()

    def down(side):
        cols = aligned(side, 2 * span)

        def step(j, carry):
            for e in range(4):
                e = 4 * j + e
                rows = pl.ds(pl.multiple_of(e * slots, slots), slots)
                ys[rows, :] = dot(hid[rows, :], dbuf[e, :, cols]).astype(bf16)
            return carry

        lax.fori_loop(0, amount // 4, step, 0)

    def pair_copy(u, p):
        return remote(csend.at[u, p], crecv.at[u, p], o_c.at[0, u, p], o_c.at[1, u, p], other_c)

    def over_copy(p):
        return remote(osend.at[p], orecv.at[p], o_x.at[0, p], o_x.at[1, p], other_x)

    def back_copy(to, origin):
        return remote(
            zsend.at[to], zrecv.at[origin], o_z.at[0, to], o_z.at[1, origin], {"seq": to}
        )

    def share_out(u, p):
        rows = aligned(p, local)
        csend[u, p] = dot(mix[rows, :], ys[:, aligned(1 - core, span)]).astype(bf16)
        go(pair_copy(u, p))
        keep[p] = dot(mix[rows, :], ys[:, aligned(core, span)])

    order = near[::-1]

    def hand_over(p):
        pair_copy(0, p).wait_recv()
        osend[p] = (keep[p] + crecv[0, p].astype(f32)).astype(bf16)
        go(over_copy(p))

    down(1 - col)
    for n in range(n_seq + 1):
        if n < n_seq:
            share_out(0, order[n])
        if n > 0:
            hand_over(order[n - 1])

    def add_up(p):
        pair_copy(1, p).wait_recv()
        over_copy(p).wait_recv()
        return keep[p] + crecv[1, p].astype(f32) + orecv[p].astype(f32)

    down(col)
    for p in order:
        share_out(1, p)
    for p in order[:-1]:
        zsend[p] = add_up(p).astype(bf16)
        go(back_copy(p, seq))
    mine_cols = aligned(head, span)
    summed = add_up(seq) + res[aligned(seq, local), mine_cols].astype(f32)
    for p in order[:-1]:
        back_copy(p, p).wait_recv()
        summed = summed + zrecv[p].astype(f32)
    share[...] = summed.astype(bf16)

    def final_copy(owner, n, k, target):
        rows = pl.ds(n * (local // 2), local // 2)
        ref = o_ref.at[rows, aligned(owner, span)]
        source = share.at[rows] if k < 2 else ref
        return remote(source, ref, f_sems.at[0, n, k], f_sems.at[1, n, k], target)

    for k, target in enumerate((other_x, other_c)):
        for n in range(2):
            go(final_copy(head, n, k, target))
    o_ref[:, mine_cols] = share[...]
    for n in range(2):
        final_copy(head, n, 0, other_x).wait_recv()
        go(final_copy(flip(head, 2), n, 2, other_c))
    for n in range(2):
        for k in (1, 2):
            final_copy(head, n, k, other_c).wait_recv()

    for wait in left:
        wait()


def layer(
    tokens, attn_weight, attn_gain, moe_gain, routes, gates, expert_gate, expert_up, expert_down
):
    local, width = tokens.shape
    n_seq = lax.axis_size("seq")
    total = n_seq * local
    depth, columns = attn_weight.shape[1:]
    own = columns // n_seq
    amount, _, inner = expert_gate.shape
    slots = -(-CAP * n_seq // 16) * 16
    span = width // 4
    bf16, f32 = jnp.bfloat16, jnp.float32
    vmem, sem = pltpu.VMEM, pltpu.SemaphoreType.DMA
    block = total // CUTS // 2
    here, away = pl.BlockSpec(memory_space=pltpu.VMEM), pl.BlockSpec(memory_space=pl.ANY)
    return pl.pallas_call(
        functools.partial(layer_kernel, slots),
        out_shape=jax.ShapeDtypeStruct(tokens.shape, tokens.dtype),
        in_specs=[here, away, here, here, here, here, away, away, away],
        out_specs=here,
        scratch_shapes=[
            vmem((total, width), bf16),
            vmem((total, width), bf16),
            vmem((n_seq, depth, 3 * own), bf16),
            vmem((depth, columns), bf16),
            vmem((total, 3 * own), f32),
            vmem((total, 3 * own), bf16),
            vmem((total, columns), bf16),
            vmem((CUTS, block, depth), bf16),
            vmem((CUTS, block, depth), bf16),
            vmem((CUTS, block, depth), f32),
            vmem((CUTS, block, depth), bf16),
            vmem((CUTS, block, depth), bf16),
            vmem((total, width), bf16),
            vmem((2 * routes.shape[1], total), f32),
            vmem((amount * slots, total), bf16),
            vmem((total, amount * slots), bf16),
            vmem((amount * slots, depth), bf16),
            vmem((amount * slots, 2 * span), bf16),
            vmem((amount * slots, 2 * inner), f32),
            vmem((total, 128), f32),
            vmem((amount * slots, 128), f32),
            vmem((total, depth), bf16),
            vmem((amount * slots, inner), bf16),
            vmem((2, amount, depth, 2 * inner), bf16),
            vmem((amount, inner, width), bf16),
            vmem((2, n_seq, local, span), bf16),
            vmem((2, n_seq, local, span), bf16),
            vmem((n_seq, local, span), f32),
            vmem((n_seq, local, span), bf16),
            vmem((n_seq, local, span), bf16),
            vmem((n_seq, local, span), bf16),
            vmem((n_seq, local, span), bf16),
            vmem((local, span), bf16),
            sem((4,)),
            sem((2, 6, n_seq)),
            sem((2, 6, n_seq)),
            sem((XCUT, 2, n_seq)),
            sem((XCUT, n_seq)),
            sem((2, XCUT, n_seq)),
            sem((2, 2, XCUT, n_seq)),
            sem((2, n_seq)),
            sem((CUTS, 2, n_seq)),
            sem((CUTS, n_seq)),
            sem((2, CUTS)),
            sem((2, CUTS)),
            sem((CUTS, 2, n_seq)),
            sem((CUTS, n_seq)),
            sem((2, CUTS, n_seq)),
            sem((2, 2, CUTS, n_seq)),
            sem((2,)),
            sem((2,)),
            sem((1,)),
            sem((2, 2, n_seq)),
            sem((2, n_seq)),
            sem((2, n_seq)),
            sem((2, 2, 3)),
        ],
        compiler_params=pltpu.CompilerParams(
            collective_id=2, has_side_effects=True, vmem_limit_bytes=VMEM_LIMIT
        ),
    )(
        tokens, attn_weight, attn_gain[None], moe_gain[None], routes.T, gates.T,
        expert_gate, expert_up, expert_down,
    )


def fits(mesh, tokens, attn_weight, expert_gate):
    n_seq, local = mesh.shape["seq"], tokens.shape[0]
    own = attn_weight.shape[2] // n_seq
    return (
        mesh.shape["head"] == 4
        and mesh.shape["grp"] <= 2
        and n_seq > 1
        and own % HEAD_DIM == 0
        and attn_weight.shape[2] % n_seq == 0
        and local % 128 == 0
        and attn_weight.shape[1] % 256 == 0
        and n_seq * local <= 512
        and expert_gate.shape[0] <= 16
        and expert_gate.shape[0] % 4 == 0
    )


def solution(mesh):
    def run(tokens, attn_weight, attn_gain, moe_gain, routes, gates, *experts):
        whole = layer if fits(mesh, tokens, attn_weight, experts[0]) else body
        return whole(tokens, attn_weight, attn_gain, moe_gain, routes, gates, *experts)

    return jax.shard_map(
        run,
        mesh=mesh,
        in_specs=(
            P(("grp", "seq"), None),
            P(None, "seq", "head"),
            P(),
            P(),
            P(("grp", "seq"), None),
            P(("grp", "seq"), None),
            P("seq", None, "head"),
            P("seq", None, "head"),
            P("seq", "head", None),
        ),
        out_specs=P(("grp", "seq"), None),
        check_vma=False,
    )
```

```python
import functools

import jax
import jax.numpy as jnp
from jax import lax
from jax.experimental import pallas as pl
from jax.experimental.pallas import tpu as pltpu
from jax.sharding import PartitionSpec as P

HEAD_DIM = 128
EXPERTS = 64
TOPK = 8
CAP = 18
MESH = pl.DeviceIdType.MESH
VMEM_LIMIT = 63 * 1024 * 1024
XCUT = 2
SCHEDULE = [
    "s0", "x1", "x2", "s1", "x3", "s2", "w0", "s3", "a1", "w1", "s4", "a2",
    "w2", "s5", "a3", "w3", "n1", "n2", "n3", "w4", "t", "w5",
]
SPLIT = 4
CUTS = 4


PRECISE = lax.Precision.HIGHEST


def prefix_2(array, axis, combine, identity):
    peers, position = (lax.axis_size(axis), lax.axis_index(axis))
    everything = lax.all_gather(array.astype(jnp.bfloat16), axis)
    start = jnp.broadcast_to(jnp.asarray(identity, array.dtype), array.shape)

    def hop(k, before):
        reached = k < position
        new = combine(before, everything[k].astype(array.dtype))
        return jnp.where(reached, new, before)

    return lax.fori_loop(0, peers, hop, start)


def rms_scale(row_block, gain_vec):
    widened = row_block.astype(jnp.float32)
    factor = lax.rsqrt(jnp.mean(widened * widened, axis=-1, keepdims=True) + 1e-06)
    return widened * factor * gain_vec


def head_norm(outputs):
    return outputs * lax.rsqrt(jnp.mean(outputs * outputs, axis=-1, keepdims=True) + 1e-06)


def add_states(earlier, later):
    return earlier + later


def slot_numbers(route_flat):
    one_hot = (route_flat[:, None] == jnp.arange(EXPERTS, dtype=jnp.int32)[None, :]).astype(
        jnp.int32
    )
    earlier = jnp.cumsum(one_hot, axis=0) - one_hot
    return route_flat * CAP + jnp.sum(earlier * one_hot, axis=1)


def make_runner(expert_gate, expert_up, expert_down):

    def run_experts(received):
        gate_val = jnp.einsum(
            "necd,edf->necf", received, expert_gate, preferred_element_type=jnp.float32
        )
        up_val = jnp.einsum(
            "necd,edf->necf", received, expert_up, preferred_element_type=jnp.float32
        )
        hidden = (jax.nn.silu(gate_val) * up_val).astype(jnp.bfloat16)
        partial_value = jnp.einsum(
            "necf,efd->necd", hidden, expert_down, preferred_element_type=jnp.float32
        ).astype(jnp.bfloat16)
        groups = lax.axis_size("head")
        shape_now = partial_value.shape
        split = partial_value.reshape(
            shape_now[0], shape_now[1], shape_now[2], groups, shape_now[3] // groups
        )
        by_group = lax.all_to_all(split, "head", split_axis=3, concat_axis=3, tiled=True)
        summed = jnp.sum(by_group.astype(jnp.float32), axis=3)
        return lax.all_to_all(
            summed.astype(jnp.bfloat16), "seq", split_axis=0, concat_axis=0, tiled=True
        ).astype(summed.dtype)

    return run_experts


def body(
    tokens, attn_weight, attn_gain, moe_gain, routes, gates, expert_gate, expert_up, expert_down
):
    local_rows = tokens.shape[0]
    normed = rms_scale(tokens, attn_gain).astype(jnp.bfloat16)
    weights = lax.all_gather(attn_weight, "seq", axis=1, tiled=True)
    head_count = weights.shape[2] // HEAD_DIM
    projected = [
        jnp.dot(normed, weights[which], preferred_element_type=jnp.float32)
        .astype(jnp.bfloat16)
        .reshape(local_rows, head_count, HEAD_DIM)
        for which in range(3)
    ]
    query_rows, key_rows, value_rows = projected
    own_state = jnp.einsum("thd,the->hde", key_rows, value_rows, preferred_element_type=jnp.float32)
    prefix = prefix_2(own_state, "seq", add_states, jnp.zeros_like(own_state))
    inter_part = jnp.einsum(
        "thd,hde->the", query_rows.astype(jnp.float32), prefix, precision=PRECISE
    )
    scores = jnp.einsum("thd,shd->hts", query_rows, key_rows, preferred_element_type=jnp.float32)
    lower_mask = jnp.arange(local_rows)[:, None] >= jnp.arange(local_rows)[None, :]
    scores = jnp.where(lower_mask[None], scores, 0.0)
    intra_part = jnp.einsum(
        "hts,she->the", scores, value_rows.astype(jnp.float32), precision=PRECISE
    )
    attended = (
        head_norm(inter_part + intra_part)
        .reshape(local_rows, head_count * HEAD_DIM)
        .astype(jnp.bfloat16)
    )
    out_part = lax.dot_general(
        attended, weights[3], (((1,), (1,)), ((), ())), preferred_element_type=jnp.float32
    )
    residual = (
        tokens.astype(jnp.float32)
        + lax.psum(out_part.astype(jnp.bfloat16), "head").astype(jnp.float32)
    ).astype(jnp.bfloat16)
    moe_in = rms_scale(residual, moe_gain).astype(jnp.bfloat16)
    route_flat = routes.reshape(-1)
    slots = slot_numbers(route_flat)
    owners = lax.axis_size("seq")
    local_experts = expert_gate.shape[0]
    source_row = jnp.arange(route_flat.shape[0], dtype=jnp.int32) // TOPK
    run_experts = make_runner(expert_gate, expert_up, expert_down)
    outbound = (
        jnp.zeros((EXPERTS * CAP, moe_in.shape[1]), jnp.bfloat16).at[slots].set(moe_in[source_row])
    )
    outbound = outbound.reshape(owners, local_experts, CAP, moe_in.shape[1])
    returned = run_experts(lax.all_to_all(outbound, "seq", split_axis=0, concat_axis=0, tiled=True))
    arrived = returned.reshape(EXPERTS * CAP, -1)[slots].reshape(local_rows, TOPK, -1)
    moe_partial = jnp.einsum("tkd,tk->td", arrived, gates, precision=PRECISE)
    column_span = moe_partial.shape[1]
    residual_share = lax.dynamic_slice_in_dim(
        residual, lax.axis_index("head") * column_span, column_span, 1
    )
    mixed_share = (residual_share.astype(jnp.float32) + moe_partial).astype(jnp.bfloat16)
    return lax.all_gather(mixed_share, "head", axis=1, tiled=True)


def flip(index, bit):
    return index + bit * (1 - 2 * lax.rem(index // bit, 2))


def remote(source, dest, send_sem, recv_sem, target):
    return pltpu.make_async_remote_copy(
        src_ref=source,
        dst_ref=dest,
        send_sem=send_sem,
        recv_sem=recv_sem,
        device_id=target,
        device_id_type=MESH,
    )


def aligned(index, size):
    return pl.ds(pl.multiple_of(index * size, size), size)


def dot(a, b):
    return jnp.dot(a, b, preferred_element_type=jnp.float32)


def dot_nt(a, b):
    return lax.dot_general(a, b, (((1,), (1,)), ((), ())), preferred_element_type=jnp.float32)


def nearest(i, me, peers):
    both = jnp.minimum(me, peers - 1 - me)
    step = (i + 1) // 2
    side = -1 if i % 2 else 1
    rest = jnp.where(me <= peers - 1 - me, i - both, both - i)
    return me + jnp.where(i <= 2 * both, side * step, rest)


class Chain:
    def __init__(self, piece, sends, recvs, left):
        self.piece, self.sends, self.recvs, self.left = piece, sends, recvs, left
        self.peers, self.me = lax.axis_size("seq"), lax.axis_index("seq")

    def copy(self, origin, way):
        ref = self.piece(origin)
        to = lax.rem(self.me + (self.peers - 1 if way else 1), self.peers)
        return remote(ref, ref, self.sends.at[way, origin], self.recvs.at[origin], {"seq": to})

    def wanted(self, origin, way):
        if way:
            return (origin >= self.me) & (self.me > 0)
        return (origin <= self.me) & (self.me < self.peers - 1)

    def arrive(self, origin):
        self.copy(origin, 0).wait_recv()

    def forward(self, origin):
        self.left.append(lambda: self.sent(origin))
        for way in range(2):

            @pl.when(self.wanted(origin, way))
            def _():
                self.copy(origin, way).start()

    def sent(self, origin):
        for way in range(2):

            @pl.when(self.wanted(origin, way))
            def _():
                self.copy(origin, way).wait_send()


def layer_kernel(slots, *refs):
    (
        tok, aw, attn_gain, moe_gain, routes, gates, eg, eu, ed, o_ref,
        xall, xn, wbuf, w3, acc, qkv, att, psend, precv, pown, xsend, xrecv, res, sm, pick, mix, xs, ys, both, ssq,
        fs, ms, hid, wide, dbuf, csend, crecv, keep, osend, orecv, zsend, zrecv, share,
        own_sems, w_z, w_y, x_zs, x_zr, x_x, x_c, s_sems, a_zs, a_zr, p_c, p_x, r_zs, r_zr, r_x, r_c,
        g_sems, u_sems, d_sems, o_c, o_x, o_z, f_sems,
    ) = refs
    f32, bf16 = jnp.float32, jnp.bfloat16
    n_seq, n_grp = lax.axis_size("seq"), lax.axis_size("grp")
    grp, seq, head = lax.axis_index("grp"), lax.axis_index("seq"), lax.axis_index("head")
    core, col = lax.rem(head, 2), head // 2
    other_x, other_c = {"head": flip(head, 2)}, {"head": flip(head, 1)}
    other_y = {"grp": lax.rem(grp + 1, n_grp)}
    local, width = tok.shape
    total = n_seq * local
    depth, columns = aw.shape[1:]
    own = columns // n_seq
    part = depth // n_grp
    quarter = local // 4
    amount, inner = ed.shape[:2]
    span = width // 4
    near = [nearest(i, seq, n_seq) for i in range(n_seq)]

    left = []

    def go(copy):
        left.append(copy.wait_send)
        copy.start()

    barrier = pltpu.get_barrier_semaphore()
    friends = [{"seq": lax.rem(seq + k, n_seq)} for k in range(1, n_seq)] + [other_x, other_c]
    if n_grp > 1:
        friends.append(other_y)
    for friend in friends:
        pl.semaphore_signal(barrier, inc=1, device_id=friend, device_id_type=MESH)

    own_copies = [
        pltpu.make_async_copy(
            aw.at[which, :, aligned(seq, own)],
            wbuf.at[seq, :, pl.ds(which * own, own)],
            own_sems.at[which],
        )
        for which in range(3)
    ] + [pltpu.make_async_copy(aw.at[3], w3, own_sems.at[3])]
    for copy in own_copies:
        copy.start()
    xall[aligned(seq, local), :] = tok[...]
    top = routes.shape[0]
    sm[0:top, aligned(seq, local)] = routes[...].astype(f32)
    sm[top:, aligned(seq, local)] = gates[...]
    pl.semaphore_wait(barrier, len(friends))

    def token_rows(p, owner, n):
        start = p * local + owner * quarter + n * (quarter // XCUT)
        return xall.at[pl.ds(pl.multiple_of(start, quarter // XCUT), quarter // XCUT), :]

    tokens_z = [
        Chain(lambda p, n=n: token_rows(p, head, n), x_zs.at[n], x_zr.at[n], left)
        for n in range(XCUT)
    ]
    for chain in tokens_z:
        chain.forward(seq)

    def table_copy(to, origin):
        ref = sm.at[:, aligned(origin, local)]
        return remote(ref, ref, s_sems.at[0, to], s_sems.at[1, origin], {"seq": to})

    twice = 3 * depth // 8 if n_grp > 1 else 0
    once = (depth - twice) // n_grp
    batches = [(w, k * (part // 2), part // 2, part) for w in range(2) for k in range(2)]
    batches.append((2, 0, once, once))
    if twice:
        batches.append((2, depth - twice, twice, 0))
    passed_on = [n for n, batch in enumerate(batches) if batch[3] and n_grp > 1]

    def w_rows(side, n):
        _, start, size, stride = batches[n]
        return pl.ds(pl.multiple_of(side * stride + start, 16), size)

    def w_cols(n):
        return pl.ds(batches[n][0] * own, own)

    def w_copy(n, to):
        return remote(
            aw.at[batches[n][0], w_rows(grp, n), aligned(to, own)],
            wbuf.at[seq, w_rows(grp, n), w_cols(n)],
            w_z.at[0, n, to], w_z.at[1, n, seq], {"seq": to},
        )

    def w_arrival(n, origin):
        ref = wbuf.at[origin, w_rows(grp, n), w_cols(n)]
        return remote(ref, ref, w_z.at[0, n, origin], w_z.at[1, n, origin], {"seq": origin})

    def w_over(n, origin, side):
        ref = wbuf.at[origin, w_rows(side, n), w_cols(n)]
        return remote(ref, ref, w_y.at[0, n, origin], w_y.at[1, n, origin], other_y)

    def send_w(n):
        for p in reversed(near[1:]):
            go(w_copy(n, p))

    for p in near[1:]:
        go(table_copy(p, seq))

    def fetch(i):
        rows, place = aligned(near[i], depth), i % 2
        return [
            pltpu.make_async_copy(
                eg.at[:, rows], wide.at[place, :, :, pl.ds(0, inner)], g_sems.at[place]
            ),
            pltpu.make_async_copy(
                eu.at[:, rows], wide.at[place, :, :, pl.ds(inner, inner)], u_sems.at[place]
            ),
        ]

    fetch_down = pltpu.make_async_copy(ed, dbuf, d_sems.at[0])
    for i in range(2):
        for copy in fetch(i):
            copy.start()
    fetch_down.start()

    def norm_rows(p):
        def step(j, carry):
            rows = pl.ds(pl.multiple_of(p * local + j * quarter, quarter), quarter)
            value = xall[rows, :].astype(f32)
            factor = lax.rsqrt(jnp.mean(value * value, axis=-1, keepdims=True) + 1e-06)
            xn[rows, :] = (value * factor * attn_gain[...]).astype(bf16)
            return carry

        lax.fori_loop(0, 4, step, 0)

    norm_rows(seq)

    def across(p, n):
        ref = token_rows(p, head, n)
        return remote(ref, ref, x_x.at[0, n, p], x_x.at[1, n, p], other_x)

    def beside(p, which, n):
        ref = token_rows(p, flip(head, 2) if which else head, n)
        return remote(ref, ref, x_c.at[0, which, n, p], x_c.at[1, which, n, p], other_c)

    def tables():
        for p in near[1:]:
            table_copy(p, p).wait_recv()
        ids = lax.broadcasted_iota(jnp.int32, (128, total), 0).astype(f32)
        ids = ids + (seq * amount).astype(f32)
        named = jnp.zeros((128, total), f32)
        weight = jnp.zeros((128, total), f32)
        for k in range(top):
            hit = sm[k : k + 1, :] == ids
            named = jnp.where(hit, 1.0, named)
            weight = jnp.where(hit, sm[top + k : top + k + 1, :], weight)
        before = lax.broadcasted_iota(jnp.int32, (total, total), 0) < lax.broadcasted_iota(
            jnp.int32, (total, total), 1
        )
        rank = dot(named.astype(bf16), jnp.where(before, 1.0, 0.0).astype(bf16))
        place = jnp.where(named > 0.0, rank, -1.0)
        spot = lax.broadcasted_iota(jnp.int32, (slots, total), 0).astype(f32)
        for e in range(amount):
            pick[e * slots : (e + 1) * slots, :] = jnp.where(
                place[e : e + 1, :] == spot, 1.0, 0.0
            ).astype(bf16)
        lanes = lax.broadcasted_iota(jnp.int32, (128, amount * slots), 1).astype(f32)
        owner = jnp.floor((lanes + 0.5) * (1.0 / slots))
        mine = lax.broadcasted_iota(jnp.int32, (128, amount * slots), 0).astype(f32)
        spread = jnp.where(owner == mine, 1.0, 0.0).astype(bf16)
        spot_of = (lanes - owner * slots)[:1, :]
        place_t = jnp.transpose(place).astype(bf16)
        weight_t = jnp.transpose(weight).astype(bf16)
        for b in range(0, total, 128):
            mix[b : b + 128, :] = jnp.where(
                dot(place_t[b : b + 128], spread) == spot_of, dot(weight_t[b : b + 128], spread), 0.0
            ).astype(bf16)

    for event in SCHEDULE:
        kind, at = event[0], int(event[1:] or 0)
        if kind == "s":
            if at < len(batches):
                send_w(at)
        elif kind == "w":
            if at < len(batches):
                for p in near[1:]:
                    w_arrival(at, p).wait_recv()
                    if at in passed_on:
                        go(w_over(at, p, grp))
        elif kind == "t":
            tables()
        elif kind == "n":
            if at < n_seq:
                for n in range(XCUT):
                    beside(near[at], 0, n).wait_recv()
                    beside(near[at], 1, n).wait_recv()
                norm_rows(near[at])
        elif at < n_seq:
            for n in range(XCUT):
                if kind == "x":
                    tokens_z[n].arrive(near[at])
                    tokens_z[n].forward(near[at])
                    go(across(near[at], n))
                    go(beside(near[at], 0, n))
                else:
                    across(near[at], n).wait_recv()
                    go(beside(near[at], 1, n))

    for copy in own_copies:
        copy.wait()
    acc[...] = dot(xn[:, aligned(seq, depth)], wbuf[seq])
    for i in range(1, n_seq):
        p = near[i]
        for n in passed_on:
            w_over(n, p, lax.rem(grp + 1, n_grp)).wait_recv()
        acc[...] += dot(xn[:, aligned(p, depth)], wbuf[p])
    qkv[...] = acc[...].astype(bf16)

    cut = total // CUTS
    attended = [
        Chain(
            lambda p, n=n: att.at[pl.ds(n * cut, cut), aligned(p, own)],
            a_zs.at[n], a_zr.at[n], left,
        )
        for n in range(CUTS)
    ]
    for n in range(CUTS):
        seen = (n + 1) * cut
        lower = (
            lax.broadcasted_iota(jnp.int32, (cut, seen), 0) + n * cut
            >= lax.broadcasted_iota(jnp.int32, (cut, seen), 1)
        )
        for a in range(own // HEAD_DIM):
            at = a * HEAD_DIM
            query = qkv[n * cut : seen, at : at + HEAD_DIM]
            key = qkv[0:seen, own + at : own + at + HEAD_DIM]
            value = qkv[0:seen, 2 * own + at : 2 * own + at + HEAD_DIM]
            scores = jnp.where(lower, dot_nt(query, key), 0.0).astype(bf16)
            result = head_norm(dot(scores, value)).astype(bf16)
            place_at = pl.ds(pl.multiple_of(seq * own + at, HEAD_DIM), HEAD_DIM)
            att[n * cut : seen, place_at] = result
        attended[n].forward(seq)

    block = cut // 2

    def block_rows(n, side):
        return pl.ds(pl.multiple_of(n * cut + side * block, block), block)

    def part_copy(n):
        return remote(psend.at[n], precv.at[n], p_c.at[0, n], p_c.at[1, n], other_c)

    def owned(n):
        if n >= SPLIT:
            return block_rows(n, core)
        return split_rows(n, core, col)

    def split_rows(n, side, across):
        start = n * cut + side * block + across * (block // 2)
        return pl.ds(pl.multiple_of(start, block // 2), block // 2)

    def part_rows(n, across):
        if n >= SPLIT:
            return pl.ds(0, block)
        return pl.ds(pl.multiple_of(across * (block // 2), block // 2), block // 2)

    def sum_copy(n):
        rows = part_rows(n, 1 - col)
        return remote(
            xsend.at[n, rows], xrecv.at[n, rows], p_x.at[0, n], p_x.at[1, n], other_x
        )

    residual = [
        Chain(
            lambda p, n=n: res.at[owned(n), aligned(p, depth)], r_zs.at[n], r_zr.at[n], left
        )
        for n in range(CUTS)
    ]

    def res_across(p, n):
        ref = res.at[owned(n), aligned(p, depth)]
        return remote(ref, ref, r_x.at[0, n, p], r_x.at[1, n, p], other_x)

    def res_over(p, n, side, which):
        if n >= SPLIT:
            rows = block_rows(n, side)
        else:
            rows = split_rows(n, side, 1 - col if which else col)
        ref = res.at[rows, aligned(p, depth)]
        return remote(ref, ref, r_c.at[0, which, n, p], r_c.at[1, which, n, p], other_c)

    def pass_on(p, n):
        residual[n].forward(p)
        if n < SPLIT:
            go(res_across(p, n))
        go(res_over(p, n, core, 0))

    def project(n):
        psend[n] = dot_nt(att[block_rows(n, 1 - core), :], w3[...]).astype(bf16)
        go(part_copy(n))
        pown[n] = dot_nt(att[block_rows(n, core), :], w3[...])

    def join(n):
        part_copy(n).wait_recv()
        xsend[n] = (pown[n] + precv[n].astype(f32)).astype(bf16)
        go(sum_copy(n))

    def settle(n):
        sum_copy(n).wait_recv()
        rows, cols, at = owned(n), aligned(seq, depth), part_rows(n, col)
        summed = xsend[n, at, :].astype(f32) + xrecv[n, at, :].astype(f32)
        res[rows, cols] = (xall[rows, cols].astype(f32) + summed).astype(bf16)
        pass_on(seq, n)

    for i in range(1, n_seq):
        for n in range(CUTS):
            attended[n].arrive(near[i])
            attended[n].forward(near[i])
            if i == n_seq - 1:
                project(n)
                if n > 0:
                    join(n - 1)
    join(CUTS - 1)
    for n in range(CUTS):
        settle(n)

    def gather(p):
        for n in range(SPLIT):
            res_across(p, n).wait_recv()
            go(res_over(p, n, core, 1))
        for n in range(CUTS):
            res_over(p, n, 1 - core, 0).wait_recv()
            if n < SPLIT:
                res_over(p, n, 1 - core, 1).wait_recv()
        cols = aligned(p, depth)

        def scale(j, carry):
            rows = pl.ds(pl.multiple_of(j * 64, 64), 64)
            value = res[rows, cols].astype(f32)
            square = value * value
            add = square[:, 0:128]
            for k in range(128, depth, 128):
                add += square[:, k : k + 128]
            ssq[rows, :] += add
            ms[rows, :] = (value * moe_gain[:, cols]).astype(bf16)
            return carry

        lax.fori_loop(0, total // 64, scale, 0)
        for k in range(0, depth, 256):
            xs[:, k : k + 256] = dot(pick[...], ms[:, k : k + 256]).astype(bf16)

    def products(i):
        for copy in fetch(i):
            copy.wait()

        def step(j, carry):
            for e in range(8):
                e = 8 * j + e
                rows = pl.ds(pl.multiple_of(e * slots, slots), slots)
                value = dot(xs[rows, :], wide[i % 2, e])
                both[rows, :] = value if i == 0 else both[rows, :] + value
            return carry

        lax.fori_loop(0, amount // 8, step, 0)
        if i + 2 < n_seq:
            for copy in fetch(i + 2):
                copy.start()

    ssq[...] = jnp.zeros_like(ssq)
    def reach_res(i):
        for n in range(CUTS):
            residual[n].arrive(near[i])
            pass_on(near[i], n)

    for i in range(1, n_seq + 1):
        if i < n_seq:
            reach_res(i)
        if i > 1:
            gather(near[i - 2])
            products(i - 2)
    gather(near[n_seq - 1])
    products(n_seq - 1)
    factor = lax.rsqrt(jnp.sum(ssq[...], axis=-1, keepdims=True) * (1.0 / width) + 1e-06)
    high = factor.astype(bf16).astype(f32)
    middle = (factor - high).astype(bf16).astype(f32)
    lane = lax.broadcasted_iota(jnp.int32, (total, 128), 1)
    terms = jnp.where(
        lane == 0, high, jnp.where(lane == 1, middle, jnp.where(lane == 2, factor - high - middle, 0.0))
    )
    per_slot = jnp.sum(dot(pick[...], terms.astype(bf16)), axis=-1, keepdims=True)
    fs[...] = jnp.broadcast_to(per_slot, fs.shape)

    def activate(j, carry):
        for e in range(4):
            e = 4 * j + e
            rows = pl.ds(pl.multiple_of(e * slots, slots), slots)
            scale = fs[rows, 0:1]
            gate_val = both[rows, 0:inner] * scale
            up_val = both[rows, inner : 2 * inner] * scale
            hid[rows, :] = (gate_val * jax.nn.sigmoid(gate_val) * up_val).astype(bf16)
        return carry

    lax.fori_loop(0, amount // 4, activate, 0)

    fetch_down.wait()

    def down(side):
        cols = aligned(side, 2 * span)

        def step(j, carry):
            for e in range(8):
                e = 8 * j + e
                rows = pl.ds(pl.multiple_of(e * slots, slots), slots)
                ys[rows, :] = dot(hid[rows, :], dbuf[e, :, cols]).astype(bf16)
            return carry

        lax.fori_loop(0, amount // 8, step, 0)

    def pair_copy(u, p):
        return remote(csend.at[u, p], crecv.at[u, p], o_c.at[0, u, p], o_c.at[1, u, p], other_c)

    def over_copy(p):
        return remote(osend.at[p], orecv.at[p], o_x.at[0, p], o_x.at[1, p], other_x)

    def back_copy(to, origin):
        return remote(
            zsend.at[to], zrecv.at[origin], o_z.at[0, to], o_z.at[1, origin], {"seq": to}
        )

    def share_out(u, p):
        rows = aligned(p, local)
        csend[u, p] = dot(mix[rows, :], ys[:, aligned(1 - core, span)]).astype(bf16)
        go(pair_copy(u, p))
        keep[p] = dot(mix[rows, :], ys[:, aligned(core, span)])

    order = near[::-1]

    def hand_over(p):
        pair_copy(0, p).wait_recv()
        osend[p] = (keep[p] + crecv[0, p].astype(f32)).astype(bf16)
        go(over_copy(p))

    down(1 - col)
    for n in range(n_seq + 1):
        if n < n_seq:
            share_out(0, order[n])
        if n > 0:
            hand_over(order[n - 1])

    def add_up(p):
        pair_copy(1, p).wait_recv()
        over_copy(p).wait_recv()
        return keep[p] + crecv[1, p].astype(f32) + orecv[p].astype(f32)

    down(col)
    for p in order:
        share_out(1, p)
    for p in order[:-1]:
        zsend[p] = add_up(p).astype(bf16)
        go(back_copy(p, seq))
    mine_cols = aligned(head, span)
    summed = add_up(seq) + res[aligned(seq, local), mine_cols].astype(f32)
    for p in order[:-1]:
        back_copy(p, p).wait_recv()
        summed = summed + zrecv[p].astype(f32)
    share[...] = summed.astype(bf16)

    def final_copy(owner, n, k, target):
        rows = pl.ds(n * (local // 2), local // 2)
        ref = o_ref.at[rows, aligned(owner, span)]
        source = share.at[rows] if k < 2 else ref
        return remote(source, ref, f_sems.at[0, n, k], f_sems.at[1, n, k], target)

    for k, target in enumerate((other_x, other_c)):
        for n in range(2):
            go(final_copy(head, n, k, target))
    o_ref[:, mine_cols] = share[...]
    for n in range(2):
        final_copy(head, n, 0, other_x).wait_recv()
        go(final_copy(flip(head, 2), n, 2, other_c))
    for n in range(2):
        for k in (1, 2):
            final_copy(head, n, k, other_c).wait_recv()

    for wait in left:
        wait()


def layer(
    tokens, attn_weight, attn_gain, moe_gain, routes, gates, expert_gate, expert_up, expert_down
):
    local, width = tokens.shape
    n_seq = lax.axis_size("seq")
    total = n_seq * local
    depth, columns = attn_weight.shape[1:]
    own = columns // n_seq
    amount, _, inner = expert_gate.shape
    slots = -(-CAP * n_seq // 16) * 16
    span = width // 4
    bf16, f32 = jnp.bfloat16, jnp.float32
    vmem, sem = pltpu.VMEM, pltpu.SemaphoreType.DMA
    block = total // CUTS // 2
    here, away = pl.BlockSpec(memory_space=pltpu.VMEM), pl.BlockSpec(memory_space=pl.ANY)
    return pl.pallas_call(
        functools.partial(layer_kernel, slots),
        out_shape=jax.ShapeDtypeStruct(tokens.shape, tokens.dtype),
        in_specs=[here, away, here, here, here, here, away, away, away],
        out_specs=here,
        scratch_shapes=[
            vmem((total, width), bf16),
            vmem((total, width), bf16),
            vmem((n_seq, depth, 3 * own), bf16),
            vmem((depth, columns), bf16),
            vmem((total, 3 * own), f32),
            vmem((total, 3 * own), bf16),
            vmem((total, columns), bf16),
            vmem((CUTS, block, depth), bf16),
            vmem((CUTS, block, depth), bf16),
            vmem((CUTS, block, depth), f32),
            vmem((CUTS, block, depth), bf16),
            vmem((CUTS, block, depth), bf16),
            vmem((total, width), bf16),
            vmem((2 * routes.shape[1], total), f32),
            vmem((amount * slots, total), bf16),
            vmem((total, amount * slots), bf16),
            vmem((amount * slots, depth), bf16),
            vmem((amount * slots, 2 * span), bf16),
            vmem((amount * slots, 2 * inner), f32),
            vmem((total, 128), f32),
            vmem((amount * slots, 128), f32),
            vmem((total, depth), bf16),
            vmem((amount * slots, inner), bf16),
            vmem((2, amount, depth, 2 * inner), bf16),
            vmem((amount, inner, width), bf16),
            vmem((2, n_seq, local, span), bf16),
            vmem((2, n_seq, local, span), bf16),
            vmem((n_seq, local, span), f32),
            vmem((n_seq, local, span), bf16),
            vmem((n_seq, local, span), bf16),
            vmem((n_seq, local, span), bf16),
            vmem((n_seq, local, span), bf16),
            vmem((local, span), bf16),
            sem((4,)),
            sem((2, 6, n_seq)),
            sem((2, 6, n_seq)),
            sem((XCUT, 2, n_seq)),
            sem((XCUT, n_seq)),
            sem((2, XCUT, n_seq)),
            sem((2, 2, XCUT, n_seq)),
            sem((2, n_seq)),
            sem((CUTS, 2, n_seq)),
            sem((CUTS, n_seq)),
            sem((2, CUTS)),
            sem((2, CUTS)),
            sem((CUTS, 2, n_seq)),
            sem((CUTS, n_seq)),
            sem((2, CUTS, n_seq)),
            sem((2, 2, CUTS, n_seq)),
            sem((2,)),
            sem((2,)),
            sem((1,)),
            sem((2, 2, n_seq)),
            sem((2, n_seq)),
            sem((2, n_seq)),
            sem((2, 2, 3)),
        ],
        compiler_params=pltpu.CompilerParams(
            collective_id=2, has_side_effects=True, vmem_limit_bytes=VMEM_LIMIT
        ),
    )(
        tokens, attn_weight, attn_gain[None], moe_gain[None], routes.T, gates.T,
        expert_gate, expert_up, expert_down,
    )


def fits(mesh, tokens, attn_weight, expert_gate):
    n_seq, local = mesh.shape["seq"], tokens.shape[0]
    own = attn_weight.shape[2] // n_seq
    return (
        mesh.shape["head"] == 4
        and mesh.shape["grp"] <= 2
        and n_seq > 1
        and own % HEAD_DIM == 0
        and attn_weight.shape[2] % n_seq == 0
        and local % 128 == 0
        and attn_weight.shape[1] % 256 == 0
        and n_seq * local <= 512
        and expert_gate.shape[0] <= 16
        and expert_gate.shape[0] % 8 == 0
    )


def solution(mesh):
    def run(tokens, attn_weight, attn_gain, moe_gain, routes, gates, *experts):
        whole = layer if fits(mesh, tokens, attn_weight, experts[0]) else body
        return whole(tokens, attn_weight, attn_gain, moe_gain, routes, gates, *experts)

    return jax.shard_map(
        run,
        mesh=mesh,
        in_specs=(
            P(("grp", "seq"), None),
            P(None, "seq", "head"),
            P(),
            P(),
            P(("grp", "seq"), None),
            P(("grp", "seq"), None),
            P("seq", None, "head"),
            P("seq", None, "head"),
            P("seq", "head", None),
        ),
        out_specs=P(("grp", "seq"), None),
        check_vma=False,
    )
```

```python
import functools

import jax
import jax.numpy as jnp
from jax import lax
from jax.experimental import pallas as pl
from jax.experimental.pallas import tpu as pltpu
from jax.sharding import PartitionSpec as P

HEAD_DIM = 128
EXPERTS = 64
TOPK = 8
CAP = 18
MESH = pl.DeviceIdType.MESH
VMEM_LIMIT = 63 * 1024 * 1024
XCUT = 2
SCHEDULE = [
    "s0", "x1", "x2", "s1", "x3", "s2", "w0", "s3", "a1", "w1", "s4", "a2",
    "w2", "s5", "a3", "w3", "n1", "n2", "n3", "w4", "t", "w5",
]
SPLIT = 4
CUTS = 4


PRECISE = lax.Precision.HIGHEST


def prefix_2(array, axis, combine, identity):
    peers, position = (lax.axis_size(axis), lax.axis_index(axis))
    everything = lax.all_gather(array.astype(jnp.bfloat16), axis)
    start = jnp.broadcast_to(jnp.asarray(identity, array.dtype), array.shape)

    def hop(k, before):
        reached = k < position
        new = combine(before, everything[k].astype(array.dtype))
        return jnp.where(reached, new, before)

    return lax.fori_loop(0, peers, hop, start)


def rms_scale(row_block, gain_vec):
    widened = row_block.astype(jnp.float32)
    factor = lax.rsqrt(jnp.mean(widened * widened, axis=-1, keepdims=True) + 1e-06)
    return widened * factor * gain_vec


def head_norm(outputs):
    return outputs * lax.rsqrt(jnp.mean(outputs * outputs, axis=-1, keepdims=True) + 1e-06)


def add_states(earlier, later):
    return earlier + later


def slot_numbers(route_flat):
    one_hot = (route_flat[:, None] == jnp.arange(EXPERTS, dtype=jnp.int32)[None, :]).astype(
        jnp.int32
    )
    earlier = jnp.cumsum(one_hot, axis=0) - one_hot
    return route_flat * CAP + jnp.sum(earlier * one_hot, axis=1)


def make_runner(expert_gate, expert_up, expert_down):

    def run_experts(received):
        gate_val = jnp.einsum(
            "necd,edf->necf", received, expert_gate, preferred_element_type=jnp.float32
        )
        up_val = jnp.einsum(
            "necd,edf->necf", received, expert_up, preferred_element_type=jnp.float32
        )
        hidden = (jax.nn.silu(gate_val) * up_val).astype(jnp.bfloat16)
        partial_value = jnp.einsum(
            "necf,efd->necd", hidden, expert_down, preferred_element_type=jnp.float32
        ).astype(jnp.bfloat16)
        groups = lax.axis_size("head")
        shape_now = partial_value.shape
        split = partial_value.reshape(
            shape_now[0], shape_now[1], shape_now[2], groups, shape_now[3] // groups
        )
        by_group = lax.all_to_all(split, "head", split_axis=3, concat_axis=3, tiled=True)
        summed = jnp.sum(by_group.astype(jnp.float32), axis=3)
        return lax.all_to_all(
            summed.astype(jnp.bfloat16), "seq", split_axis=0, concat_axis=0, tiled=True
        ).astype(summed.dtype)

    return run_experts


def body(
    tokens, attn_weight, attn_gain, moe_gain, routes, gates, expert_gate, expert_up, expert_down
):
    local_rows = tokens.shape[0]
    normed = rms_scale(tokens, attn_gain).astype(jnp.bfloat16)
    weights = lax.all_gather(attn_weight, "seq", axis=1, tiled=True)
    head_count = weights.shape[2] // HEAD_DIM
    projected = [
        jnp.dot(normed, weights[which], preferred_element_type=jnp.float32)
        .astype(jnp.bfloat16)
        .reshape(local_rows, head_count, HEAD_DIM)
        for which in range(3)
    ]
    query_rows, key_rows, value_rows = projected
    own_state = jnp.einsum("thd,the->hde", key_rows, value_rows, preferred_element_type=jnp.float32)
    prefix = prefix_2(own_state, "seq", add_states, jnp.zeros_like(own_state))
    inter_part = jnp.einsum(
        "thd,hde->the", query_rows.astype(jnp.float32), prefix, precision=PRECISE
    )
    scores = jnp.einsum("thd,shd->hts", query_rows, key_rows, preferred_element_type=jnp.float32)
    lower_mask = jnp.arange(local_rows)[:, None] >= jnp.arange(local_rows)[None, :]
    scores = jnp.where(lower_mask[None], scores, 0.0)
    intra_part = jnp.einsum(
        "hts,she->the", scores, value_rows.astype(jnp.float32), precision=PRECISE
    )
    attended = (
        head_norm(inter_part + intra_part)
        .reshape(local_rows, head_count * HEAD_DIM)
        .astype(jnp.bfloat16)
    )
    out_part = lax.dot_general(
        attended, weights[3], (((1,), (1,)), ((), ())), preferred_element_type=jnp.float32
    )
    residual = (
        tokens.astype(jnp.float32)
        + lax.psum(out_part.astype(jnp.bfloat16), "head").astype(jnp.float32)
    ).astype(jnp.bfloat16)
    moe_in = rms_scale(residual, moe_gain).astype(jnp.bfloat16)
    route_flat = routes.reshape(-1)
    slots = slot_numbers(route_flat)
    owners = lax.axis_size("seq")
    local_experts = expert_gate.shape[0]
    source_row = jnp.arange(route_flat.shape[0], dtype=jnp.int32) // TOPK
    run_experts = make_runner(expert_gate, expert_up, expert_down)
    outbound = (
        jnp.zeros((EXPERTS * CAP, moe_in.shape[1]), jnp.bfloat16).at[slots].set(moe_in[source_row])
    )
    outbound = outbound.reshape(owners, local_experts, CAP, moe_in.shape[1])
    returned = run_experts(lax.all_to_all(outbound, "seq", split_axis=0, concat_axis=0, tiled=True))
    arrived = returned.reshape(EXPERTS * CAP, -1)[slots].reshape(local_rows, TOPK, -1)
    moe_partial = jnp.einsum("tkd,tk->td", arrived, gates, precision=PRECISE)
    column_span = moe_partial.shape[1]
    residual_share = lax.dynamic_slice_in_dim(
        residual, lax.axis_index("head") * column_span, column_span, 1
    )
    mixed_share = (residual_share.astype(jnp.float32) + moe_partial).astype(jnp.bfloat16)
    return lax.all_gather(mixed_share, "head", axis=1, tiled=True)


def flip(index, bit):
    return index + bit * (1 - 2 * lax.rem(index // bit, 2))


def remote(source, dest, send_sem, recv_sem, target):
    return pltpu.make_async_remote_copy(
        src_ref=source,
        dst_ref=dest,
        send_sem=send_sem,
        recv_sem=recv_sem,
        device_id=target,
        device_id_type=MESH,
    )


def aligned(index, size):
    return pl.ds(pl.multiple_of(index * size, size), size)


def dot(a, b):
    return jnp.dot(a, b, preferred_element_type=jnp.float32)


def dot_nt(a, b):
    return lax.dot_general(a, b, (((1,), (1,)), ((), ())), preferred_element_type=jnp.float32)


def nearest(i, me, peers):
    both = jnp.minimum(me, peers - 1 - me)
    step = (i + 1) // 2
    side = -1 if i % 2 else 1
    rest = jnp.where(me <= peers - 1 - me, i - both, both - i)
    return me + jnp.where(i <= 2 * both, side * step, rest)


class Chain:
    def __init__(self, piece, sends, recvs, left):
        self.piece, self.sends, self.recvs, self.left = piece, sends, recvs, left
        self.peers, self.me = lax.axis_size("seq"), lax.axis_index("seq")

    def copy(self, origin, way):
        ref = self.piece(origin)
        to = lax.rem(self.me + (self.peers - 1 if way else 1), self.peers)
        return remote(ref, ref, self.sends.at[way, origin], self.recvs.at[origin], {"seq": to})

    def wanted(self, origin, way):
        if way:
            return (origin >= self.me) & (self.me > 0)
        return (origin <= self.me) & (self.me < self.peers - 1)

    def arrive(self, origin):
        self.copy(origin, 0).wait_recv()

    def forward(self, origin):
        self.left.append(lambda: self.sent(origin))
        for way in range(2):

            @pl.when(self.wanted(origin, way))
            def _():
                self.copy(origin, way).start()

    def sent(self, origin):
        for way in range(2):

            @pl.when(self.wanted(origin, way))
            def _():
                self.copy(origin, way).wait_send()


def layer_kernel(slots, *refs):
    (
        tok, aw, attn_gain, moe_gain, routes, gates, eg, eu, ed, o_ref,
        xall, xn, wbuf, w3, acc, qkv, att, psend, precv, pown, xsend, xrecv, res, sm, pick, mix, xs, ys, both, ssq,
        fs, ms, hid, wide, dbuf, csend, crecv, keep, osend, orecv, zsend, zrecv, share,
        own_sems, w_z, w_y, x_zs, x_zr, x_x, x_c, s_sems, a_zs, a_zr, p_c, p_x, r_zs, r_zr, r_x, r_c,
        g_sems, u_sems, d_sems, o_c, o_x, o_z, f_sems,
    ) = refs
    f32, bf16 = jnp.float32, jnp.bfloat16
    n_seq, n_grp = lax.axis_size("seq"), lax.axis_size("grp")
    grp, seq, head = lax.axis_index("grp"), lax.axis_index("seq"), lax.axis_index("head")
    core, col = lax.rem(head, 2), head // 2
    other_x, other_c = {"head": flip(head, 2)}, {"head": flip(head, 1)}
    other_y = {"grp": lax.rem(grp + 1, n_grp)}
    local, width = tok.shape
    total = n_seq * local
    depth, columns = aw.shape[1:]
    own = columns // n_seq
    part = depth // n_grp
    quarter = local // 4
    amount, inner = ed.shape[:2]
    span = width // 4
    near = [nearest(i, seq, n_seq) for i in range(n_seq)]

    left = []

    def go(copy):
        left.append(copy.wait_send)
        copy.start()

    barrier = pltpu.get_barrier_semaphore()
    friends = [{"seq": lax.rem(seq + k, n_seq)} for k in range(1, n_seq)] + [other_x, other_c]
    if n_grp > 1:
        friends.append(other_y)
    for friend in friends:
        pl.semaphore_signal(barrier, inc=1, device_id=friend, device_id_type=MESH)

    own_copies = [
        pltpu.make_async_copy(
            aw.at[which, :, aligned(seq, own)],
            wbuf.at[seq, :, pl.ds(which * own, own)],
            own_sems.at[which],
        )
        for which in range(3)
    ] + [pltpu.make_async_copy(aw.at[3], w3, own_sems.at[3])]
    for copy in own_copies:
        copy.start()
    xall[aligned(seq, local), :] = tok[...]
    top = routes.shape[0]
    sm[0:top, aligned(seq, local)] = routes[...].astype(f32)
    sm[top:, aligned(seq, local)] = gates[...]
    pl.semaphore_wait(barrier, len(friends))

    def token_rows(p, owner, n):
        start = p * local + owner * quarter + n * (quarter // XCUT)
        return xall.at[pl.ds(pl.multiple_of(start, quarter // XCUT), quarter // XCUT), :]

    tokens_z = [
        Chain(lambda p, n=n: token_rows(p, head, n), x_zs.at[n], x_zr.at[n], left)
        for n in range(XCUT)
    ]
    for chain in tokens_z:
        chain.forward(seq)

    def table_copy(to, origin):
        ref = sm.at[:, aligned(origin, local)]
        return remote(ref, ref, s_sems.at[0, to], s_sems.at[1, origin], {"seq": to})

    twice = 3 * depth // 8 if n_grp > 1 else 0
    once = (depth - twice) // n_grp
    batches = [(w, k * (part // 2), part // 2, part) for w in range(2) for k in range(2)]
    batches.append((2, 0, once, once))
    if twice:
        batches.append((2, depth - twice, twice, 0))
    passed_on = [n for n, batch in enumerate(batches) if batch[3] and n_grp > 1]

    def w_rows(side, n):
        _, start, size, stride = batches[n]
        return pl.ds(pl.multiple_of(side * stride + start, 16), size)

    def w_cols(n):
        return pl.ds(batches[n][0] * own, own)

    def w_copy(n, to):
        return remote(
            aw.at[batches[n][0], w_rows(grp, n), aligned(to, own)],
            wbuf.at[seq, w_rows(grp, n), w_cols(n)],
            w_z.at[0, n, to], w_z.at[1, n, seq], {"seq": to},
        )

    def w_arrival(n, origin):
        ref = wbuf.at[origin, w_rows(grp, n), w_cols(n)]
        return remote(ref, ref, w_z.at[0, n, origin], w_z.at[1, n, origin], {"seq": origin})

    def w_over(n, origin, side):
        ref = wbuf.at[origin, w_rows(side, n), w_cols(n)]
        return remote(ref, ref, w_y.at[0, n, origin], w_y.at[1, n, origin], other_y)

    def send_w(n):
        for p in reversed(near[1:]):
            go(w_copy(n, p))

    for p in near[1:]:
        go(table_copy(p, seq))

    def fetch(i):
        rows, place = aligned(near[i], depth), i % 2
        return [
            pltpu.make_async_copy(
                eg.at[:, rows], wide.at[place, :, :, pl.ds(0, inner)], g_sems.at[place]
            ),
            pltpu.make_async_copy(
                eu.at[:, rows], wide.at[place, :, :, pl.ds(inner, inner)], u_sems.at[place]
            ),
        ]

    fetch_down = pltpu.make_async_copy(ed, dbuf, d_sems.at[0])
    for i in range(2):
        for copy in fetch(i):
            copy.start()
    fetch_down.start()

    def norm_rows(p):
        def step(j, carry):
            rows = pl.ds(pl.multiple_of(p * local + j * quarter, quarter), quarter)
            value = xall[rows, :].astype(f32)
            factor = lax.rsqrt(jnp.mean(value * value, axis=-1, keepdims=True) + 1e-06)
            xn[rows, :] = (value * factor * attn_gain[...]).astype(bf16)
            return carry

        lax.fori_loop(0, 4, step, 0)

    norm_rows(seq)

    def across(p, n):
        ref = token_rows(p, head, n)
        return remote(ref, ref, x_x.at[0, n, p], x_x.at[1, n, p], other_x)

    def beside(p, which, n):
        ref = token_rows(p, flip(head, 2) if which else head, n)
        return remote(ref, ref, x_c.at[0, which, n, p], x_c.at[1, which, n, p], other_c)

    def tables():
        for p in near[1:]:
            table_copy(p, p).wait_recv()
        ids = lax.broadcasted_iota(jnp.int32, (128, total), 0).astype(f32)
        ids = ids + (seq * amount).astype(f32)
        named = jnp.zeros((128, total), f32)
        weight = jnp.zeros((128, total), f32)
        for k in range(top):
            hit = sm[k : k + 1, :] == ids
            named = jnp.where(hit, 1.0, named)
            weight = jnp.where(hit, sm[top + k : top + k + 1, :], weight)
        before = lax.broadcasted_iota(jnp.int32, (total, total), 0) < lax.broadcasted_iota(
            jnp.int32, (total, total), 1
        )
        rank = dot(named.astype(bf16), jnp.where(before, 1.0, 0.0).astype(bf16))
        place = jnp.where(named > 0.0, rank, -1.0)
        spot = lax.broadcasted_iota(jnp.int32, (slots, total), 0).astype(f32)
        for e in range(amount):
            pick[e * slots : (e + 1) * slots, :] = jnp.where(
                place[e : e + 1, :] == spot, 1.0, 0.0
            ).astype(bf16)
        lanes = lax.broadcasted_iota(jnp.int32, (128, amount * slots), 1).astype(f32)
        owner = jnp.floor((lanes + 0.5) * (1.0 / slots))
        mine = lax.broadcasted_iota(jnp.int32, (128, amount * slots), 0).astype(f32)
        spread = jnp.where(owner == mine, 1.0, 0.0).astype(bf16)
        spot_of = (lanes - owner * slots)[:1, :]
        place_t = jnp.transpose(place).astype(bf16)
        weight_t = jnp.transpose(weight).astype(bf16)
        for b in range(0, total, 128):
            mix[b : b + 128, :] = jnp.where(
                dot(place_t[b : b + 128], spread) == spot_of, dot(weight_t[b : b + 128], spread), 0.0
            ).astype(bf16)

    for event in SCHEDULE:
        kind, at = event[0], int(event[1:] or 0)
        if kind == "s":
            if at < len(batches):
                send_w(at)
        elif kind == "w":
            if at < len(batches):
                for p in near[1:]:
                    w_arrival(at, p).wait_recv()
                    if at in passed_on:
                        go(w_over(at, p, grp))
        elif kind == "t":
            tables()
        elif kind == "n":
            if at < n_seq:
                for n in range(XCUT):
                    beside(near[at], 0, n).wait_recv()
                    beside(near[at], 1, n).wait_recv()
                norm_rows(near[at])
        elif at < n_seq:
            for n in range(XCUT):
                if kind == "x":
                    tokens_z[n].arrive(near[at])
                    tokens_z[n].forward(near[at])
                    go(across(near[at], n))
                    go(beside(near[at], 0, n))
                else:
                    across(near[at], n).wait_recv()
                    go(beside(near[at], 1, n))

    for copy in own_copies:
        copy.wait()
    acc[...] = dot(xn[:, aligned(seq, depth)], wbuf[seq])
    for i in range(1, n_seq):
        p = near[i]
        for n in passed_on:
            w_over(n, p, lax.rem(grp + 1, n_grp)).wait_recv()
        acc[...] += dot(xn[:, aligned(p, depth)], wbuf[p])
    qkv[...] = acc[...].astype(bf16)

    cut = total // CUTS
    attended = [
        Chain(
            lambda p, n=n: att.at[pl.ds(n * cut, cut), aligned(p, own)],
            a_zs.at[n], a_zr.at[n], left,
        )
        for n in range(CUTS)
    ]
    for n in range(CUTS):
        seen = (n + 1) * cut
        lower = (
            lax.broadcasted_iota(jnp.int32, (cut, seen), 0) + n * cut
            >= lax.broadcasted_iota(jnp.int32, (cut, seen), 1)
        )
        for a in range(own // HEAD_DIM):
            at = a * HEAD_DIM
            query = qkv[n * cut : seen, at : at + HEAD_DIM]
            key = qkv[0:seen, own + at : own + at + HEAD_DIM]
            value = qkv[0:seen, 2 * own + at : 2 * own + at + HEAD_DIM]
            scores = jnp.where(lower, dot_nt(query, key), 0.0).astype(bf16)
            result = head_norm(dot(scores, value)).astype(bf16)
            place_at = pl.ds(pl.multiple_of(seq * own + at, HEAD_DIM), HEAD_DIM)
            att[n * cut : seen, place_at] = result
        attended[n].forward(seq)

    block = cut // 2

    def block_rows(n, side):
        return pl.ds(pl.multiple_of(n * cut + side * block, block), block)

    def part_copy(n):
        return remote(psend.at[n], precv.at[n], p_c.at[0, n], p_c.at[1, n], other_c)

    def owned(n):
        if n >= SPLIT:
            return block_rows(n, core)
        return split_rows(n, core, col)

    def split_rows(n, side, across):
        start = n * cut + side * block + across * (block // 2)
        return pl.ds(pl.multiple_of(start, block // 2), block // 2)

    def part_rows(n, across):
        if n >= SPLIT:
            return pl.ds(0, block)
        return pl.ds(pl.multiple_of(across * (block // 2), block // 2), block // 2)

    def sum_copy(n):
        rows = part_rows(n, 1 - col)
        return remote(
            xsend.at[n, rows], xrecv.at[n, rows], p_x.at[0, n], p_x.at[1, n], other_x
        )

    residual = [
        Chain(
            lambda p, n=n: res.at[owned(n), aligned(p, depth)], r_zs.at[n], r_zr.at[n], left
        )
        for n in range(CUTS)
    ]

    def res_across(p, n):
        ref = res.at[owned(n), aligned(p, depth)]
        return remote(ref, ref, r_x.at[0, n, p], r_x.at[1, n, p], other_x)

    def res_over(p, n, side, which):
        if n >= SPLIT:
            rows = block_rows(n, side)
        else:
            rows = split_rows(n, side, 1 - col if which else col)
        ref = res.at[rows, aligned(p, depth)]
        return remote(ref, ref, r_c.at[0, which, n, p], r_c.at[1, which, n, p], other_c)

    def pass_on(p, n):
        residual[n].forward(p)
        if n < SPLIT:
            go(res_across(p, n))
        go(res_over(p, n, core, 0))

    def project(n):
        psend[n] = dot_nt(att[block_rows(n, 1 - core), :], w3[...]).astype(bf16)
        go(part_copy(n))
        pown[n] = dot_nt(att[block_rows(n, core), :], w3[...])

    def join(n):
        part_copy(n).wait_recv()
        xsend[n] = (pown[n] + precv[n].astype(f32)).astype(bf16)
        go(sum_copy(n))

    def settle(n):
        sum_copy(n).wait_recv()
        rows, cols, at = owned(n), aligned(seq, depth), part_rows(n, col)
        summed = xsend[n, at, :].astype(f32) + xrecv[n, at, :].astype(f32)
        res[rows, cols] = (xall[rows, cols].astype(f32) + summed).astype(bf16)
        pass_on(seq, n)

    for i in range(1, n_seq):
        for n in range(CUTS):
            attended[n].arrive(near[i])
            attended[n].forward(near[i])
            if i == n_seq - 1:
                project(n)
                if n > 0:
                    join(n - 1)
    join(CUTS - 1)
    for n in range(CUTS):
        settle(n)

    def gather(p):
        for n in range(SPLIT):
            res_across(p, n).wait_recv()
            go(res_over(p, n, core, 1))
        for n in range(CUTS):
            res_over(p, n, 1 - core, 0).wait_recv()
            if n < SPLIT:
                res_over(p, n, 1 - core, 1).wait_recv()
        cols = aligned(p, depth)

        def scale(j, carry):
            rows = pl.ds(pl.multiple_of(j * 64, 64), 64)
            value = res[rows, cols].astype(f32)
            square = value * value
            add = square[:, 0:128]
            for k in range(128, depth, 128):
                add += square[:, k : k + 128]
            ssq[rows, :] += add
            ms[rows, :] = (value * moe_gain[:, cols]).astype(bf16)
            return carry

        lax.fori_loop(0, total // 64, scale, 0, unroll=2)
        for k in range(0, depth, 256):
            xs[:, k : k + 256] = dot(pick[...], ms[:, k : k + 256]).astype(bf16)

    def products(i):
        for copy in fetch(i):
            copy.wait()

        def step(j, carry):
            for e in range(16):
                e = 16 * j + e
                rows = pl.ds(pl.multiple_of(e * slots, slots), slots)
                value = dot(xs[rows, :], wide[i % 2, e])
                both[rows, :] = value if i == 0 else both[rows, :] + value
            return carry

        lax.fori_loop(0, amount // 16, step, 0)
        if i + 2 < n_seq:
            for copy in fetch(i + 2):
                copy.start()

    ssq[...] = jnp.zeros_like(ssq)
    def reach_res(i):
        for n in range(CUTS):
            residual[n].arrive(near[i])
            pass_on(near[i], n)

    for i in range(1, n_seq + 1):
        if i < n_seq:
            reach_res(i)
        if i > 1:
            gather(near[i - 2])
            products(i - 2)
    gather(near[n_seq - 1])
    products(n_seq - 1)
    factor = lax.rsqrt(jnp.sum(ssq[...], axis=-1, keepdims=True) * (1.0 / width) + 1e-06)
    high = factor.astype(bf16).astype(f32)
    middle = (factor - high).astype(bf16).astype(f32)
    lane = lax.broadcasted_iota(jnp.int32, (total, 128), 1)
    terms = jnp.where(
        lane == 0, high, jnp.where(lane == 1, middle, jnp.where(lane == 2, factor - high - middle, 0.0))
    )
    per_slot = jnp.sum(dot(pick[...], terms.astype(bf16)), axis=-1, keepdims=True)
    fs[...] = jnp.broadcast_to(per_slot, fs.shape)

    def activate(j, carry):
        for e in range(4):
            e = 4 * j + e
            rows = pl.ds(pl.multiple_of(e * slots, slots), slots)
            scale = fs[rows, 0:1]
            gate_val = both[rows, 0:inner] * scale
            up_val = both[rows, inner : 2 * inner] * scale
            hid[rows, :] = (gate_val * jax.nn.sigmoid(gate_val) * up_val).astype(bf16)
        return carry

    lax.fori_loop(0, amount // 4, activate, 0, unroll=2)

    fetch_down.wait()

    def down(side):
        cols = aligned(side, 2 * span)

        def step(j, carry):
            for e in range(16):
                e = 16 * j + e
                rows = pl.ds(pl.multiple_of(e * slots, slots), slots)
                ys[rows, :] = dot(hid[rows, :], dbuf[e, :, cols]).astype(bf16)
            return carry

        lax.fori_loop(0, amount // 16, step, 0)

    def pair_copy(u, p):
        return remote(csend.at[u, p], crecv.at[u, p], o_c.at[0, u, p], o_c.at[1, u, p], other_c)

    def over_copy(p):
        return remote(osend.at[p], orecv.at[p], o_x.at[0, p], o_x.at[1, p], other_x)

    def back_copy(to, origin):
        return remote(
            zsend.at[to], zrecv.at[origin], o_z.at[0, to], o_z.at[1, origin], {"seq": to}
        )

    def share_out(u, p):
        rows = aligned(p, local)
        csend[u, p] = dot(mix[rows, :], ys[:, aligned(1 - core, span)]).astype(bf16)
        go(pair_copy(u, p))
        keep[p] = dot(mix[rows, :], ys[:, aligned(core, span)])

    order = near[::-1]

    def hand_over(p):
        pair_copy(0, p).wait_recv()
        osend[p] = (keep[p] + crecv[0, p].astype(f32)).astype(bf16)
        go(over_copy(p))

    down(1 - col)
    for n in range(n_seq + 1):
        if n < n_seq:
            share_out(0, order[n])
        if n > 0:
            hand_over(order[n - 1])

    def add_up(p):
        pair_copy(1, p).wait_recv()
        over_copy(p).wait_recv()
        return keep[p] + crecv[1, p].astype(f32) + orecv[p].astype(f32)

    down(col)
    for p in order:
        share_out(1, p)
    for p in order[:-1]:
        zsend[p] = add_up(p).astype(bf16)
        go(back_copy(p, seq))
    mine_cols = aligned(head, span)
    summed = add_up(seq) + res[aligned(seq, local), mine_cols].astype(f32)
    for p in order[:-1]:
        back_copy(p, p).wait_recv()
        summed = summed + zrecv[p].astype(f32)
    share[...] = summed.astype(bf16)

    def final_copy(owner, n, k, target):
        rows = pl.ds(n * (local // 2), local // 2)
        ref = o_ref.at[rows, aligned(owner, span)]
        source = share.at[rows] if k < 2 else ref
        return remote(source, ref, f_sems.at[0, n, k], f_sems.at[1, n, k], target)

    for k, target in enumerate((other_x, other_c)):
        for n in range(2):
            go(final_copy(head, n, k, target))
    o_ref[:, mine_cols] = share[...]
    for n in range(2):
        final_copy(head, n, 0, other_x).wait_recv()
        go(final_copy(flip(head, 2), n, 2, other_c))
    for n in range(2):
        for k in (1, 2):
            final_copy(head, n, k, other_c).wait_recv()

    for wait in left:
        wait()


def layer(
    tokens, attn_weight, attn_gain, moe_gain, routes, gates, expert_gate, expert_up, expert_down
):
    local, width = tokens.shape
    n_seq = lax.axis_size("seq")
    total = n_seq * local
    depth, columns = attn_weight.shape[1:]
    own = columns // n_seq
    amount, _, inner = expert_gate.shape
    slots = -(-CAP * n_seq // 16) * 16
    span = width // 4
    bf16, f32 = jnp.bfloat16, jnp.float32
    vmem, sem = pltpu.VMEM, pltpu.SemaphoreType.DMA
    block = total // CUTS // 2
    here, away = pl.BlockSpec(memory_space=pltpu.VMEM), pl.BlockSpec(memory_space=pl.ANY)
    return pl.pallas_call(
        functools.partial(layer_kernel, slots),
        out_shape=jax.ShapeDtypeStruct(tokens.shape, tokens.dtype),
        in_specs=[here, away, here, here, here, here, away, away, away],
        out_specs=here,
        scratch_shapes=[
            vmem((total, width), bf16),
            vmem((total, width), bf16),
            vmem((n_seq, depth, 3 * own), bf16),
            vmem((depth, columns), bf16),
            vmem((total, 3 * own), f32),
            vmem((total, 3 * own), bf16),
            vmem((total, columns), bf16),
            vmem((CUTS, block, depth), bf16),
            vmem((CUTS, block, depth), bf16),
            vmem((CUTS, block, depth), f32),
            vmem((CUTS, block, depth), bf16),
            vmem((CUTS, block, depth), bf16),
            vmem((total, width), bf16),
            vmem((2 * routes.shape[1], total), f32),
            vmem((amount * slots, total), bf16),
            vmem((total, amount * slots), bf16),
            vmem((amount * slots, depth), bf16),
            vmem((amount * slots, 2 * span), bf16),
            vmem((amount * slots, 2 * inner), f32),
            vmem((total, 128), f32),
            vmem((amount * slots, 128), f32),
            vmem((total, depth), bf16),
            vmem((amount * slots, inner), bf16),
            vmem((2, amount, depth, 2 * inner), bf16),
            vmem((amount, inner, width), bf16),
            vmem((2, n_seq, local, span), bf16),
            vmem((2, n_seq, local, span), bf16),
            vmem((n_seq, local, span), f32),
            vmem((n_seq, local, span), bf16),
            vmem((n_seq, local, span), bf16),
            vmem((n_seq, local, span), bf16),
            vmem((n_seq, local, span), bf16),
            vmem((local, span), bf16),
            sem((4,)),
            sem((2, 6, n_seq)),
            sem((2, 6, n_seq)),
            sem((XCUT, 2, n_seq)),
            sem((XCUT, n_seq)),
            sem((2, XCUT, n_seq)),
            sem((2, 2, XCUT, n_seq)),
            sem((2, n_seq)),
            sem((CUTS, 2, n_seq)),
            sem((CUTS, n_seq)),
            sem((2, CUTS)),
            sem((2, CUTS)),
            sem((CUTS, 2, n_seq)),
            sem((CUTS, n_seq)),
            sem((2, CUTS, n_seq)),
            sem((2, 2, CUTS, n_seq)),
            sem((2,)),
            sem((2,)),
            sem((1,)),
            sem((2, 2, n_seq)),
            sem((2, n_seq)),
            sem((2, n_seq)),
            sem((2, 2, 3)),
        ],
        compiler_params=pltpu.CompilerParams(
            collective_id=2, has_side_effects=True, vmem_limit_bytes=VMEM_LIMIT
        ),
    )(
        tokens, attn_weight, attn_gain[None], moe_gain[None], routes.T, gates.T,
        expert_gate, expert_up, expert_down,
    )


def fits(mesh, tokens, attn_weight, expert_gate):
    n_seq, local = mesh.shape["seq"], tokens.shape[0]
    own = attn_weight.shape[2] // n_seq
    return (
        mesh.shape["head"] == 4
        and mesh.shape["grp"] <= 2
        and n_seq > 1
        and own % HEAD_DIM == 0
        and attn_weight.shape[2] % n_seq == 0
        and local % 128 == 0
        and attn_weight.shape[1] % 256 == 0
        and n_seq * local <= 512
        and expert_gate.shape[0] <= 16
        and expert_gate.shape[0] % 16 == 0
    )


def solution(mesh):
    def run(tokens, attn_weight, attn_gain, moe_gain, routes, gates, *experts):
        whole = layer if fits(mesh, tokens, attn_weight, experts[0]) else body
        return whole(tokens, attn_weight, attn_gain, moe_gain, routes, gates, *experts)

    return jax.shard_map(
        run,
        mesh=mesh,
        in_specs=(
            P(("grp", "seq"), None),
            P(None, "seq", "head"),
            P(),
            P(),
            P(("grp", "seq"), None),
            P(("grp", "seq"), None),
            P("seq", None, "head"),
            P("seq", None, "head"),
            P("seq", "head", None),
        ),
        out_specs=P(("grp", "seq"), None),
        check_vma=False,
    )
```
